32 devices in a mesh: pairs: 8 (over z, x), win: 4 (over y, core).
Axes of the slice: x: 2, y: 2, z: 4, core: 2. Of those that a mesh axis runs over, the one named last changes fastest.
Arguments:
- spectra: float32 [128, 8, 2, 3200], P('pairs', 'win'), as said below
- requests: int32 [8, 8, 8], P('pairs'), may hold values from -1 to 15, as said below
- pair_first: int32 [4096], P('pairs'), may hold values from 0 to 63, as said below
- pair_second: int32 [4096], P('pairs'), may hold values from 0 to 63, as said below
Outputs:
- stacks: float32 [2048, 4096], P('win', 'pairs')
The draws below stay inside these ranges and needn't reach their ends.
Inputs may be any that keep to these rules, and one draw needn't show every extreme that they name: requests[o, s, c] is a row of source device s's 16 stations that owner o needs, or -1 for an empty slot; an owner's rows from one source are distinct and fill the slots from 0 onward; every owner takes 8 rows from some source. `pair_first`: pair p belongs to owner p // 512 and names one of that owner's 8 x 8 slots, source-major, never an empty one. `pair_second`: as pair_first. Finite band spectra.
All inputs are finite; a program needn't handle non-finite values.
Results may differ from the reference program's by a relative error of at most 0.01.
Values may be sent and summed in bfloat16 or wider, within the bound.
No kernel may reach another device: no remote copies, remote signals or barrier semaphores. Data moves between devices by JAX's collectives and lax.ppermute only.
A program may use at most 128 MiB of HBM per device.

```python
import math
import jax
import jax.numpy as jnp
from jax import lax

F = 3200
LAGS = 2048
NFFT = 18000
K0 = 360
STA_DEV = 16
CAP = 8
W_DEV = 2
PAIR_DEV = 512
STATIONS = 128
WINDOWS = 8
PAIRS = 4096
N_PAIRS = 8
N_WIN = 4


def slot_plan(key):
    base = jax.random.fold_in(key, 7)
    key_count, key_rows = jax.random.split(base)
    counts = jax.random.randint(key_count, (N_PAIRS, N_PAIRS), CAP // 2, CAP + 1)
    owners = jnp.arange(N_PAIRS)
    forced = (owners[:, None] * 5 + 3) % N_PAIRS == owners[None, :]
    counts = jnp.where(forced, CAP, counts)
    scores = jax.random.randint(key_rows, (N_PAIRS, N_PAIRS, STA_DEV), 0, 1 << 20) * STA_DEV + jnp.arange(STA_DEV)[None, None, :]
    chosen = jnp.argsort(scores, axis=2)[:, :, :CAP]
    slot_index = jnp.arange(CAP)
    return jnp.where(slot_index[None, None, :] < counts[:, :, None], chosen, -1).astype(jnp.int32)


def pair_slots(key, salt):
    requests = slot_plan(key)
    valid = (requests >= 0).reshape(N_PAIRS, N_PAIRS * CAP).astype(jnp.int32)
    totals = jnp.sum(valid, axis=1)
    order = jnp.argsort((1 - valid) * (N_PAIRS * CAP) + jnp.arange(N_PAIRS * CAP)[None, :], axis=1)
    picks = jax.random.randint(jax.random.fold_in(key, salt), (N_PAIRS, PAIR_DEV), 0, totals[:, None])
    return jnp.take_along_axis(order, picks, axis=1).reshape(N_PAIRS * PAIR_DEV).astype(jnp.int32)


def draw_requests(key, part):
    return slot_plan(key)


def draw_pair_first(key, part):
    return pair_slots(key, 21)


def draw_pair_second(key, part):
    return pair_slots(key, 22)


def draw_spectra(key, part):
    key_base, key_scale = jax.random.split(jax.random.fold_in(key, 31), 2)
    block_count = F // 128
    log_top = jnp.log(10.0)
    base = jax.random.normal(key_base, (STATIONS, WINDOWS, 2, block_count, 128), jnp.float32)
    scales = jnp.exp(jax.random.uniform(key_scale, (STATIONS, WINDOWS, 1, block_count, 1), jnp.float32, 0.0, 1.0) * log_top)
    return (base * scales).reshape(STATIONS, WINDOWS, 2, F).astype(jnp.float32)


def setup_inputs(seed: int = 0) -> dict:
    key_of = jax.random.split(jax.random.key(seed), 5)
    spectra = draw_spectra(jax.random.fold_in(key_of[4], 71), 0)
    requests = draw_requests(jax.random.fold_in(key_of[4], 71), 0)
    pair_first = draw_pair_first(jax.random.fold_in(key_of[4], 71), 0)
    pair_second = draw_pair_second(jax.random.fold_in(key_of[4], 71), 0)
    return dict(spectra=spectra, requests=requests, pair_first=pair_first, pair_second=pair_second)


def whiten(spectra):
    shape = spectra.shape
    blocks = spectra.astype(jnp.float32).reshape(shape[0], shape[1], shape[2], shape[3] // 128, 128)
    block_power = lax.optimization_barrier(jnp.mean(blocks * blocks, axis=(2, 4), keepdims=True))
    return (blocks / jnp.sqrt(block_power + 1e-06)).reshape(shape).astype(jnp.bfloat16)

def lag_table(lag_start, lag_count):
    lag_index = (lag_start + jnp.arange(lag_count, dtype=jnp.int32) - LAGS // 2).astype(jnp.int32)
    bin_index = (K0 + jnp.arange(F, dtype=jnp.int32)).astype(jnp.int32)
    angles = (lag_index[:, None] * bin_index[None, :] % NFFT).astype(jnp.float32) * (2.0 * math.pi / NFFT)
    return jnp.concatenate([jnp.cos(angles), -jnp.sin(angles)], axis=1).astype(jnp.bfloat16)

def reference(spectra, requests, pair_first, pair_second):
    white = whiten(spectra)
    owner_slots = (jnp.arange(N_PAIRS, dtype=jnp.int32)[None, :, None] * STA_DEV + jnp.maximum(requests, 0)).reshape(N_PAIRS, N_PAIRS * CAP).astype(jnp.int32)
    owner_index = (jnp.arange(PAIRS, dtype=jnp.int32) // PAIR_DEV).astype(jnp.int32)
    station_first = owner_slots[owner_index, pair_first]
    station_second = owner_slots[owner_index, pair_second]
    table_full = lag_table(0, LAGS).astype(jnp.float32)
    norm_scale = 1.0 / math.sqrt(F * WINDOWS)
    block_size = math.gcd(PAIRS, 512)
    pair_blocks = PAIRS // block_size

    def one_block(indices):
        first_spec = white[indices[0]].astype(jnp.float32).reshape(block_size, N_WIN, W_DEV, 2, F)
        second_spec = white[indices[1]].astype(jnp.float32).reshape(block_size, N_WIN, W_DEV, 2, F)
        real_part = lax.optimization_barrier(jnp.sum(first_spec[:, :, :, 0] * second_spec[:, :, :, 0] + first_spec[:, :, :, 1] * second_spec[:, :, :, 1], axis=2))
        imag_part = lax.optimization_barrier(jnp.sum(first_spec[:, :, :, 1] * second_spec[:, :, :, 0] - first_spec[:, :, :, 0] * second_spec[:, :, :, 1], axis=2))
        partial_value = jnp.concatenate([real_part, imag_part], axis=2).astype(jnp.bfloat16)
        summed = lax.optimization_barrier(jnp.sum(partial_value.astype(jnp.float32), axis=1))
        return norm_scale * jnp.dot(table_full, summed.T, precision=lax.Precision.HIGHEST)
    result = lax.map(one_block, (station_first.reshape(pair_blocks, block_size), station_second.reshape(pair_blocks, block_size)))
    return jnp.transpose(result, (1, 0, 2)).reshape(LAGS, PAIRS)
```

```python
import functools
import math

import jax
import jax.numpy as jnp
from jax import lax
from jax.experimental import pallas as pl
from jax.experimental.pallas import tpu as pltpu
from jax.sharding import PartitionSpec as P

LAGS = 2048
NFFT = 18000
K0 = 360
LANES = 128
EPS = 1e-06
FINE = 32
VMEM = pl.BlockSpec(memory_space=pltpu.VMEM)
SMEM = pl.BlockSpec(memory_space=pltpu.SMEM)


def params(**kw):
    return pltpu.CompilerParams(vmem_limit_bytes=60 * 1024 * 1024, **kw)


def whiten_kernel(half, blocks, core_ref, own_ref, got_ref, big_ref, small_ref, tmp):
    stations = big_ref.shape[0]
    core = core_ref[0]

    def white(re, im):
        power = jnp.sum(re * re + im * im, axis=1, keepdims=True) * (1.0 / (2 * LANES))
        scale = lax.rsqrt(power + EPS)
        return re * scale, im * scale

    def station(s, carry):
        for side in range(2):
            for w in range(2):
                if side == 0:
                    ref, base = own_ref, ((s * 2 + w) * blocks + core * half) * 2
                else:
                    ref, base = got_ref, (s * 2 + w) * half * 2
                re = ref[pl.ds(base, 8, stride=2), :]
                im = ref[pl.ds(base + 1, 8, stride=2), :]
                re, im = white(re, im)
                big_ref[s, (side * 2 + w) * 16 : (side * 2 + w + 1) * 16, :] = jnp.concatenate(
                    [re, im], axis=0
                ).astype(jnp.bfloat16)
                for part in range(2):
                    tmp[side * 16 + part * 8 + w * 4 : side * 16 + part * 8 + w * 4 + 4, :] = ref[
                        pl.ds(base + 16 + part, 4, stride=2), :
                    ]
            re = tmp[side * 16 : side * 16 + 8, :]
            im = tmp[side * 16 + 8 : side * 16 + 16, :]
            re, im = white(re, im)
            small_ref[s, side * 16 : side * 16 + 16, :] = jnp.concatenate([re, im], axis=0).astype(
                jnp.bfloat16
            )
        for w in range(2):
            base = ((s * 2 + w) * blocks + 2 * half) * 2
            for part in range(2):
                tmp[32 + part * 8 + w : 32 + part * 8 + w + 1, :] = own_ref[pl.ds(base + part, 1), :]
        re, im = white(tmp[32:40, :], tmp[40:48, :])
        tmp[48:50, :] = re[0:2]
        tmp[50:52, :] = im[0:2]
        small_ref[s, 32:40, :] = tmp[48:56, :].astype(jnp.bfloat16)
        return carry

    tmp[...] = jnp.zeros_like(tmp)
    lax.fori_loop(0, stations, station, 0)


def whiten(core, own, got, stations, half, blocks):
    return pl.pallas_call(
        functools.partial(whiten_kernel, half, blocks),
        name="whiten",
        out_shape=(
            jax.ShapeDtypeStruct((stations, 64, LANES), jnp.bfloat16),
            jax.ShapeDtypeStruct((stations, 40, LANES), jnp.bfloat16),
        ),
        in_specs=[SMEM, VMEM, VMEM],
        out_specs=(VMEM, VMEM),
        scratch_shapes=[pltpu.VMEM((56, LANES), jnp.float32)],
        compiler_params=params(),
        cost_estimate=pl.CostEstimate(flops=2_000_000, bytes_accessed=2_000_000, transcendentals=0),
    )(core, own, got)


def select_kernel(peers, sources, cap, me_ref, *refs):
    asked = refs[:peers]
    near, far = refs[peers : peers + 2]
    outs = refs[peers + 2 :]
    me = me_ref[0]
    for d in range(peers):
        for h, chunk in enumerate((near, far)):
            source = me ^ (h * (sources // 2))
            for c in range(cap):
                row = jnp.maximum(asked[d][source, c], 0)
                outs[d][h * cap + c] = chunk[row]


def select(me, asked, near, far, cap):
    peers = len(asked)
    sources = asked[0].shape[0]
    out = jax.ShapeDtypeStruct((2 * cap,) + near.shape[1:], near.dtype)
    return pl.pallas_call(
        functools.partial(select_kernel, peers, sources, cap),
        name="select",
        out_shape=(out,) * peers,
        in_specs=[SMEM] * (1 + peers) + [VMEM, VMEM],
        out_specs=(VMEM,) * peers,
        compiler_params=params(),
        cost_estimate=pl.CostEstimate(flops=0, bytes_accessed=1_000_000, transcendentals=0),
    )(me, *asked, near, far)


def load_table(bufs, table):
    at = 0
    for buf in bufs:

        def copy(i, carry, buf=buf, at=at):
            table[at + i] = buf[i].astype(jnp.float32)
            return carry

        lax.fori_loop(0, buf.shape[0], copy, 0)
        at += buf.shape[0]


def cross_big_kernel(count, first_ref, second_ref, *refs):
    bufs = refs[:count]
    out, table, cross = refs[count:]
    pairs = out.shape[0]
    load_table(bufs, table)

    def pair(p, carry):
        i = first_ref[p]
        j = second_ref[p]
        re = im = None
        for w in range(4):
            ar = table[i, w * 16 : w * 16 + 8, :]
            ai = table[i, w * 16 + 8 : w * 16 + 16, :]
            br = table[j, w * 16 : w * 16 + 8, :]
            bi = table[j, w * 16 + 8 : w * 16 + 16, :]
            r = ar * br + ai * bi
            m = ai * br - ar * bi
            re = r if re is None else re + r
            im = m if im is None else im + m
        at = pl.multiple_of(p * 16, 16)
        cross[pl.ds(at, 8), :] = re
        cross[pl.ds(at + 8, 8), :] = im
        return carry

    lax.fori_loop(0, pairs, pair, 0, unroll=4)
    for k in range(16):
        out[:, k * LANES : (k + 1) * LANES] = cross[pl.ds(k, pairs, stride=16), :].astype(
            jnp.bfloat16
        )


def cross_small_kernel(count, first_ref, second_ref, *refs):
    bufs = refs[:count]
    out, table, cross = refs[count:]
    pairs = out.shape[0]
    load_table(bufs, table)

    def pair(p, carry):
        i = first_ref[p]
        j = second_ref[p]
        re = im = None
        for g in range(2):
            ar = table[i, g * 16 : g * 16 + 8, :]
            ai = table[i, g * 16 + 8 : g * 16 + 16, :]
            br = table[j, g * 16 : g * 16 + 8, :]
            bi = table[j, g * 16 + 8 : g * 16 + 16, :]
            r = ar * br + ai * bi
            m = ai * br - ar * bi
            re = r if re is None else re + r
            im = m if im is None else im + m
        at = pl.multiple_of(p * 24, 8)
        cross[pl.ds(at, 8), :] = re
        cross[pl.ds(at + 8, 8), :] = im
        a = table[i, 32:40, :]
        b = table[j, 32:40, :]
        r = a[0:2] * b[0:2] + a[2:4] * b[2:4]
        m = a[2:4] * b[0:2] - a[0:2] * b[2:4]
        cross[pl.ds(at + 16, 2), :] = r
        cross[pl.ds(at + 18, 2), :] = m
        return carry

    lax.fori_loop(0, pairs, pair, 0, unroll=4)
    for k in range(8):
        row = (k // 4) * 8 + k % 4
        out[:, k * LANES : (k + 1) * LANES] = (
            cross[pl.ds(row, pairs, stride=24), :] + cross[pl.ds(row + 4, pairs, stride=24), :]
        ).astype(jnp.bfloat16)
    for k in range(2):
        row = 16 + 2 * k
        out[:, (8 + k) * LANES : (9 + k) * LANES] = (
            cross[pl.ds(row, pairs, stride=24), :] + cross[pl.ds(row + 1, pairs, stride=24), :]
        ).astype(jnp.bfloat16)


def cross_spectra(kernel, name, first, second, bufs, rows, columns):
    pairs = first.shape[0]
    slots = sum(buf.shape[0] for buf in bufs)
    return pl.pallas_call(
        functools.partial(kernel, len(bufs)),
        name=name,
        out_shape=jax.ShapeDtypeStruct((pairs, columns), jnp.bfloat16),
        in_specs=[SMEM, SMEM] + [VMEM] * len(bufs),
        out_specs=VMEM,
        scratch_shapes=[
            pltpu.VMEM((slots,) + bufs[0].shape[1:], jnp.float32),
            pltpu.VMEM((pairs * rows, LANES), jnp.float32),
        ],
        compiler_params=params(),
        cost_estimate=pl.CostEstimate(
            flops=pairs * columns * 12, bytes_accessed=pairs * columns * 2, transcendentals=0
        ),
    )(first, second, *bufs)


def table_kernel(coarse_ref, fine_ref, big_ref, small_ref):
    half = fine_ref.shape[2] // LANES - 1
    for g in range(half + 1):
        at = slice(g * LANES, (g + 1) * LANES)
        cf = fine_ref[0, :, at]
        sf = fine_ref[1, :, at]
        if g < 8:
            ref, re, im = big_ref, g, g + 8
        elif g < half:
            ref, re, im = small_ref, g - 8, g - 8 + half - 8
        else:
            ref, re, im = small_ref, 2 * (half - 8), 2 * (half - 8) + 1
        for u in range(coarse_ref.shape[1]):
            cc = coarse_ref[0, u : u + 1, at]
            sc = coarse_ref[1, u : u + 1, at]
            rows = slice(u * FINE, (u + 1) * FINE)
            ref[rows, re * LANES : (re + 1) * LANES] = (cc * cf - sc * sf).astype(jnp.bfloat16)
            ref[rows, im * LANES : (im + 1) * LANES] = -(sc * cf + cc * sf).astype(jnp.bfloat16)


def lag_table(core, half, blocks):
    block_index = jnp.concatenate(
        [core * half + jnp.arange(half, dtype=jnp.int32), jnp.full((1,), blocks - 1, jnp.int32)]
    )
    bins = (K0 + block_index[:, None] * LANES + jnp.arange(LANES, dtype=jnp.int32)).reshape(-1)

    def base(lags):
        angles = (lags[:, None] * bins[None, :] % NFFT).astype(jnp.float32) * (2.0 * math.pi / NFFT)
        return jnp.stack([jnp.cos(angles), jnp.sin(angles)])

    coarse = base(jnp.arange(LAGS // FINE, dtype=jnp.int32) * FINE - LAGS // 2)
    fine = base(jnp.arange(FINE, dtype=jnp.int32))
    width = bins.shape[0]
    step = 8
    return pl.pallas_call(
        table_kernel,
        name="lagtable",
        grid=(LAGS // FINE // step,),
        out_shape=(
            jax.ShapeDtypeStruct((LAGS, 16 * LANES), jnp.bfloat16),
            jax.ShapeDtypeStruct((LAGS, 2 * (half + 1 - 8) * LANES), jnp.bfloat16),
        ),
        in_specs=[
            pl.BlockSpec((2, step, width), lambda u: (0, u, 0)),
            pl.BlockSpec((2, FINE, width), lambda u: (0, 0, 0)),
        ],
        out_specs=(
            pl.BlockSpec((step * FINE, 16 * LANES), lambda u: (u, 0)),
            pl.BlockSpec((step * FINE, 2 * (half + 1 - 8) * LANES), lambda u: (u, 0)),
        ),
        compiler_params=params(),
        cost_estimate=pl.CostEstimate(
            flops=LAGS * width * 6, bytes_accessed=LAGS * width * 4, transcendentals=0
        ),
    )(coarse, fine)


def dot_nt(a, b):
    return lax.dot_general(a, b, (((1,), (1,)), ((), ())), preferred_element_type=jnp.float32)


def matmul_kernel(table_ref, cross_ref, out_ref):
    out_ref[...] = dot_nt(table_ref[...], cross_ref[...])


def matmul(table, cross, tile):
    lags, depth = table.shape
    pairs = cross.shape[0]
    return pl.pallas_call(
        matmul_kernel,
        name="stack0",
        grid=(lags // tile,),
        out_shape=jax.ShapeDtypeStruct((lags, pairs), jnp.float32),
        in_specs=[
            pl.BlockSpec((tile, depth), lambda i: (i, 0)),
            pl.BlockSpec((pairs, depth), lambda i: (0, 0)),
        ],
        out_specs=pl.BlockSpec((tile, pairs), lambda i: (i, 0)),
        compiler_params=params(),
        cost_estimate=pl.CostEstimate(
            flops=2 * lags * depth * pairs,
            bytes_accessed=2 * lags * depth + 4 * lags * pairs,
            transcendentals=0,
        ),
    )(table, cross)


def final_kernel(outer, core_ref, table_ref, cross_ref, acc_ref, send_ref, keep_ref):
    i = pl.program_id(0)
    value = acc_ref[...] + dot_nt(table_ref[...], cross_ref[...])

    @pl.when(i < outer)
    def _():
        send_ref[0] = value.astype(send_ref.dtype)

    @pl.when(i >= outer)
    def _():
        keep_ref[0] = value


def final_matmul(core, table, cross, acc, groups, part, parts):
    lags, depth = table.shape
    pairs = cross.shape[0]
    outer = groups // 2
    tile = lags // groups // parts

    def rows(i, core_ref):
        mine = i // outer
        group = 2 * (i % outer) + (core_ref[0] + 1 + mine) % 2
        return group * parts + part, 0

    return pl.pallas_call(
        functools.partial(final_kernel, outer),
        name=f"stack1_{part}",
        grid_spec=pltpu.PrefetchScalarGridSpec(
            num_scalar_prefetch=1,
            grid=(groups,),
            in_specs=[
                pl.BlockSpec((tile, depth), rows),
                pl.BlockSpec((pairs, depth), lambda i, core_ref: (0, 0)),
                pl.BlockSpec((tile, pairs), rows),
            ],
            out_specs=(
                pl.BlockSpec((1, tile, pairs), lambda i, core_ref: (jnp.minimum(i, outer - 1), 0, 0)),
                pl.BlockSpec((1, tile, pairs), lambda i, core_ref: (jnp.maximum(i - outer, 0), 0, 0)),
            ),
        ),
        out_shape=(
            jax.ShapeDtypeStruct((outer, tile, pairs), jnp.bfloat16),
            jax.ShapeDtypeStruct((outer, tile, pairs), jnp.float32),
        ),
        compiler_params=params(),
        cost_estimate=pl.CostEstimate(
            flops=2 * lags // parts * depth * pairs,
            bytes_accessed=(2 * lags * depth + 8 * lags * pairs) // parts,
            transcendentals=0,
        ),
    )(core, table, cross, acc)


def swap(x, axis, mask):
    return lax.ppermute(x, axis, [(i, i ^ mask) for i in range(lax.axis_size(axis))])


def local(spectra, requests, pair_first, pair_second):
    stations, windows, parts, bins = spectra.shape
    sources = lax.axis_size("pairs")
    groups = lax.axis_size("win")
    cap = requests.shape[2]
    me = lax.axis_index("pairs").astype(jnp.int32)
    group = lax.axis_index("win").astype(jnp.int32)
    core = group % 2
    blocks = bins // LANES
    half = blocks // 2
    wanted = requests[0]

    raw = spectra.reshape(stations, windows, parts, blocks, LANES).transpose(0, 1, 3, 2, 4)
    other = lax.dynamic_slice_in_dim(raw, (1 - core) * half, half, axis=2)
    got = swap(other, "win", 1)
    big, small = whiten(
        core[None],
        raw.reshape(-1, LANES),
        got.reshape(-1, LANES),
        stations,
        half,
        blocks,
    )

    slots = sources * cap
    if sources & (sources - 1) == 0 and 4 <= sources <= 16:
        far = sources // 2
        asked = [wanted] + [swap(wanted, "pairs", d) for d in range(1, far)]
        exchange = []
        for chunk in (big, small):
            far_chunk = swap(chunk, "pairs", far)
            outs = select(me[None], asked, chunk, far_chunk, cap)
            exchange.append([outs[0]] + [swap(outs[d], "pairs", d) for d in range(1, far)])

        def row_of(slot):
            apart = (slot // cap) ^ me
            return (apart % far) * (2 * cap) + (apart // far) * cap + slot % cap

    else:
        asked_rows = lax.all_to_all(wanted, "pairs", split_axis=0, concat_axis=0, tiled=True)
        exchange = []
        for chunk in (big, small):
            outgoing = chunk[jnp.maximum(asked_rows, 0)]
            arrived = lax.all_to_all(outgoing, "pairs", split_axis=0, concat_axis=0, tiled=True)
            exchange.append([arrived.reshape((slots,) + chunk.shape[1:])])

        def row_of(slot):
            return slot

    first = row_of(pair_first)
    second = row_of(pair_second)
    table_big, table_small = lag_table(core, half, blocks)
    pairs = pair_first.shape[0]
    cross_big = cross_spectra(
        cross_big_kernel, "cross0", first, second, exchange[0], 16, table_big.shape[1]
    )
    acc = matmul(table_big, cross_big, LAGS // groups)
    cross_small = cross_spectra(
        cross_small_kernel, "cross1", first, second, exchange[1], 24, table_small.shape[1]
    )

    norm_scale = 1.0 / math.sqrt(bins * windows * groups)
    outer = groups // 2
    place = group // 2
    pieces = []
    parts_out = 2
    for part in range(parts_out):
        send, keep = final_matmul(core[None], table_small, cross_small, acc, groups, part, parts_out)
        summed = keep + swap(send, "win", 1).astype(jnp.float32)
        piece = lax.dynamic_index_in_dim(summed, place, 0, keepdims=False)
        for d in range(1, outer):
            away = lax.dynamic_index_in_dim(summed, place ^ d, 0, keepdims=False)
            piece = piece + swap(away.astype(jnp.bfloat16), "win", 2 * d).astype(jnp.float32)
        pieces.append(piece)
    return norm_scale * jnp.concatenate(pieces, axis=0)


def solution(mesh):
    return jax.shard_map(
        local,
        mesh=mesh,
        in_specs=(P("pairs", "win", None, None), P("pairs", None, None), P("pairs"), P("pairs")),
        out_specs=P("win", "pairs"),
        check_vma=False,
    )
```

```python
import functools
import math

import jax
import jax.numpy as jnp
from jax import lax
from jax.experimental import pallas as pl
from jax.experimental.pallas import tpu as pltpu
from jax.sharding import PartitionSpec as P

LAGS = 2048
NFFT = 18000
K0 = 360
LANES = 128
EPS = 1e-06
FINE = 32
VMEM = pl.BlockSpec(memory_space=pltpu.VMEM)
SMEM = pl.BlockSpec(memory_space=pltpu.SMEM)


def params(*nbytes):
    return pltpu.CompilerParams(vmem_limit_bytes=sum(nbytes) + 4 * 1024 * 1024)


def size(shape, dtype):
    return math.prod(shape) * jnp.dtype(dtype).itemsize


def whiten_kernel(core_ref, raw_ref, keep_big, keep_small, give_big, give_small, tmp):
    stations, windows, _, bins = raw_ref.shape
    blocks = bins // LANES
    half = blocks // 2
    core = core_ref[0]

    def white(re, im):
        power = jnp.sum(re * re + im * im, axis=1, keepdims=True) * (1.0 / (2 * LANES))
        scale = lax.rsqrt(power + EPS)
        return re * scale, im * scale

    def station(s, slot):
        for w in range(windows):
            for b in range(blocks):
                value = raw_ref[s, w, :, b * LANES : (b + 1) * LANES]
                side, at = divmod(b, half)
                if side == 2:
                    row = 96 + w
                elif at < 8:
                    row = side * 48 + w * 16 + at
                else:
                    row = side * 48 + 32 + w * 4 + at - 8
                tmp[slot, pl.ds(row, 2, stride=8), :] = value
        for mine, big, small in ((True, keep_big, keep_small), (False, give_big, give_small)):
            base = pl.multiple_of((core if mine else 1 - core) * 48, 16)
            for g in range(3):
                re = tmp[slot, pl.ds(base + g * 16, 8), :]
                im = tmp[slot, pl.ds(base + g * 16 + 8, 8), :]
                rows = jnp.concatenate(white(re, im), axis=0).astype(jnp.bfloat16)
                if g < 2:
                    big[s, g * 16 : g * 16 + 16, :] = rows
                else:
                    small[s, 0:16, :] = rows
        re, im = white(tmp[slot, 96:104, :], tmp[slot, 104:112, :])
        tmp[slot, 112:114, :] = re[0:windows]
        tmp[slot, 114:116, :] = im[0:windows]
        keep_small[s, 16:24, :] = tmp[slot, 112:120, :].astype(jnp.bfloat16)

    tmp[...] = jnp.zeros_like(tmp)

    def several(i, carry):
        for slot in range(2):
            station(2 * i + slot, slot)
        return carry

    lax.fori_loop(0, stations // 2, several, 0)


def whiten(core, raw):
    stations = raw.shape[0]
    rows = (32, 24, 32, 16)
    return pl.pallas_call(
        whiten_kernel,
        name="whiten",
        out_shape=tuple(jax.ShapeDtypeStruct((stations, r, LANES), jnp.bfloat16) for r in rows),
        in_specs=[SMEM, VMEM],
        out_specs=(VMEM,) * 4,
        scratch_shapes=[pltpu.VMEM((2, 120, LANES), jnp.float32)],
        compiler_params=params(2 * size(raw.shape, raw.dtype)),
        cost_estimate=pl.CostEstimate(flops=2_000_000, bytes_accessed=2_000_000, transcendentals=0),
    )(core, raw)


def join(keep, got, small):
    if small:
        return jnp.concatenate([keep[:, :16], got, keep[:, 16:]], axis=1)
    return jnp.concatenate([keep, got], axis=1)


def select_kernel(peers, sources, cap, small, me_ref, *refs):
    asked = refs[:peers]
    chunks = refs[peers : peers + 4]
    outs = refs[peers + 4 :]
    me = me_ref[0]
    for d in range(peers):
        for h in range(2):
            source = me ^ (h * (sources // 2))
            keep, got = chunks[2 * h : 2 * h + 2]
            for c in range(cap):
                row = jnp.maximum(asked[d][source, c], 0)
                out = outs[d].at[h * cap + c]
                if small:
                    out[0:16] = keep[row, 0:16]
                    out[16:32] = got[row]
                    out[32:40] = keep[row, 16:24]
                else:
                    out[0:32] = keep[row]
                    out[32:64] = got[row]


def select(me, asked, chunks, cap, small):
    peers = len(asked)
    sources = asked[0].shape[0]
    rows = chunks[0].shape[1] + chunks[1].shape[1]
    out = jax.ShapeDtypeStruct((2 * cap, rows, LANES), chunks[0].dtype)
    return pl.pallas_call(
        functools.partial(select_kernel, peers, sources, cap, small),
        name="select",
        out_shape=(out,) * peers,
        in_specs=[SMEM] * (1 + peers) + [VMEM] * 4,
        out_specs=(VMEM,) * peers,
        compiler_params=params(2 * (peers + 2) * size(out.shape, out.dtype)),
        cost_estimate=pl.CostEstimate(flops=0, bytes_accessed=1_000_000, transcendentals=0),
    )(me, *asked, *chunks)


def load_table(bufs, table):
    at = 0
    for buf in bufs:

        def copy(i, carry, buf=buf, at=at):
            table[at + i] = buf[i].astype(jnp.float32)
            return carry

        lax.fori_loop(0, buf.shape[0], copy, 0, unroll=4)
        at += buf.shape[0]


def products(table, i, j, groups):
    re = im = None
    for g in range(groups):
        ar = table[i, g * 16 : g * 16 + 8, :]
        ai = table[i, g * 16 + 8 : g * 16 + 16, :]
        br = table[j, g * 16 : g * 16 + 8, :]
        bi = table[j, g * 16 + 8 : g * 16 + 16, :]
        r = ar * br + ai * bi
        m = ai * br - ar * bi
        re = r if re is None else re + r
        im = m if im is None else im + m
    return re, im


BIG_ROWS = 17
SMALL_ROWS = 25


def cross_big(first_ref, second_ref, bufs, table, cross, out):
    pairs = out.shape[0]
    load_table(bufs, table)

    def pair(p, carry):
        re, im = products(table, first_ref[p], second_ref[p], 4)
        cross[pl.ds(p * BIG_ROWS, 8), :] = re
        cross[pl.ds(p * BIG_ROWS + 8, 8), :] = im
        return carry

    lax.fori_loop(0, pairs, pair, 0, unroll=8)
    for k in range(16):
        out[:, k * LANES : (k + 1) * LANES] = cross[pl.ds(k, pairs, stride=BIG_ROWS), :].astype(
            jnp.bfloat16
        )


def cross_small(first_ref, second_ref, bufs, table, cross, out):
    pairs = out.shape[0]
    load_table(bufs, table)

    def pair(p, carry):
        i = first_ref[p]
        j = second_ref[p]
        re, im = products(table, i, j, 2)
        at = p * SMALL_ROWS
        cross[pl.ds(at, 8), :] = re
        cross[pl.ds(at + 8, 8), :] = im
        a = table[i, 32:40, :]
        b = table[j, 32:40, :]
        cross[pl.ds(at + 16, 2), :] = a[0:2] * b[0:2] + a[2:4] * b[2:4]
        cross[pl.ds(at + 18, 2), :] = a[2:4] * b[0:2] - a[0:2] * b[2:4]
        return carry

    lax.fori_loop(0, pairs, pair, 0, unroll=8)

    def column(row):
        return cross[pl.ds(row, pairs, stride=SMALL_ROWS), :]

    for k in range(8):
        row = (k // 4) * 8 + k % 4
        out[:, k * LANES : (k + 1) * LANES] = (column(row) + column(row + 4)).astype(jnp.bfloat16)
    for k in range(2):
        row = 16 + 2 * k
        out[:, (8 + k) * LANES : (9 + k) * LANES] = (column(row) + column(row + 1)).astype(
            jnp.bfloat16
        )


def table_kernel(coarse_ref, fine_ref, big_ref, small_ref):
    half = fine_ref.shape[2] // LANES - 1
    for g in range(half + 1):
        at = slice(g * LANES, (g + 1) * LANES)
        cf = fine_ref[0, :, at]
        sf = fine_ref[1, :, at]
        if g < 8:
            ref, re, im = big_ref, g, g + 8
        elif g < half:
            ref, re, im = small_ref, g - 8, g - 8 + half - 8
        else:
            ref, re, im = small_ref, 2 * (half - 8), 2 * (half - 8) + 1
        for u in range(coarse_ref.shape[1]):
            cc = coarse_ref[0, u : u + 1, at]
            sc = coarse_ref[1, u : u + 1, at]
            rows = slice(u * FINE, (u + 1) * FINE)
            ref[rows, re * LANES : (re + 1) * LANES] = (cc * cf - sc * sf).astype(jnp.bfloat16)
            ref[rows, im * LANES : (im + 1) * LANES] = (sc * cf + cc * sf).astype(jnp.bfloat16)


def lag_table(core, half, blocks):
    block_index = jnp.concatenate(
        [core * half + jnp.arange(half, dtype=jnp.int32), jnp.full((1,), blocks - 1, jnp.int32)]
    )
    bins = (K0 + block_index[:, None] * LANES + jnp.arange(LANES, dtype=jnp.int32)).reshape(-1)

    def base(lags):
        angles = (lags[:, None] * bins[None, :] % NFFT).astype(jnp.float32) * (2.0 * math.pi / NFFT)
        return jnp.stack([jnp.cos(angles), -jnp.sin(angles)])

    coarse = base(jnp.arange(LAGS // FINE, dtype=jnp.int32) * FINE - LAGS // 2)
    fine = base(jnp.arange(FINE, dtype=jnp.int32))
    width = bins.shape[0]
    step = 8
    return pl.pallas_call(
        table_kernel,
        name="lagtable",
        grid=(LAGS // FINE // step,),
        out_shape=(
            jax.ShapeDtypeStruct((LAGS, 16 * LANES), jnp.bfloat16),
            jax.ShapeDtypeStruct((LAGS, 2 * (half + 1 - 8) * LANES), jnp.bfloat16),
        ),
        in_specs=[
            pl.BlockSpec((2, step, width), lambda u: (0, u, 0)),
            pl.BlockSpec((2, FINE, width), lambda u: (0, 0, 0)),
        ],
        out_specs=(
            pl.BlockSpec((step * FINE, 16 * LANES), lambda u: (u, 0)),
            pl.BlockSpec((step * FINE, 2 * (half + 1 - 8) * LANES), lambda u: (u, 0)),
        ),
        compiler_params=params(),
        cost_estimate=pl.CostEstimate(
            flops=LAGS * width * 6, bytes_accessed=LAGS * width * 4, transcendentals=0
        ),
    )(coarse, fine)


def dot_nt(a, b):
    return lax.dot_general(a, b, (((1,), (1,)), ((), ())), preferred_element_type=jnp.float32)


def whole(shape):
    return pl.BlockSpec(shape, lambda *_: (0,) * len(shape), pipeline_mode=pl.Buffered(1))


def stack_big_kernel(count, first_ref, second_ref, *refs):
    bufs = refs[:count]
    lag_ref, acc_ref, table, rows, cross = refs[count:]

    @pl.when(pl.program_id(0) == 0)
    def _():
        cross_big(first_ref, second_ref, bufs, table, rows, cross)

    acc_ref[...] = dot_nt(lag_ref[...], cross[...])


def stack_big(first, second, bufs, lag_table, tile):
    lags, depth = lag_table.shape
    pairs = first.shape[0]
    slots = sum(buf.shape[0] for buf in bufs)
    table = ((slots,) + bufs[0].shape[1:], jnp.float32)
    rows = ((pairs * BIG_ROWS, LANES), jnp.float32)
    cross = ((pairs, depth), jnp.bfloat16)
    return pl.pallas_call(
        functools.partial(stack_big_kernel, len(bufs)),
        name="stack0",
        grid=(lags // tile,),
        out_shape=jax.ShapeDtypeStruct((lags, pairs), jnp.float32),
        in_specs=[SMEM, SMEM]
        + [whole(buf.shape) for buf in bufs]
        + [pl.BlockSpec((tile, depth), lambda i: (i, 0))],
        out_specs=pl.BlockSpec((tile, pairs), lambda i: (i, 0)),
        scratch_shapes=[pltpu.VMEM(*table), pltpu.VMEM(*rows), pltpu.VMEM(*cross)],
        compiler_params=params(
            size(*table),
            size(table[0], jnp.bfloat16),
            size(*rows),
            size(*cross),
            2 * size((tile, depth), jnp.bfloat16),
            2 * size((tile, pairs), jnp.float32),
        ),
        cost_estimate=pl.CostEstimate(
            flops=2 * lags * depth * pairs,
            bytes_accessed=2 * lags * depth + 4 * lags * pairs,
            transcendentals=0,
        ),
    )(first, second, *bufs, lag_table)


def finish(outer, lag_ref, cross, acc_ref, send_ref, keep_ref):
    i = pl.program_id(0)
    value = acc_ref[...] + dot_nt(lag_ref[...], cross[...])

    @pl.when(i < outer)
    def _():
        send_ref[0] = value.astype(send_ref.dtype)

    @pl.when(i >= outer)
    def _():
        keep_ref[0] = value


def stack_first_kernel(outer, count, core_ref, first_ref, second_ref, *refs):
    bufs = refs[:count]
    lag_ref, acc_ref, send_ref, keep_ref, cross, table, rows = refs[count:]

    @pl.when(pl.program_id(0) == 0)
    def _():
        cross_small(first_ref, second_ref, bufs, table, rows, cross)

    finish(outer, lag_ref, cross, acc_ref, send_ref, keep_ref)


def stack_next_kernel(outer, core_ref, cross, lag_ref, acc_ref, send_ref, keep_ref):
    finish(outer, lag_ref, cross, acc_ref, send_ref, keep_ref)


def stack_small(core, lag_table, acc, groups, part, parts, first=None, second=None, bufs=None, cross=None):
    lags, depth = lag_table.shape
    pairs = acc.shape[1]
    outer = groups // 2
    tile = lags // groups // parts

    def block(i, core_ref):
        group = 2 * (i % outer) + (core_ref[0] + 1 + i // outer) % 2
        return group * parts + part, 0

    tiles = [pl.BlockSpec((tile, depth), block), pl.BlockSpec((tile, pairs), block)]
    out_shape = [
        jax.ShapeDtypeStruct((outer, tile, pairs), jnp.bfloat16),
        jax.ShapeDtypeStruct((outer, tile, pairs), jnp.float32),
    ]
    out_specs = [
        pl.BlockSpec((1, tile, pairs), lambda i, core_ref: (jnp.minimum(i, outer - 1), 0, 0)),
        pl.BlockSpec((1, tile, pairs), lambda i, core_ref: (jnp.maximum(i - outer, 0), 0, 0)),
    ]
    nbytes = [
        size((pairs, depth), jnp.bfloat16),
        2 * size((tile, depth), jnp.bfloat16),
        5 * size((tile, pairs), jnp.float32),
    ]
    if cross is None:
        slots = sum(buf.shape[0] for buf in bufs)
        table = ((slots,) + bufs[0].shape[1:], jnp.float32)
        rows = ((pairs * SMALL_ROWS, LANES), jnp.float32)
        kernel = functools.partial(stack_first_kernel, outer, len(bufs))
        operands = (first, second, *bufs, lag_table, acc)
        in_specs = [SMEM, SMEM] + [whole(buf.shape) for buf in bufs] + tiles
        scratch = [pltpu.VMEM(*table), pltpu.VMEM(*rows)]
        nbytes += [size(*table), size(table[0], jnp.bfloat16), size(*rows)]
        out_shape.append(jax.ShapeDtypeStruct((pairs, depth), jnp.bfloat16))
        out_specs.append(whole((pairs, depth)))
    else:
        kernel = functools.partial(stack_next_kernel, outer)
        operands = (cross, lag_table, acc)
        in_specs = [whole(cross.shape)] + tiles
        scratch = []
    return pl.pallas_call(
        kernel,
        name=f"stack1_{part}",
        grid_spec=pltpu.PrefetchScalarGridSpec(
            num_scalar_prefetch=1,
            grid=(groups,),
            in_specs=in_specs,
            out_specs=out_specs,
            scratch_shapes=scratch,
        ),
        out_shape=out_shape,
        compiler_params=params(*nbytes),
        cost_estimate=pl.CostEstimate(
            flops=2 * lags // parts * depth * pairs,
            bytes_accessed=(2 * lags * depth + 8 * lags * pairs) // parts,
            transcendentals=0,
        ),
    )(core, *operands)


def swap(x, axis, mask):
    return lax.ppermute(x, axis, [(i, i ^ mask) for i in range(lax.axis_size(axis))])


def local(spectra, requests, pair_first, pair_second):
    stations, windows, _, bins = spectra.shape
    sources = lax.axis_size("pairs")
    groups = lax.axis_size("win")
    cap = requests.shape[2]
    me = lax.axis_index("pairs").astype(jnp.int32)
    group = lax.axis_index("win").astype(jnp.int32)
    core = group & 1
    blocks = bins // LANES
    half = blocks // 2
    assert windows == 2 and blocks == 2 * half + 1 and half == 12 and groups % 2 == 0

    keep_big, keep_small, give_big, give_small = whiten(core[None], spectra)
    kept = (keep_big, keep_small)
    got = (swap(give_big, "win", 1), swap(give_small, "win", 1))

    slots = sources * cap
    wanted, _ = lax.optimization_barrier((requests[0], keep_big))
    exchange = []
    if sources & (sources - 1) == 0 and 4 <= sources <= 16:
        far = sources // 2
        asked = [wanted] + [swap(wanted, "pairs", d) for d in range(1, far)]
        for i in range(2):
            chunks = (kept[i], got[i], swap(kept[i], "pairs", far), swap(got[i], "pairs", far))
            outs = select(me[None], asked, chunks, cap, i == 1)
            exchange.append([outs[0]] + [swap(outs[d], "pairs", d) for d in range(1, far)])

        def row_of(slot):
            apart = (slot // cap) ^ me
            return (apart % far) * (2 * cap) + (apart // far) * cap + slot % cap

    else:
        asked_rows = lax.all_to_all(wanted, "pairs", split_axis=0, concat_axis=0, tiled=True)
        for i in range(2):
            chunk = join(kept[i], got[i], i == 1)
            outgoing = chunk[jnp.maximum(asked_rows, 0)]
            arrived = lax.all_to_all(outgoing, "pairs", split_axis=0, concat_axis=0, tiled=True)
            exchange.append([arrived.reshape((slots,) + chunk.shape[1:])])

        def row_of(slot):
            return slot

    first = row_of(pair_first)
    second = row_of(pair_second)
    table_big, table_small = lag_table(core, half, blocks)
    acc = stack_big(first, second, exchange[0], table_big, LAGS // groups)

    norm_scale = 1.0 / math.sqrt(bins * windows * groups)
    outer = groups // 2
    place = group >> 1
    parts = 2
    pieces = []
    cross = None
    for part in range(parts):
        if part == 0:
            send, keep, cross = stack_small(
                core[None], table_small, acc, groups, part, parts, first, second, exchange[1]
            )
        else:
            send, keep = stack_small(core[None], table_small, acc, groups, part, parts, cross=cross)
        near = swap(send, "win", 1)

        def total(at):
            return lax.dynamic_index_in_dim(keep, at, 0, False) + lax.dynamic_index_in_dim(
                near, at, 0, False
            ).astype(jnp.float32)

        away = [
            swap(total(place ^ d).astype(jnp.bfloat16), "win", 2 * d) for d in range(1, outer)
        ]
        pieces.append(sum((x.astype(jnp.float32) for x in away), total(place)))
    return norm_scale * jnp.concatenate(pieces, axis=0)


def solution(mesh):
    return jax.shard_map(
        local,
        mesh=mesh,
        in_specs=(P("pairs", "win", None, None), P("pairs", None, None), P("pairs"), P("pairs")),
        out_specs=P("win", "pairs"),
        check_vma=False,
    )
```

```python
import functools
import math

import jax
import jax.numpy as jnp
from jax import lax
from jax.experimental import pallas as pl
from jax.experimental.pallas import tpu as pltpu
from jax.sharding import PartitionSpec as P

LAGS = 2048
NFFT = 18000
K0 = 360
LANES = 128
EPS = 1e-06
FINE = 32
VMEM = pl.BlockSpec(memory_space=pltpu.VMEM)
SMEM = pl.BlockSpec(memory_space=pltpu.SMEM)


def params(*nbytes):
    return pltpu.CompilerParams(vmem_limit_bytes=sum(nbytes) + 4 * 1024 * 1024)


def size(shape, dtype):
    return math.prod(shape) * jnp.dtype(dtype).itemsize


def whiten_kernel(core_ref, raw_ref, keep_big, keep_small, give_big, give_small, tmp):
    stations, windows, _, bins = raw_ref.shape
    blocks = bins // LANES
    half = blocks // 2
    core = core_ref[0]

    def white(re, im):
        power = jnp.sum(re * re + im * im, axis=1, keepdims=True) * (1.0 / (2 * LANES))
        scale = lax.rsqrt(power + EPS)
        return re * scale, im * scale

    def station(s, slot):
        for w in range(windows):
            for b in range(blocks):
                value = raw_ref[s, w, :, b * LANES : (b + 1) * LANES]
                side, at = divmod(b, half)
                if side == 2:
                    row = 96 + w
                elif at < 8:
                    row = side * 48 + w * 16 + at
                else:
                    row = side * 48 + 32 + w * 4 + at - 8
                tmp[slot, pl.ds(row, 2, stride=8), :] = value
        for mine, big, small in ((True, keep_big, keep_small), (False, give_big, give_small)):
            base = pl.multiple_of((core if mine else 1 - core) * 48, 16)
            for g in range(3):
                re = tmp[slot, pl.ds(base + g * 16, 8), :]
                im = tmp[slot, pl.ds(base + g * 16 + 8, 8), :]
                rows = jnp.concatenate(white(re, im), axis=0).astype(jnp.bfloat16)
                if g < 2:
                    big[s, g * 16 : g * 16 + 16, :] = rows
                else:
                    small[s, 0:16, :] = rows
        re, im = white(tmp[slot, 96:104, :], tmp[slot, 104:112, :])
        tmp[slot, 112:114, :] = re[0:windows]
        tmp[slot, 114:116, :] = im[0:windows]
        keep_small[s, 16:24, :] = tmp[slot, 112:120, :].astype(jnp.bfloat16)

    tmp[...] = jnp.zeros_like(tmp)

    def several(i, carry):
        for slot in range(2):
            station(2 * i + slot, slot)
        return carry

    lax.fori_loop(0, stations // 2, several, 0)


def whiten(core, raw):
    stations = raw.shape[0]
    rows = (32, 24, 32, 16)
    return pl.pallas_call(
        whiten_kernel,
        name="whiten",
        out_shape=tuple(jax.ShapeDtypeStruct((stations, r, LANES), jnp.bfloat16) for r in rows),
        in_specs=[SMEM, VMEM],
        out_specs=(VMEM,) * 4,
        scratch_shapes=[pltpu.VMEM((2, 120, LANES), jnp.float32)],
        compiler_params=params(2 * size(raw.shape, raw.dtype)),
        cost_estimate=pl.CostEstimate(flops=2_000_000, bytes_accessed=2_000_000, transcendentals=0),
    )(core, raw)


def join(keep, got, small):
    if small:
        return jnp.concatenate([keep[:, :16], got, keep[:, 16:]], axis=1)
    return jnp.concatenate([keep, got], axis=1)


def select_kernel(peers, sources, cap, small, me_ref, *refs):
    asked = refs[:peers]
    chunks = refs[peers : peers + 4]
    outs = refs[peers + 4 :]
    me = me_ref[0]
    for d in range(peers):
        for h in range(2):
            source = me ^ (h * (sources // 2))
            keep, got = chunks[2 * h : 2 * h + 2]
            for c in range(cap):
                row = jnp.maximum(asked[d][source, c], 0)
                out = outs[d].at[h * cap + c]
                if small:
                    out[0:16] = keep[row, 0:16]
                    out[16:32] = got[row]
                    out[32:40] = keep[row, 16:24]
                else:
                    out[0:32] = keep[row]
                    out[32:64] = got[row]


def select(me, asked, chunks, cap, small):
    peers = len(asked)
    sources = asked[0].shape[0]
    rows = chunks[0].shape[1] + chunks[1].shape[1]
    out = jax.ShapeDtypeStruct((2 * cap, rows, LANES), chunks[0].dtype)
    return pl.pallas_call(
        functools.partial(select_kernel, peers, sources, cap, small),
        name="select",
        out_shape=(out,) * peers,
        in_specs=[SMEM] * (1 + peers) + [VMEM] * 4,
        out_specs=(VMEM,) * peers,
        compiler_params=params(2 * (peers + 2) * size(out.shape, out.dtype)),
        cost_estimate=pl.CostEstimate(flops=0, bytes_accessed=1_000_000, transcendentals=0),
    )(me, *asked, *chunks)


def load_table(bufs, table):
    at = 0
    for buf in bufs:

        def copy(i, carry, buf=buf, at=at):
            table[at + i] = buf[i].astype(jnp.float32)
            return carry

        lax.fori_loop(0, buf.shape[0], copy, 0, unroll=4)
        at += buf.shape[0]


def products(table, i, j, groups):
    re = im = None
    for g in range(groups):
        ar = table[i, g * 16 : g * 16 + 8, :]
        ai = table[i, g * 16 + 8 : g * 16 + 16, :]
        br = table[j, g * 16 : g * 16 + 8, :]
        bi = table[j, g * 16 + 8 : g * 16 + 16, :]
        r = ar * br + ai * bi
        m = ai * br - ar * bi
        re = r if re is None else re + r
        im = m if im is None else im + m
    return re, im


BIG_ROWS = 17
SMALL_ROWS = 25


def cross_big(first_ref, second_ref, bufs, table, cross, out):
    pairs = out.shape[0]
    load_table(bufs, table)

    def pair(p, carry):
        re, im = products(table, first_ref[p], second_ref[p], 4)
        cross[pl.ds(p * BIG_ROWS, 8), :] = re
        cross[pl.ds(p * BIG_ROWS + 8, 8), :] = im
        return carry

    lax.fori_loop(0, pairs, pair, 0, unroll=8)
    for k in range(16):
        out[:, k * LANES : (k + 1) * LANES] = cross[pl.ds(k, pairs, stride=BIG_ROWS), :].astype(
            jnp.bfloat16
        )


def cross_small(start, first_ref, second_ref, bufs, table, cross, out):
    pairs = out.shape[0]
    load_table(bufs, table)

    def pair(p, carry):
        i = first_ref[start + p]
        j = second_ref[start + p]
        re, im = products(table, i, j, 2)
        at = p * SMALL_ROWS
        cross[pl.ds(at, 8), :] = re
        cross[pl.ds(at + 8, 8), :] = im
        a = table[i, 32:40, :]
        b = table[j, 32:40, :]
        cross[pl.ds(at + 16, 2), :] = a[0:2] * b[0:2] + a[2:4] * b[2:4]
        cross[pl.ds(at + 18, 2), :] = a[2:4] * b[0:2] - a[0:2] * b[2:4]
        return carry

    lax.fori_loop(0, pairs, pair, 0, unroll=8)

    def column(row):
        return cross[pl.ds(row, pairs, stride=SMALL_ROWS), :]

    for k in range(8):
        row = (k // 4) * 8 + k % 4
        out[:, k * LANES : (k + 1) * LANES] = (column(row) + column(row + 4)).astype(jnp.bfloat16)
    for k in range(2):
        row = 16 + 2 * k
        out[:, (8 + k) * LANES : (9 + k) * LANES] = (column(row) + column(row + 1)).astype(
            jnp.bfloat16
        )


def table_kernel(coarse_ref, fine_ref, big_ref, small_ref):
    half = fine_ref.shape[2] // LANES - 1
    for g in range(half + 1):
        at = slice(g * LANES, (g + 1) * LANES)
        cf = fine_ref[0, :, at]
        sf = fine_ref[1, :, at]
        if g < 8:
            ref, re, im = big_ref, g, g + 8
        elif g < half:
            ref, re, im = small_ref, g - 8, g - 8 + half - 8
        else:
            ref, re, im = small_ref, 2 * (half - 8), 2 * (half - 8) + 1
        for u in range(coarse_ref.shape[1]):
            cc = coarse_ref[0, u : u + 1, at]
            sc = coarse_ref[1, u : u + 1, at]
            rows = slice(u * FINE, (u + 1) * FINE)
            ref[rows, re * LANES : (re + 1) * LANES] = (cc * cf - sc * sf).astype(jnp.bfloat16)
            ref[rows, im * LANES : (im + 1) * LANES] = (sc * cf + cc * sf).astype(jnp.bfloat16)


def lag_table(core, half, blocks):
    block_index = jnp.concatenate(
        [core * half + jnp.arange(half, dtype=jnp.int32), jnp.full((1,), blocks - 1, jnp.int32)]
    )
    bins = (K0 + block_index[:, None] * LANES + jnp.arange(LANES, dtype=jnp.int32)).reshape(-1)

    def base(lags):
        angles = (lags[:, None] * bins[None, :] % NFFT).astype(jnp.float32) * (2.0 * math.pi / NFFT)
        return jnp.stack([jnp.cos(angles), -jnp.sin(angles)])

    coarse = base(jnp.arange(LAGS // FINE, dtype=jnp.int32) * FINE - LAGS // 2)
    fine = base(jnp.arange(FINE, dtype=jnp.int32))
    width = bins.shape[0]
    step = 8
    return pl.pallas_call(
        table_kernel,
        name="lagtable",
        grid=(LAGS // FINE // step,),
        out_shape=(
            jax.ShapeDtypeStruct((LAGS, 16 * LANES), jnp.bfloat16),
            jax.ShapeDtypeStruct((LAGS, 2 * (half + 1 - 8) * LANES), jnp.bfloat16),
        ),
        in_specs=[
            pl.BlockSpec((2, step, width), lambda u: (0, u, 0)),
            pl.BlockSpec((2, FINE, width), lambda u: (0, 0, 0)),
        ],
        out_specs=(
            pl.BlockSpec((step * FINE, 16 * LANES), lambda u: (u, 0)),
            pl.BlockSpec((step * FINE, 2 * (half + 1 - 8) * LANES), lambda u: (u, 0)),
        ),
        compiler_params=params(),
        cost_estimate=pl.CostEstimate(
            flops=LAGS * width * 6, bytes_accessed=LAGS * width * 4, transcendentals=0
        ),
    )(coarse, fine)


def dot_nt(a, b):
    return lax.dot_general(a, b, (((1,), (1,)), ((), ())), preferred_element_type=jnp.float32)


def whole(shape):
    return pl.BlockSpec(shape, lambda *_: (0,) * len(shape), pipeline_mode=pl.Buffered(1))


def stack_big_kernel(count, first_ref, second_ref, *refs):
    bufs = refs[:count]
    lag_ref, acc_ref, table, rows, cross = refs[count:]

    @pl.when(pl.program_id(0) == 0)
    def _():
        cross_big(first_ref, second_ref, bufs, table, rows, cross)

    acc_ref[...] = dot_nt(lag_ref[...], cross[...])


def stack_big(first, second, bufs, lag_table, tile):
    lags, depth = lag_table.shape
    pairs = first.shape[0]
    slots = sum(buf.shape[0] for buf in bufs)
    table = ((slots,) + bufs[0].shape[1:], jnp.float32)
    rows = ((pairs * BIG_ROWS, LANES), jnp.float32)
    cross = ((pairs, depth), jnp.bfloat16)
    return pl.pallas_call(
        functools.partial(stack_big_kernel, len(bufs)),
        name="stack0",
        grid=(lags // tile,),
        out_shape=jax.ShapeDtypeStruct((lags, pairs), jnp.float32),
        in_specs=[SMEM, SMEM]
        + [whole(buf.shape) for buf in bufs]
        + [pl.BlockSpec((tile, depth), lambda i: (i, 0))],
        out_specs=pl.BlockSpec((tile, pairs), lambda i: (i, 0)),
        scratch_shapes=[pltpu.VMEM(*table), pltpu.VMEM(*rows), pltpu.VMEM(*cross)],
        compiler_params=params(
            size(*table),
            size(table[0], jnp.bfloat16),
            size(*rows),
            size(*cross),
            2 * size((tile, depth), jnp.bfloat16),
            2 * size((tile, pairs), jnp.float32),
        ),
        cost_estimate=pl.CostEstimate(
            flops=2 * lags * depth * pairs,
            bytes_accessed=2 * lags * depth + 4 * lags * pairs,
            transcendentals=0,
        ),
    )(first, second, *bufs, lag_table)


def stack_small_kernel(outer, start, count, core_ref, first_ref, second_ref, *refs):
    bufs = refs[:count]
    lag_ref, acc_ref, send_ref, keep_ref, table, rows, cross = refs[count:]
    i = pl.program_id(0)

    @pl.when(i == 0)
    def _():
        cross_small(start, first_ref, second_ref, bufs, table, rows, cross)

    value = acc_ref[...] + dot_nt(lag_ref[...], cross[...])

    @pl.when(i < outer)
    def _():
        send_ref[0] = value.astype(send_ref.dtype)

    @pl.when(i >= outer)
    def _():
        keep_ref[0] = value


def stack_small(core, first, second, bufs, lag_table, acc, groups, part, parts):
    lags, depth = lag_table.shape
    pairs = acc.shape[1] // parts
    outer = groups // 2
    tile = lags // groups

    def group(i, core_ref):
        return 2 * (i % outer) + (core_ref[0] + 1 + i // outer) % 2

    slots = sum(buf.shape[0] for buf in bufs)
    table = ((slots,) + bufs[0].shape[1:], jnp.float32)
    rows = ((pairs * SMALL_ROWS, LANES), jnp.float32)
    cross = ((pairs, depth), jnp.bfloat16)
    return pl.pallas_call(
        functools.partial(stack_small_kernel, outer, part * pairs, len(bufs)),
        name=f"stack1_{part}",
        grid_spec=pltpu.PrefetchScalarGridSpec(
            num_scalar_prefetch=1,
            grid=(groups,),
            in_specs=[SMEM, SMEM]
            + [whole(buf.shape) for buf in bufs]
            + [
                pl.BlockSpec((tile, depth), lambda i, core_ref: (group(i, core_ref), 0)),
                pl.BlockSpec((tile, pairs), lambda i, core_ref: (group(i, core_ref), part)),
            ],
            out_specs=[
                pl.BlockSpec((1, tile, pairs), lambda i, core_ref: (jnp.minimum(i, outer - 1), 0, 0)),
                pl.BlockSpec((1, tile, pairs), lambda i, core_ref: (jnp.maximum(i - outer, 0), 0, 0)),
            ],
            scratch_shapes=[pltpu.VMEM(*table), pltpu.VMEM(*rows), pltpu.VMEM(*cross)],
        ),
        out_shape=[
            jax.ShapeDtypeStruct((outer, tile, pairs), jnp.bfloat16),
            jax.ShapeDtypeStruct((outer, tile, pairs), jnp.float32),
        ],
        compiler_params=params(
            size(*table),
            size(table[0], jnp.bfloat16),
            size(*rows),
            size(*cross),
            2 * size((tile, depth), jnp.bfloat16),
            6 * size((tile, pairs), jnp.float32),
        ),
        cost_estimate=pl.CostEstimate(
            flops=2 * lags * depth * pairs,
            bytes_accessed=2 * lags * depth + 8 * lags * pairs,
            transcendentals=0,
        ),
    )(core, first, second, *bufs, lag_table, acc)


def away_kernel(place_ref, keep_ref, near_ref, *outs):
    for d, out in enumerate(outs):
        at = place_ref[0] ^ (d + 1)
        out[...] = (keep_ref[at] + near_ref[at].astype(jnp.float32)).astype(out.dtype)


def sum_away(place, keep, near):
    outer, lags, pairs = keep.shape
    return pl.pallas_call(
        away_kernel,
        name="away",
        out_shape=[jax.ShapeDtypeStruct((lags, pairs), near.dtype)] * (outer - 1),
        in_specs=[SMEM, VMEM, VMEM],
        out_specs=[VMEM] * (outer - 1),
        compiler_params=params(2 * size(keep.shape, jnp.float32)),
        cost_estimate=pl.CostEstimate(
            flops=keep.size, bytes_accessed=6 * keep.size, transcendentals=0
        ),
    )(place, keep, near)


def result_kernel(scale, parts, place_ref, *refs):
    out = refs[-1]
    each = (len(refs) - 1) // parts
    place = place_ref[0]
    for part in range(parts):
        keep, near, *far = refs[part * each : (part + 1) * each]
        total = keep[place] + near[place].astype(jnp.float32)
        for ref in far:
            total = total + ref[...].astype(jnp.float32)
        pairs = total.shape[1]
        out[:, part * pairs : (part + 1) * pairs] = scale * total


def result(place, pieces, scale):
    operands = [x for piece in pieces for x in piece]
    _, lags, pairs = pieces[0][0].shape
    return pl.pallas_call(
        functools.partial(result_kernel, scale, len(pieces)),
        name="result",
        out_shape=jax.ShapeDtypeStruct((lags, pairs * len(pieces)), jnp.float32),
        in_specs=[SMEM] + [VMEM] * len(operands),
        out_specs=VMEM,
        compiler_params=params(
            *(size(x.shape, x.dtype) for x in operands), 2 * size((lags, pairs * len(pieces)), jnp.float32)
        ),
        cost_estimate=pl.CostEstimate(
            flops=lags * pairs * 4, bytes_accessed=lags * pairs * 16, transcendentals=0
        ),
    )(place, *operands)


def swap(x, axis, mask):
    return lax.ppermute(x, axis, [(i, i ^ mask) for i in range(lax.axis_size(axis))])


def swap_both(x, mask_pairs, mask_win):
    groups = lax.axis_size("win")
    perm = [
        (p * groups + w, (p ^ mask_pairs) * groups + (w ^ mask_win))
        for p in range(lax.axis_size("pairs"))
        for w in range(groups)
    ]
    return lax.ppermute(x, ("pairs", "win"), perm)


def after(x, *earlier):
    return lax.optimization_barrier((x,) + earlier)[0]


def local(spectra, requests, pair_first, pair_second):
    stations, windows, _, bins = spectra.shape
    sources = lax.axis_size("pairs")
    groups = lax.axis_size("win")
    cap = requests.shape[2]
    me = lax.axis_index("pairs").astype(jnp.int32)
    group = lax.axis_index("win").astype(jnp.int32)
    core = group & 1
    blocks = bins // LANES
    half = blocks // 2
    assert windows == 2 and blocks == 2 * half + 1 and half == 12 and groups % 2 == 0

    keep_big, keep_small, give_big, give_small = whiten(core[None], spectra)
    table_big, table_small = lag_table(core, half, blocks)

    slots = sources * cap
    exchange = []
    if sources & (sources - 1) == 0 and 4 <= sources <= 16:
        far = sources // 2
        got_big = swap(give_big, "win", 1)
        big = [keep_big, got_big, swap(keep_big, "pairs", far), swap_both(give_big, far, 1)]
        wanted = after(requests[0], keep_big)
        asked = [wanted] + [swap(wanted, "pairs", d) for d in range(1, far)]
        keep_small = after(keep_small, table_small)
        give_small = after(give_small, table_small)
        got_small = swap(give_small, "win", 1)
        small = [keep_small, got_small, swap(keep_small, "pairs", far), swap_both(give_small, far, 1)]
        for i, chunks in enumerate((big, small)):
            outs = select(me[None], asked, chunks, cap, i == 1)
            exchange.append([outs[0]] + [swap(outs[d], "pairs", d) for d in range(1, far)])

        def row_of(slot):
            apart = (slot // cap) ^ me
            return (apart % far) * (2 * cap) + (apart // far) * cap + slot % cap

    else:
        asked_rows = lax.all_to_all(requests[0], "pairs", split_axis=0, concat_axis=0, tiled=True)
        for i, (keep, give) in enumerate(((keep_big, give_big), (keep_small, give_small))):
            chunk = join(keep, swap(give, "win", 1), i == 1)
            outgoing = chunk[jnp.maximum(asked_rows, 0)]
            arrived = lax.all_to_all(outgoing, "pairs", split_axis=0, concat_axis=0, tiled=True)
            exchange.append([arrived.reshape((slots,) + chunk.shape[1:])])

        def row_of(slot):
            return slot

    first = row_of(pair_first)
    second = row_of(pair_second)
    acc = stack_big(first, second, exchange[0], table_big, LAGS // groups)

    outer = groups // 2
    place = (group >> 1)[None]
    parts = 2
    pieces = []
    for part in range(parts):
        send, keep = stack_small(
            core[None], first, second, exchange[1], table_small, acc, groups, part, parts
        )
        near = swap(send, "win", 1)
        away = sum_away(place, keep, near)
        pieces.append([keep, near] + [swap(x, "win", 2 * (d + 1)) for d, x in enumerate(away)])
    return result(place, pieces, 1.0 / math.sqrt(bins * windows * groups))


def solution(mesh):
    return jax.shard_map(
        local,
        mesh=mesh,
        in_specs=(P("pairs", "win", None, None), P("pairs", None, None), P("pairs"), P("pairs")),
        out_specs=P("win", "pairs"),
        check_vma=False,
    )
```

```python
import functools
import math

import jax
import jax.numpy as jnp
from jax import lax
from jax.experimental import pallas as pl
from jax.experimental.pallas import tpu as pltpu
from jax.sharding import PartitionSpec as P


LAGS = 2048
NFFT = 18000
K0 = 360
LANES = 128
EPS = 1e-06
FINE = 32
VMEM = pl.BlockSpec(memory_space=pltpu.VMEM)
SMEM = pl.BlockSpec(memory_space=pltpu.SMEM)


def params(*nbytes, roomy=False):
    limit = 60 if roomy else sum(nbytes) // 1024**2 + 5
    return pltpu.CompilerParams(vmem_limit_bytes=limit * 1024**2)


def size(shape, dtype):
    return math.prod(shape) * jnp.dtype(dtype).itemsize


def whiten_kernel(core_ref, raw_ref, keep_big, keep_small, give_big, give_small, tmp):
    stations, windows, _, bins = raw_ref.shape
    blocks = bins // LANES
    half = blocks // 2
    core = core_ref[0]

    def white(re, im):
        power = jnp.sum(re * re + im * im, axis=1, keepdims=True) * (1.0 / (2 * LANES))
        scale = lax.rsqrt(power + EPS)
        return re * scale, im * scale

    def station(s, slot):
        for w in range(windows):
            for b in range(blocks):
                value = raw_ref[s, w, :, b * LANES : (b + 1) * LANES]
                side, at = divmod(b, half)
                if side == 2:
                    row = 96 + w
                elif at < 8:
                    row = side * 48 + w * 16 + at
                else:
                    row = side * 48 + 32 + w * 4 + at - 8
                tmp[slot, pl.ds(row, 2, stride=8), :] = value
        for mine, big, small in ((True, keep_big, keep_small), (False, give_big, give_small)):
            base = pl.multiple_of((core if mine else 1 - core) * 48, 16)
            for g in range(3):
                re = tmp[slot, pl.ds(base + g * 16, 8), :]
                im = tmp[slot, pl.ds(base + g * 16 + 8, 8), :]
                rows = jnp.concatenate(white(re, im), axis=0).astype(jnp.bfloat16)
                if g < 2:
                    big[s, g * 16 : g * 16 + 16, :] = rows
                else:
                    small[s, 0:16, :] = rows
        re, im = white(tmp[slot, 96:104, :], tmp[slot, 104:112, :])
        tmp[slot, 112:114, :] = re[0:windows]
        tmp[slot, 114:116, :] = im[0:windows]
        keep_small[s, 16:24, :] = tmp[slot, 112:120, :].astype(jnp.bfloat16)

    tmp[...] = jnp.zeros_like(tmp)

    def several(i, carry):
        for slot in range(2):
            station(2 * i + slot, slot)
        return carry

    lax.fori_loop(0, stations // 2, several, 0)


def whiten(core, raw):
    stations = raw.shape[0]
    rows = (32, 24, 32, 16)
    return pl.pallas_call(
        whiten_kernel,
        name="whiten",
        out_shape=tuple(jax.ShapeDtypeStruct((stations, r, LANES), jnp.bfloat16) for r in rows),
        in_specs=[SMEM, VMEM],
        out_specs=(VMEM,) * 4,
        scratch_shapes=[pltpu.VMEM((2, 120, LANES), jnp.float32)],
        compiler_params=params(2 * size(raw.shape, raw.dtype)),
        cost_estimate=pl.CostEstimate(flops=2_000_000, bytes_accessed=2_000_000, transcendentals=0),
    )(core, raw)


def join(keep, got, small):
    if small:
        return jnp.concatenate([keep[:, :16], got, keep[:, 16:]], axis=1)
    return jnp.concatenate([keep, got], axis=1)


def select_kernel(peers, sources, cap, small, me_ref, *refs):
    asked = refs[:peers]
    chunks = refs[peers : peers + 4]
    outs = refs[peers + 4 :]
    me = me_ref[0]
    for d in range(peers):
        for h in range(2):
            source = me ^ (h * (sources // 2))
            keep, got = chunks[2 * h : 2 * h + 2]
            for c in range(cap):
                row = jnp.maximum(asked[d][source, c], 0)
                out = outs[d].at[h * cap + c]
                if small:
                    out[0:16] = keep[row, 0:16]
                    out[16:32] = got[row]
                    out[32:40] = keep[row, 16:24]
                else:
                    out[0:32] = keep[row]
                    out[32:64] = got[row]


def select(me, asked, chunks, cap, small):
    peers = len(asked)
    sources = asked[0].shape[0]
    rows = chunks[0].shape[1] + chunks[1].shape[1]
    out = jax.ShapeDtypeStruct((2 * cap, rows, LANES), chunks[0].dtype)
    return pl.pallas_call(
        functools.partial(select_kernel, peers, sources, cap, small),
        name="select",
        out_shape=(out,) * peers,
        in_specs=[SMEM] * (1 + peers) + [VMEM] * 4,
        out_specs=(VMEM,) * peers,
        compiler_params=params(2 * (peers + 2) * size(out.shape, out.dtype)),
        cost_estimate=pl.CostEstimate(flops=0, bytes_accessed=1_000_000, transcendentals=0),
    )(me, *asked, *chunks)


def load_table(bufs, table):
    at = 0
    for buf in bufs:

        def copy(i, carry, buf=buf, at=at):
            table[at + i] = buf[i].astype(jnp.float32)
            return carry

        lax.fori_loop(0, buf.shape[0], copy, 0, unroll=4)
        at += buf.shape[0]


def products(table, i, j, groups):
    re = im = None
    for g in range(groups):
        ar = table[i, g * 16 : g * 16 + 8, :]
        ai = table[i, g * 16 + 8 : g * 16 + 16, :]
        br = table[j, g * 16 : g * 16 + 8, :]
        bi = table[j, g * 16 + 8 : g * 16 + 16, :]
        r = ar * br + ai * bi
        m = ai * br - ar * bi
        re = r if re is None else re + r
        im = m if im is None else im + m
    return re, im


BIG_ROWS = 17
SMALL_ROWS = 25


def cross_big(first_ref, second_ref, bufs, table, cross, out):
    pairs = out.shape[0]
    load_table(bufs, table)

    def pair(p, carry):
        re, im = products(table, first_ref[p], second_ref[p], 4)
        cross[pl.ds(p * BIG_ROWS, 8), :] = re
        cross[pl.ds(p * BIG_ROWS + 8, 8), :] = im
        return carry

    lax.fori_loop(0, pairs, pair, 0, unroll=8)
    for k in range(16):
        out[:, k * LANES : (k + 1) * LANES] = cross[pl.ds(k, pairs, stride=BIG_ROWS), :].astype(
            jnp.bfloat16
        )


def cross_small(first_ref, second_ref, bufs, table, cross, out):
    pairs = out.shape[0]
    load_table(bufs, table)

    def pair(p, carry):
        i = first_ref[p]
        j = second_ref[p]
        re, im = products(table, i, j, 2)
        at = p * SMALL_ROWS
        cross[pl.ds(at, 8), :] = re
        cross[pl.ds(at + 8, 8), :] = im
        a = table[i, 32:40, :]
        b = table[j, 32:40, :]
        cross[pl.ds(at + 16, 2), :] = a[0:2] * b[0:2] + a[2:4] * b[2:4]
        cross[pl.ds(at + 18, 2), :] = a[2:4] * b[0:2] - a[0:2] * b[2:4]
        return carry

    lax.fori_loop(0, pairs, pair, 0, unroll=8)

    def column(row):
        return cross[pl.ds(row, pairs, stride=SMALL_ROWS), :]

    for k in range(8):
        row = (k // 4) * 8 + k % 4
        out[:, k * LANES : (k + 1) * LANES] = (column(row) + column(row + 4)).astype(jnp.bfloat16)
    for k in range(2):
        row = 16 + 2 * k
        out[:, (8 + k) * LANES : (9 + k) * LANES] = (column(row) + column(row + 1)).astype(
            jnp.bfloat16
        )


def table_kernel(coarse_ref, fine_ref, big_ref, small_ref):
    half = fine_ref.shape[2] // LANES - 1
    for g in range(half + 1):
        at = slice(g * LANES, (g + 1) * LANES)
        cf = fine_ref[0, :, at]
        sf = fine_ref[1, :, at]
        if g < 8:
            ref, re, im = big_ref, g, g + 8
        elif g < half:
            ref, re, im = small_ref, g - 8, g - 8 + half - 8
        else:
            ref, re, im = small_ref, 2 * (half - 8), 2 * (half - 8) + 1
        for u in range(coarse_ref.shape[1]):
            cc = coarse_ref[0, u : u + 1, at]
            sc = coarse_ref[1, u : u + 1, at]
            rows = slice(u * FINE, (u + 1) * FINE)
            ref[rows, re * LANES : (re + 1) * LANES] = (cc * cf - sc * sf).astype(jnp.bfloat16)
            ref[rows, im * LANES : (im + 1) * LANES] = (sc * cf + cc * sf).astype(jnp.bfloat16)


def lag_bases(core, half, blocks):
    block_index = jnp.concatenate(
        [core * half + jnp.arange(half, dtype=jnp.int32), jnp.full((1,), blocks - 1, jnp.int32)]
    )
    bins = (K0 + block_index[:, None] * LANES + jnp.arange(LANES, dtype=jnp.int32)).reshape(-1)

    def base(lags):
        angles = (lags[:, None] * bins[None, :] % NFFT).astype(jnp.float32) * (2.0 * math.pi / NFFT)
        return jnp.stack([jnp.cos(angles), -jnp.sin(angles)])

    coarse = base(jnp.arange(LAGS // FINE, dtype=jnp.int32) * FINE - LAGS // 2)
    fine = base(jnp.arange(FINE, dtype=jnp.int32))
    return coarse, fine


def lag_table(coarse, fine):
    width = fine.shape[2]
    half = width // LANES - 1
    step = 8
    return pl.pallas_call(
        table_kernel,
        name="lagtable",
        grid=(LAGS // FINE // step,),
        out_shape=(
            jax.ShapeDtypeStruct((LAGS, 16 * LANES), jnp.bfloat16),
            jax.ShapeDtypeStruct((LAGS, 2 * (half + 1 - 8) * LANES), jnp.bfloat16),
        ),
        in_specs=[
            pl.BlockSpec((2, step, width), lambda u: (0, u, 0)),
            pl.BlockSpec((2, FINE, width), lambda u: (0, 0, 0)),
        ],
        out_specs=(
            pl.BlockSpec((step * FINE, 16 * LANES), lambda u: (u, 0)),
            pl.BlockSpec((step * FINE, 2 * (half + 1 - 8) * LANES), lambda u: (u, 0)),
        ),
        compiler_params=params(),
        cost_estimate=pl.CostEstimate(
            flops=LAGS * width * 6, bytes_accessed=LAGS * width * 4, transcendentals=0
        ),
    )(coarse, fine)


def dot_nt(a, b):
    return lax.dot_general(a, b, (((1,), (1,)), ((), ())), preferred_element_type=jnp.float32)


def stack_big_kernel(count, tile, first_ref, second_ref, *refs):
    bufs = refs[:count]
    lag_ref, acc_ref, table, rows, cross = refs[count:]
    cross_big(first_ref, second_ref, bufs, table, rows, cross)
    for t in range(acc_ref.shape[0] // tile):
        at = slice(t * tile, (t + 1) * tile)
        acc_ref[at, :] = dot_nt(lag_ref[at, :], cross[...])


def stack_big(first, second, bufs, lag_table, tile):
    lags, depth = lag_table.shape
    pairs = first.shape[0]
    slots = sum(buf.shape[0] for buf in bufs)
    table = ((slots,) + bufs[0].shape[1:], jnp.float32)
    rows = ((pairs * BIG_ROWS, LANES), jnp.float32)
    cross = ((pairs, depth), jnp.bfloat16)
    return pl.pallas_call(
        functools.partial(stack_big_kernel, len(bufs), tile),
        name="stack0",
        out_shape=jax.ShapeDtypeStruct((lags, pairs), jnp.float32),
        in_specs=[SMEM, SMEM] + [VMEM] * (len(bufs) + 1),
        out_specs=VMEM,
        scratch_shapes=[pltpu.VMEM(*table), pltpu.VMEM(*rows), pltpu.VMEM(*cross)],
        compiler_params=params(size(*table), size(*rows), size(*cross), roomy=len(bufs) == 1),
        cost_estimate=pl.CostEstimate(
            flops=2 * lags * depth * pairs,
            bytes_accessed=2 * lags * depth + 4 * lags * pairs,
            transcendentals=0,
        ),
    )(first, second, *bufs, lag_table)


def finish(part, core, lag_ref, acc_ref, cross, send_ref, keep_ref):
    outer, tile, _ = send_ref.shape
    group_rows = lag_ref.shape[0] // (2 * outer)
    for mine in range(2):
        for at in range(outer):
            group = 2 * at + (core if mine else 1 - core)
            rows = pl.ds(pl.multiple_of(group * group_rows + part * tile, tile), tile)
            value = acc_ref[rows, :] + dot_nt(lag_ref[rows, :], cross[...])
            if mine:
                keep_ref[at] = value
            else:
                send_ref[at] = value.astype(send_ref.dtype)


def stack_first_kernel(count, core_ref, first_ref, second_ref, *refs):
    bufs = refs[:count]
    lag_ref, acc_ref, send_ref, keep_ref, cross, table, rows = refs[count:]
    cross_small(first_ref, second_ref, bufs, table, rows, cross)
    finish(0, core_ref[0], lag_ref, acc_ref, cross, send_ref, keep_ref)


def stack_next_kernel(part, core_ref, lag_ref, acc_ref, cross, send_ref, keep_ref):
    finish(part, core_ref[0], lag_ref, acc_ref, cross, send_ref, keep_ref)


def stack_outputs(acc, groups, parts):
    lags, pairs = acc.shape
    shape = (groups // 2, lags // groups // parts, pairs)
    return [jax.ShapeDtypeStruct(shape, jnp.bfloat16), jax.ShapeDtypeStruct(shape, jnp.float32)]


def stack_cost(lags, depth, pairs, parts):
    return pl.CostEstimate(
        flops=2 * lags * depth * pairs // parts,
        bytes_accessed=(2 * lags * depth + 8 * lags * pairs) // parts,
        transcendentals=0,
    )


def stack_first(core, first, second, bufs, lag_table, acc, groups, parts):
    lags, depth = lag_table.shape
    pairs = acc.shape[1]
    slots = sum(buf.shape[0] for buf in bufs)
    table = ((slots,) + bufs[0].shape[1:], jnp.float32)
    rows = ((pairs * SMALL_ROWS, LANES), jnp.float32)
    return pl.pallas_call(
        functools.partial(stack_first_kernel, len(bufs)),
        name="stack1",
        in_specs=[SMEM] * 3 + [VMEM] * (len(bufs) + 2),
        out_specs=[VMEM] * 3,
        scratch_shapes=[pltpu.VMEM(*table), pltpu.VMEM(*rows)],
        out_shape=stack_outputs(acc, groups, parts)
        + [jax.ShapeDtypeStruct((pairs, depth), jnp.bfloat16)],
        compiler_params=params(size(*table), size(*rows), roomy=len(bufs) == 1),
        cost_estimate=stack_cost(lags, depth, pairs, parts),
    )(core, first, second, *bufs, lag_table, acc)


def stack_next(core, lag_table, acc, cross, groups, part, parts):
    lags, depth = lag_table.shape
    return pl.pallas_call(
        functools.partial(stack_next_kernel, part),
        name="stack2",
        in_specs=[SMEM] + [VMEM] * 3,
        out_specs=[VMEM] * 2,
        out_shape=stack_outputs(acc, groups, parts),
        compiler_params=params(),
        cost_estimate=stack_cost(lags, depth, acc.shape[1], parts),
    )(core, lag_table, acc, cross)


def away_kernel(place_ref, keep_ref, near_ref, *outs):
    for d, out in enumerate(outs):
        at = place_ref[0] ^ (d + 1)
        out[...] = (keep_ref[at] + near_ref[at].astype(jnp.float32)).astype(out.dtype)


def sum_away(place, keep, near):
    outer, lags, pairs = keep.shape
    return pl.pallas_call(
        away_kernel,
        name="away",
        out_shape=[jax.ShapeDtypeStruct((lags, pairs), near.dtype)] * (outer - 1),
        in_specs=[SMEM, VMEM, VMEM],
        out_specs=[VMEM] * (outer - 1),
        compiler_params=params(2 * size(keep.shape, jnp.float32)),
        cost_estimate=pl.CostEstimate(
            flops=keep.size, bytes_accessed=6 * keep.size, transcendentals=0
        ),
    )(place, keep, near)


def result_kernel(scale, parts, place_ref, *refs):
    out = refs[-1]
    each = (len(refs) - 1) // parts
    place = place_ref[0]
    for part in range(parts):
        keep, near, *far = refs[part * each : (part + 1) * each]
        total = keep[place] + near[place].astype(jnp.float32)
        for ref in far:
            total = total + ref[...].astype(jnp.float32)
        lags = total.shape[0]
        out[part * lags : (part + 1) * lags, :] = scale * total


def result(place, pieces, scale):
    operands = [x for piece in pieces for x in piece]
    _, lags, pairs = pieces[0][0].shape
    return pl.pallas_call(
        functools.partial(result_kernel, scale, len(pieces)),
        name="result",
        out_shape=jax.ShapeDtypeStruct((lags * len(pieces), pairs), jnp.float32),
        in_specs=[SMEM] + [VMEM] * len(operands),
        out_specs=VMEM,
        compiler_params=params(2 * size((lags * len(pieces), pairs), jnp.float32)),
        cost_estimate=pl.CostEstimate(
            flops=lags * pairs * 4, bytes_accessed=lags * pairs * 16, transcendentals=0
        ),
    )(place, *operands)


def swap(x, axis, mask):
    return lax.ppermute(x, axis, [(i, i ^ mask) for i in range(lax.axis_size(axis))])


def swap_both(x, mask_pairs, mask_win):
    groups = lax.axis_size("win")
    perm = [
        (p * groups + w, (p ^ mask_pairs) * groups + (w ^ mask_win))
        for p in range(lax.axis_size("pairs"))
        for w in range(groups)
    ]
    return lax.ppermute(x, ("pairs", "win"), perm)


def after(x, *earlier):
    return lax.optimization_barrier((x,) + earlier)[0]


def local(spectra, requests, pair_first, pair_second):
    _, windows, _, bins = spectra.shape
    sources = lax.axis_size("pairs")
    groups = lax.axis_size("win")
    cap = requests.shape[2]
    me = lax.axis_index("pairs").astype(jnp.int32)
    group = lax.axis_index("win").astype(jnp.int32)
    core = group & 1
    blocks = bins // LANES
    half = blocks // 2
    assert windows == 2 and blocks == 2 * half + 1 and half == 12 and groups % 2 == 0

    keep_big, keep_small, give_big, give_small = whiten(core[None], spectra)
    coarse, fine = lag_bases(core, half, blocks)
    table_big, table_small = lag_table(coarse, fine)

    slots = sources * cap
    exchange = []
    if two_stage(sources):
        far = sources // 2
        big = [
            keep_big,
            swap(give_big, "win", 1),
            swap(keep_big, "pairs", far),
            swap_both(give_big, far, 1),
        ]
        wanted = after(requests[0], keep_big)
        asked = [wanted] + [swap(wanted, "pairs", d) for d in range(1, far)]
        keep_small = after(keep_small, coarse)
        give_small = after(give_small, coarse)
        small = [
            keep_small,
            swap(give_small, "win", 1),
            swap(keep_small, "pairs", far),
            swap_both(give_small, far, 1),
        ]
        for chunks, name in ((big, "big"), (small, "small")):
            outs = select(me[None], asked, chunks, cap, name == "small")
            exchange.append([outs[0]] + [swap(outs[d], "pairs", d) for d in range(1, far)])

        def row_of(slot):
            apart = (slot // cap) ^ me
            return (apart % far) * (2 * cap) + (apart // far) * cap + slot % cap

    else:
        asked_rows = lax.all_to_all(requests[0], "pairs", split_axis=0, concat_axis=0, tiled=True)
        for i, (keep, give) in enumerate(((keep_big, give_big), (keep_small, give_small))):
            chunk = join(keep, swap(give, "win", 1), i == 1)
            outgoing = chunk[jnp.maximum(asked_rows, 0)]
            arrived = lax.all_to_all(outgoing, "pairs", split_axis=0, concat_axis=0, tiled=True)
            exchange.append([arrived.reshape((slots,) + chunk.shape[1:])])

        def row_of(slot):
            return slot

    first = row_of(pair_first)
    second = row_of(pair_second)
    acc = stack_big(first, second, exchange[0], table_big, LAGS // groups)

    place = (group >> 1)[None]
    parts = 2
    pieces = []
    send, keep, cross = stack_first(
        core[None], first, second, exchange[1], table_small, acc, groups, parts
    )
    for part in range(parts):
        if part > 0:
            send, keep = stack_next(core[None], table_small, acc, cross, groups, part, parts)
        near = swap(send, "win", 1)
        away = sum_away(place, keep, near)
        pieces.append([keep, near] + [swap(x, "win", 2 * (d + 1)) for d, x in enumerate(away)])
    return result(place, pieces, 1.0 / math.sqrt(bins * windows * groups))


def two_stage(sources):
    return sources & (sources - 1) == 0 and 4 <= sources <= 16


def solution(mesh):
    return jax.shard_map(
        local,
        mesh=mesh,
        in_specs=(P("pairs", "win", None, None), P("pairs", None, None), P("pairs"), P("pairs")),
        out_specs=P("win", "pairs"),
        check_vma=False,
    )
```

```python
import functools
import math

import jax
import jax.numpy as jnp
from jax import lax
from jax.experimental import pallas as pl
from jax.experimental.pallas import tpu as pltpu
from jax.sharding import PartitionSpec as P


LAGS = 2048
NFFT = 18000
K0 = 360
LANES = 128
EPS = 1e-06
FINE = 32
VMEM = pl.BlockSpec(memory_space=pltpu.VMEM)
SMEM = pl.BlockSpec(memory_space=pltpu.SMEM)


def params(*nbytes, roomy=False):
    limit = 60 if roomy else sum(nbytes) // 1024**2 + 5
    return pltpu.CompilerParams(vmem_limit_bytes=limit * 1024**2)


def size(shape, dtype):
    return math.prod(shape) * jnp.dtype(dtype).itemsize


def whiten_kernel(core_ref, hbm_ref, keep_big, keep_small, give_big, give_small, raw_ref, tmp, sems):
    stations, windows, _, bins = raw_ref.shape
    blocks = bins // LANES
    half = blocks // 2
    core = core_ref[0]

    def white(re, im):
        power = jnp.sum(re * re + im * im, axis=1, keepdims=True) * (1.0 / (2 * LANES))
        scale = lax.rsqrt(power + EPS)
        return re * scale, im * scale

    def station(s, slot):
        for w in range(windows):
            for b in range(blocks):
                value = raw_ref[s, w, :, b * LANES : (b + 1) * LANES]
                side, at = divmod(b, half)
                if side == 2:
                    row = 96 + w
                elif at < 8:
                    row = side * 48 + w * 16 + at
                else:
                    row = side * 48 + 32 + w * 4 + at - 8
                tmp[slot, pl.ds(row, 2, stride=8), :] = value
        for mine, big, small in ((True, keep_big, keep_small), (False, give_big, give_small)):
            base = pl.multiple_of((core if mine else 1 - core) * 48, 16)
            for g in range(3):
                re = tmp[slot, pl.ds(base + g * 16, 8), :]
                im = tmp[slot, pl.ds(base + g * 16 + 8, 8), :]
                rows = jnp.concatenate(white(re, im), axis=0).astype(jnp.bfloat16)
                if g < 2:
                    big[s, g * 16 : g * 16 + 16, :] = rows
                else:
                    small[s, 0:16, :] = rows
        re, im = white(tmp[slot, 96:104, :], tmp[slot, 104:112, :])
        tmp[slot, 112:114, :] = re[0:windows]
        tmp[slot, 114:116, :] = im[0:windows]
        keep_small[s, 16:24, :] = tmp[slot, 112:120, :].astype(jnp.bfloat16)

    step = stations // sems.shape[0]
    copies = []
    for k in range(sems.shape[0]):
        rows = pl.ds(k * step, step)
        copies.append(pltpu.make_async_copy(hbm_ref.at[rows], raw_ref.at[rows], sems.at[k]))
        copies[-1].start()
    tmp[...] = jnp.zeros_like(tmp)

    def several(i, carry):
        for slot in range(2):
            station(2 * i + slot, slot)
        return carry

    for k, copy in enumerate(copies):
        copy.wait()
        lax.fori_loop(k * step // 2, (k + 1) * step // 2, several, 0)


def whiten(core, raw):
    stations = raw.shape[0]
    rows = (32, 24, 32, 16)
    return pl.pallas_call(
        whiten_kernel,
        name="whiten",
        out_shape=tuple(jax.ShapeDtypeStruct((stations, r, LANES), jnp.bfloat16) for r in rows),
        in_specs=[SMEM, pl.BlockSpec(memory_space=pltpu.HBM)],
        out_specs=(VMEM,) * 4,
        scratch_shapes=[
            pltpu.VMEM(raw.shape, raw.dtype),
            pltpu.VMEM((2, 120, LANES), jnp.float32),
            pltpu.SemaphoreType.DMA((4,)),
        ],
        compiler_params=params(size(raw.shape, raw.dtype)),
        cost_estimate=pl.CostEstimate(flops=2_000_000, bytes_accessed=2_000_000, transcendentals=0),
    )(core, raw)


def join(keep, got, small):
    if small:
        return jnp.concatenate([keep[:, :16], got, keep[:, 16:]], axis=1)
    return jnp.concatenate([keep, got], axis=1)


def select_kernel(peers, sources, cap, small, me_ref, *refs):
    asked = refs[:peers]
    chunks = refs[peers : peers + 4]
    outs = refs[peers + 4 :]
    me = me_ref[0]
    for d in range(peers):
        for h in range(2):
            source = me ^ (h * (sources // 2))
            keep, got = chunks[2 * h : 2 * h + 2]
            for c in range(cap):
                row = jnp.maximum(asked[d][source, c], 0)
                out = outs[d].at[h * cap + c]
                if small:
                    out[0:16] = keep[row, 0:16]
                    out[16:32] = got[row]
                    out[32:40] = keep[row, 16:24]
                else:
                    out[0:32] = keep[row]
                    out[32:64] = got[row]


def select(me, asked, chunks, cap, small):
    peers = len(asked)
    sources = asked[0].shape[0]
    rows = chunks[0].shape[1] + chunks[1].shape[1]
    out = jax.ShapeDtypeStruct((2 * cap, rows, LANES), chunks[0].dtype)
    return pl.pallas_call(
        functools.partial(select_kernel, peers, sources, cap, small),
        name="select",
        out_shape=(out,) * peers,
        in_specs=[SMEM] * (1 + peers) + [VMEM] * 4,
        out_specs=(VMEM,) * peers,
        compiler_params=params(2 * (peers + 2) * size(out.shape, out.dtype)),
        cost_estimate=pl.CostEstimate(flops=0, bytes_accessed=1_000_000, transcendentals=0),
    )(me, *asked, *chunks)


def load_table(bufs, table):
    at = 0
    for buf in bufs:

        def copy(i, carry, buf=buf, at=at):
            table[at + i] = buf[i].astype(jnp.float32)
            return carry

        lax.fori_loop(0, buf.shape[0], copy, 0, unroll=4)
        at += buf.shape[0]


def products(table, i, j, groups):
    re = im = None
    for g in range(groups):
        ar = table[i, g * 16 : g * 16 + 8, :]
        ai = table[i, g * 16 + 8 : g * 16 + 16, :]
        br = table[j, g * 16 : g * 16 + 8, :]
        bi = table[j, g * 16 + 8 : g * 16 + 16, :]
        r = ar * br + ai * bi
        m = ai * br - ar * bi
        re = r if re is None else re + r
        im = m if im is None else im + m
    return re, im


BIG_ROWS = 17
SMALL_ROWS = 25


def cross_big(first_ref, second_ref, bufs, table, cross, out):
    pairs = out.shape[0]
    load_table(bufs, table)

    def pair(p, carry):
        re, im = products(table, first_ref[p], second_ref[p], 4)
        cross[pl.ds(p * BIG_ROWS, 8), :] = re
        cross[pl.ds(p * BIG_ROWS + 8, 8), :] = im
        return carry

    lax.fori_loop(0, pairs, pair, 0, unroll=8)
    for k in range(16):
        out[:, k * LANES : (k + 1) * LANES] = cross[pl.ds(k, pairs, stride=BIG_ROWS), :].astype(
            jnp.bfloat16
        )


def cross_small(start, first_ref, second_ref, bufs, table, cross, out):
    pairs = out.shape[0]
    load_table(bufs, table)

    def pair(p, carry):
        i = first_ref[start + p]
        j = second_ref[start + p]
        re, im = products(table, i, j, 2)
        at = p * SMALL_ROWS
        cross[pl.ds(at, 8), :] = re
        cross[pl.ds(at + 8, 8), :] = im
        a = table[i, 32:40, :]
        b = table[j, 32:40, :]
        cross[pl.ds(at + 16, 2), :] = a[0:2] * b[0:2] + a[2:4] * b[2:4]
        cross[pl.ds(at + 18, 2), :] = a[2:4] * b[0:2] - a[0:2] * b[2:4]
        return carry

    lax.fori_loop(0, pairs, pair, 0, unroll=8)

    def column(row):
        return cross[pl.ds(row, pairs, stride=SMALL_ROWS), :]

    for k in range(8):
        row = (k // 4) * 8 + k % 4
        out[:, k * LANES : (k + 1) * LANES] = (column(row) + column(row + 4)).astype(jnp.bfloat16)
    for k in range(2):
        row = 16 + 2 * k
        out[:, (8 + k) * LANES : (9 + k) * LANES] = (column(row) + column(row + 1)).astype(
            jnp.bfloat16
        )


def table_kernel(coarse_ref, fine_ref, big_ref, small_ref):
    half = fine_ref.shape[2] // LANES - 1
    for g in range(half + 1):
        at = slice(g * LANES, (g + 1) * LANES)
        cf = fine_ref[0, :, at]
        sf = fine_ref[1, :, at]
        if g < 8:
            ref, re, im = big_ref, g, g + 8
        elif g < half:
            ref, re, im = small_ref, g - 8, g - 8 + half - 8
        else:
            ref, re, im = small_ref, 2 * (half - 8), 2 * (half - 8) + 1
        for u in range(coarse_ref.shape[1]):
            cc = coarse_ref[0, u : u + 1, at]
            sc = coarse_ref[1, u : u + 1, at]
            rows = slice(u * FINE, (u + 1) * FINE)
            ref[rows, re * LANES : (re + 1) * LANES] = (cc * cf - sc * sf).astype(jnp.bfloat16)
            ref[rows, im * LANES : (im + 1) * LANES] = (sc * cf + cc * sf).astype(jnp.bfloat16)


def lag_bases(core, half, blocks):
    block_index = jnp.concatenate(
        [core * half + jnp.arange(half, dtype=jnp.int32), jnp.full((1,), blocks - 1, jnp.int32)]
    )
    bins = (K0 + block_index[:, None] * LANES + jnp.arange(LANES, dtype=jnp.int32)).reshape(-1)

    def base(lags):
        angles = (lags[:, None] * bins[None, :] % NFFT).astype(jnp.float32) * (2.0 * math.pi / NFFT)
        return jnp.stack([jnp.cos(angles), -jnp.sin(angles)])

    coarse = base(jnp.arange(LAGS // FINE, dtype=jnp.int32) * FINE - LAGS // 2)
    fine = base(jnp.arange(FINE, dtype=jnp.int32))
    return coarse, fine


def lag_table(coarse, fine):
    width = fine.shape[2]
    half = width // LANES - 1
    step = 8
    return pl.pallas_call(
        table_kernel,
        name="lagtable",
        grid=(LAGS // FINE // step,),
        out_shape=(
            jax.ShapeDtypeStruct((LAGS, 16 * LANES), jnp.bfloat16),
            jax.ShapeDtypeStruct((LAGS, 2 * (half + 1 - 8) * LANES), jnp.bfloat16),
        ),
        in_specs=[
            pl.BlockSpec((2, step, width), lambda u: (0, u, 0)),
            pl.BlockSpec((2, FINE, width), lambda u: (0, 0, 0)),
        ],
        out_specs=(
            pl.BlockSpec((step * FINE, 16 * LANES), lambda u: (u, 0)),
            pl.BlockSpec((step * FINE, 2 * (half + 1 - 8) * LANES), lambda u: (u, 0)),
        ),
        compiler_params=params(),
        cost_estimate=pl.CostEstimate(
            flops=LAGS * width * 6, bytes_accessed=LAGS * width * 4, transcendentals=0
        ),
    )(coarse, fine)


def dot_nt(a, b):
    return lax.dot_general(a, b, (((1,), (1,)), ((), ())), preferred_element_type=jnp.float32)


def stack_big_kernel(count, tile, first_ref, second_ref, *refs):
    bufs = refs[:count]
    lag_ref, acc_ref, table, rows, cross = refs[count:]
    cross_big(first_ref, second_ref, bufs, table, rows, cross)
    for t in range(acc_ref.shape[0] // tile):
        at = slice(t * tile, (t + 1) * tile)
        acc_ref[at, :] = dot_nt(lag_ref[at, :], cross[...])


def stack_big(first, second, bufs, lag_table, tile):
    lags, depth = lag_table.shape
    pairs = first.shape[0]
    slots = sum(buf.shape[0] for buf in bufs)
    table = ((slots,) + bufs[0].shape[1:], jnp.float32)
    rows = ((pairs * BIG_ROWS, LANES), jnp.float32)
    cross = ((pairs, depth), jnp.bfloat16)
    return pl.pallas_call(
        functools.partial(stack_big_kernel, len(bufs), tile),
        name="stack0",
        out_shape=jax.ShapeDtypeStruct((lags, pairs), jnp.float32),
        in_specs=[SMEM, SMEM] + [VMEM] * (len(bufs) + 1),
        out_specs=VMEM,
        scratch_shapes=[pltpu.VMEM(*table), pltpu.VMEM(*rows), pltpu.VMEM(*cross)],
        compiler_params=params(size(*table), size(*rows), size(*cross), roomy=len(bufs) == 1),
        cost_estimate=pl.CostEstimate(
            flops=2 * lags * depth * pairs,
            bytes_accessed=2 * lags * depth + 4 * lags * pairs,
            transcendentals=0,
        ),
    )(first, second, *bufs, lag_table)


def stack_small_kernel(count, start, core_ref, first_ref, second_ref, *refs):
    bufs = refs[:count]
    lag_ref, acc_ref, send_ref, keep_ref, table, rows, cross = refs[count:]
    cross_small(start, first_ref, second_ref, bufs, table, rows, cross)
    core = core_ref[0]
    outer, tile, pairs = send_ref.shape
    for mine in range(2):
        for at in range(outer):
            group = 2 * at + (core if mine else 1 - core)
            lags = pl.ds(pl.multiple_of(group * tile, tile), tile)
            value = acc_ref[lags, start : start + pairs] + dot_nt(lag_ref[lags, :], cross[...])
            if mine:
                keep_ref[at] = value
            else:
                send_ref[at] = value.astype(send_ref.dtype)


def stack_small(core, first, second, bufs, lag_table, acc, groups, part, parts):
    lags, depth = lag_table.shape
    pairs = acc.shape[1] // parts
    slots = sum(buf.shape[0] for buf in bufs)
    table = ((slots,) + bufs[0].shape[1:], jnp.float32)
    rows = ((pairs * SMALL_ROWS, LANES), jnp.float32)
    cross = ((pairs, depth), jnp.bfloat16)
    shape = (groups // 2, lags // groups, pairs)
    return pl.pallas_call(
        functools.partial(stack_small_kernel, len(bufs), part * pairs),
        name="stack1",
        in_specs=[SMEM] * 3 + [VMEM] * (len(bufs) + 2),
        out_specs=[VMEM] * 2,
        scratch_shapes=[pltpu.VMEM(*table), pltpu.VMEM(*rows), pltpu.VMEM(*cross)],
        out_shape=[
            jax.ShapeDtypeStruct(shape, jnp.bfloat16),
            jax.ShapeDtypeStruct(shape, jnp.float32),
        ],
        compiler_params=params(size(*table), size(*rows), size(*cross), roomy=len(bufs) == 1),
        cost_estimate=pl.CostEstimate(
            flops=2 * lags * depth * pairs,
            bytes_accessed=2 * lags * depth + 8 * lags * pairs,
            transcendentals=0,
        ),
    )(core, first, second, *bufs, lag_table, acc)


def away_kernel(place_ref, keep_ref, near_ref, *outs):
    for d, out in enumerate(outs):
        at = place_ref[0] ^ (d + 1)
        out[...] = (keep_ref[at] + near_ref[at].astype(jnp.float32)).astype(out.dtype)


def sum_away(place, keep, near):
    outer, lags, pairs = keep.shape
    return pl.pallas_call(
        away_kernel,
        name="away",
        out_shape=[jax.ShapeDtypeStruct((lags, pairs), near.dtype)] * (outer - 1),
        in_specs=[SMEM, VMEM, VMEM],
        out_specs=[VMEM] * (outer - 1),
        compiler_params=params(2 * size(keep.shape, jnp.float32)),
        cost_estimate=pl.CostEstimate(
            flops=keep.size, bytes_accessed=6 * keep.size, transcendentals=0
        ),
    )(place, keep, near)


def result_kernel(scale, parts, place_ref, *refs):
    out = refs[-1]
    each = (len(refs) - 1) // parts
    place = place_ref[0]
    for part in range(parts):
        keep, near, *far = refs[part * each : (part + 1) * each]
        total = keep[place] + near[place].astype(jnp.float32)
        for ref in far:
            total = total + ref[...].astype(jnp.float32)
        pairs = total.shape[1]
        out[:, part * pairs : (part + 1) * pairs] = scale * total


def result(place, pieces, scale):
    operands = [x for piece in pieces for x in piece]
    _, lags, pairs = pieces[0][0].shape
    return pl.pallas_call(
        functools.partial(result_kernel, scale, len(pieces)),
        name="result",
        out_shape=jax.ShapeDtypeStruct((lags, pairs * len(pieces)), jnp.float32),
        in_specs=[SMEM] + [VMEM] * len(operands),
        out_specs=VMEM,
        compiler_params=params(2 * size((lags, pairs * len(pieces)), jnp.float32)),
        cost_estimate=pl.CostEstimate(
            flops=lags * pairs * 4, bytes_accessed=lags * pairs * 16, transcendentals=0
        ),
    )(place, *operands)


def swap(x, axis, mask):
    return lax.ppermute(x, axis, [(i, i ^ mask) for i in range(lax.axis_size(axis))])


def swap_both(x, mask_pairs, mask_win):
    groups = lax.axis_size("win")
    perm = [
        (p * groups + w, (p ^ mask_pairs) * groups + (w ^ mask_win))
        for p in range(lax.axis_size("pairs"))
        for w in range(groups)
    ]
    return lax.ppermute(x, ("pairs", "win"), perm)


def after(x, *earlier):
    return lax.optimization_barrier((x,) + earlier)[0]


def local(spectra, requests, pair_first, pair_second):
    stations, windows, _, bins = spectra.shape
    sources = lax.axis_size("pairs")
    groups = lax.axis_size("win")
    cap = requests.shape[2]
    me = lax.axis_index("pairs").astype(jnp.int32)
    group = lax.axis_index("win").astype(jnp.int32)
    core = group & 1
    blocks = bins // LANES
    half = blocks // 2
    assert windows == 2 and blocks == 2 * half + 1 and half == 12 and groups % 2 == 0
    assert stations % 8 == 0

    keep_big, keep_small, give_big, give_small = whiten(core[None], spectra)
    coarse, fine = lag_bases(core, half, blocks)
    table_big, table_small = lag_table(coarse, fine)

    slots = sources * cap
    exchange = []
    if two_stage(sources):
        far = sources // 2
        big = [
            keep_big,
            swap(give_big, "win", 1),
            swap(keep_big, "pairs", far),
            swap_both(give_big, far, 1),
        ]
        wanted = after(requests[0], keep_big)
        asked = [wanted] + [swap(wanted, "pairs", d) for d in range(1, far)]
        keep_small = after(keep_small, big[2], big[3])
        give_small = after(give_small, big[2], big[3])
        small = [
            keep_small,
            swap(give_small, "win", 1),
            swap(keep_small, "pairs", far),
            swap_both(give_small, far, 1),
        ]
        for chunks, name in ((big, "big"), (small, "small")):
            outs = select(me[None], asked, chunks, cap, name == "small")
            exchange.append([outs[0]] + [swap(outs[d], "pairs", d) for d in range(1, far)])

        def row_of(slot):
            apart = (slot // cap) ^ me
            return (apart % far) * (2 * cap) + (apart // far) * cap + slot % cap

    else:
        asked_rows = lax.all_to_all(requests[0], "pairs", split_axis=0, concat_axis=0, tiled=True)
        for i, (keep, give) in enumerate(((keep_big, give_big), (keep_small, give_small))):
            chunk = join(keep, swap(give, "win", 1), i == 1)
            outgoing = chunk[jnp.maximum(asked_rows, 0)]
            arrived = lax.all_to_all(outgoing, "pairs", split_axis=0, concat_axis=0, tiled=True)
            exchange.append([arrived.reshape((slots,) + chunk.shape[1:])])

        def row_of(slot):
            return slot

    first = row_of(pair_first)
    second = row_of(pair_second)
    acc = stack_big(first, second, exchange[0], table_big, LAGS // groups)

    place = (group >> 1)[None]
    parts = 2
    pieces = []
    for part in range(parts):
        send, keep = stack_small(
            core[None], first, second, exchange[1], table_small, acc, groups, part, parts
        )
        near = swap(send, "win", 1)
        away = sum_away(place, keep, near)
        pieces.append([keep, near] + [swap(x, "win", 2 * (d + 1)) for d, x in enumerate(away)])
    return result(place, pieces, 1.0 / math.sqrt(bins * windows * groups))


def two_stage(sources):
    return sources & (sources - 1) == 0 and 4 <= sources <= 16


def solution(mesh):
    return jax.shard_map(
        local,
        mesh=mesh,
        in_specs=(P("pairs", "win", None, None), P("pairs", None, None), P("pairs"), P("pairs")),
        out_specs=P("win", "pairs"),
        check_vma=False,
    )
```

```python
import functools
import math

import jax
import jax.numpy as jnp
from jax import lax
from jax.experimental import pallas as pl
from jax.experimental.pallas import tpu as pltpu
from jax.sharding import PartitionSpec as P


LAGS = 2048
NFFT = 18000
K0 = 360
LANES = 128
EPS = 1e-06
FINE = 32
VMEM = pl.BlockSpec(memory_space=pltpu.VMEM)
SMEM = pl.BlockSpec(memory_space=pltpu.SMEM)


def params(*nbytes, roomy=False):
    limit = 60 if roomy else sum(nbytes) // 1024**2 + 5
    return pltpu.CompilerParams(vmem_limit_bytes=limit * 1024**2)


def size(shape, dtype):
    return math.prod(shape) * jnp.dtype(dtype).itemsize


def whiten_kernel(core_ref, raw_ref, keep_big, keep_small, give_big, give_small, tmp):
    stations, windows, _, bins = raw_ref.shape
    blocks = bins // LANES
    half = blocks // 2
    core = core_ref[0]

    def white(re, im):
        power = jnp.sum(re * re + im * im, axis=1, keepdims=True) * (1.0 / (2 * LANES))
        scale = lax.rsqrt(power + EPS)
        return re * scale, im * scale

    def station(s, slot):
        for w in range(windows):
            for b in range(blocks):
                value = raw_ref[s, w, :, b * LANES : (b + 1) * LANES]
                side, at = divmod(b, half)
                if side == 2:
                    row = 96 + w
                elif at < 8:
                    row = side * 48 + w * 16 + at
                else:
                    row = side * 48 + 32 + w * 4 + at - 8
                tmp[slot, pl.ds(row, 2, stride=8), :] = value
        for mine, big, small in ((True, keep_big, keep_small), (False, give_big, give_small)):
            base = pl.multiple_of((core if mine else 1 - core) * 48, 16)
            for g in range(3):
                re = tmp[slot, pl.ds(base + g * 16, 8), :]
                im = tmp[slot, pl.ds(base + g * 16 + 8, 8), :]
                rows = jnp.concatenate(white(re, im), axis=0).astype(jnp.bfloat16)
                if g < 2:
                    big[s, g * 16 : g * 16 + 16, :] = rows
                else:
                    small[s, 0:16, :] = rows
        re, im = white(tmp[slot, 96:104, :], tmp[slot, 104:112, :])
        tmp[slot, 112:114, :] = re[0:windows]
        tmp[slot, 114:116, :] = im[0:windows]
        keep_small[s, 16:24, :] = tmp[slot, 112:120, :].astype(jnp.bfloat16)

    tmp[...] = jnp.zeros_like(tmp)

    def several(i, carry):
        for slot in range(2):
            station(2 * i + slot, slot)
        return carry

    lax.fori_loop(0, stations // 2, several, 0)


def whiten(core, raw):
    stations = raw.shape[0]
    rows = (32, 24, 32, 16)
    return pl.pallas_call(
        whiten_kernel,
        name="whiten",
        out_shape=tuple(jax.ShapeDtypeStruct((stations, r, LANES), jnp.bfloat16) for r in rows),
        in_specs=[SMEM, VMEM],
        out_specs=(VMEM,) * 4,
        scratch_shapes=[pltpu.VMEM((2, 120, LANES), jnp.float32)],
        compiler_params=params(size(raw.shape, raw.dtype)),
        cost_estimate=pl.CostEstimate(flops=2_000_000, bytes_accessed=2_000_000, transcendentals=0),
    )(core, raw)


def join(keep, got, small):
    if small:
        return jnp.concatenate([keep[:, :16], got, keep[:, 16:]], axis=1)
    return jnp.concatenate([keep, got], axis=1)


def select_kernel(peers, stages, sources, cap, small, me_ref, *refs):
    asked = refs[:peers]
    chunks = refs[peers : peers + 2 * stages]
    outs = refs[peers + 2 * stages :]
    me = me_ref[0]
    for d in range(peers):
        for h in range(stages):
            source = me ^ (h * (sources // 2))
            keep, got = chunks[2 * h : 2 * h + 2]
            for c in range(cap):
                row = jnp.maximum(asked[d][source, c], 0)
                out = outs[d].at[h * cap + c]
                if small:
                    out[0:16] = keep[row, 0:16]
                    out[16:32] = got[row]
                    out[32:40] = keep[row, 16:24]
                else:
                    out[0:32] = keep[row]
                    out[32:64] = got[row]


def select(me, asked, chunks, cap, small):
    peers = len(asked)
    stages = len(chunks) // 2
    sources = asked[0].shape[0]
    rows = chunks[0].shape[1] + chunks[1].shape[1]
    out = jax.ShapeDtypeStruct((stages * cap, rows, LANES), chunks[0].dtype)
    return pl.pallas_call(
        functools.partial(select_kernel, peers, stages, sources, cap, small),
        name="select",
        out_shape=(out,) * peers,
        in_specs=[SMEM] * (1 + peers) + [VMEM] * len(chunks),
        out_specs=(VMEM,) * peers,
        compiler_params=params(2 * (peers + 2) * size(out.shape, out.dtype)),
        cost_estimate=pl.CostEstimate(flops=0, bytes_accessed=1_000_000, transcendentals=0),
    )(me, *asked, *chunks)


def load_table(bufs, table):
    at = 0
    for buf in bufs:

        def copy(i, carry, buf=buf, at=at):
            table[at + i] = buf[i].astype(jnp.float32)
            return carry

        lax.fori_loop(0, buf.shape[0], copy, 0, unroll=4)
        at += buf.shape[0]


def products(table, i, j, groups):
    re = im = None
    for g in range(groups):
        ar = table[i, g * 16 : g * 16 + 8, :]
        ai = table[i, g * 16 + 8 : g * 16 + 16, :]
        br = table[j, g * 16 : g * 16 + 8, :]
        bi = table[j, g * 16 + 8 : g * 16 + 16, :]
        r = ar * br + ai * bi
        m = ai * br - ar * bi
        re = r if re is None else re + r
        im = m if im is None else im + m
    return re, im


BIG_ROWS = 17
SMALL_ROWS = 25


def cross_big(start, first_ref, second_ref, bufs, table, cross, out):
    pairs = out.shape[0]
    load_table(bufs, table)

    def pair(p, carry):
        re, im = products(table, first_ref[start + p], second_ref[start + p], 4)
        cross[pl.ds(p * BIG_ROWS, 8), :] = re
        cross[pl.ds(p * BIG_ROWS + 8, 8), :] = im
        return carry

    lax.fori_loop(0, pairs, pair, 0, unroll=8)
    for k in range(16):
        out[:, k * LANES : (k + 1) * LANES] = cross[pl.ds(k, pairs, stride=BIG_ROWS), :].astype(
            jnp.bfloat16
        )


def cross_small(first_ref, second_ref, bufs, table, cross, out):
    pairs = out.shape[0]
    load_table(bufs, table)

    def pair(p, carry):
        i = first_ref[p]
        j = second_ref[p]
        re, im = products(table, i, j, 2)
        at = p * SMALL_ROWS
        cross[pl.ds(at, 8), :] = re
        cross[pl.ds(at + 8, 8), :] = im
        a = table[i, 32:40, :]
        b = table[j, 32:40, :]
        cross[pl.ds(at + 16, 2), :] = a[0:2] * b[0:2] + a[2:4] * b[2:4]
        cross[pl.ds(at + 18, 2), :] = a[2:4] * b[0:2] - a[0:2] * b[2:4]
        return carry

    lax.fori_loop(0, pairs, pair, 0, unroll=8)

    def column(row):
        return cross[pl.ds(row, pairs, stride=SMALL_ROWS), :]

    for k in range(8):
        row = (k // 4) * 8 + k % 4
        out[:, k * LANES : (k + 1) * LANES] = (column(row) + column(row + 4)).astype(jnp.bfloat16)
    for k in range(2):
        row = 16 + 2 * k
        out[:, (8 + k) * LANES : (9 + k) * LANES] = (column(row) + column(row + 1)).astype(
            jnp.bfloat16
        )


def table_kernel(coarse_ref, fine_ref, big_ref, small_ref):
    half = fine_ref.shape[2] // LANES - 1
    for g in range(half + 1):
        at = slice(g * LANES, (g + 1) * LANES)
        cf = fine_ref[0, :, at]
        sf = fine_ref[1, :, at]
        if g < 8:
            ref, re, im = big_ref, g, g + 8
        elif g < half:
            ref, re, im = small_ref, g - 8, g - 8 + half - 8
        else:
            ref, re, im = small_ref, 2 * (half - 8), 2 * (half - 8) + 1
        for u in range(coarse_ref.shape[1]):
            cc = coarse_ref[0, u : u + 1, at]
            sc = coarse_ref[1, u : u + 1, at]
            rows = slice(u * FINE, (u + 1) * FINE)
            ref[rows, re * LANES : (re + 1) * LANES] = (cc * cf - sc * sf).astype(jnp.bfloat16)
            ref[rows, im * LANES : (im + 1) * LANES] = (sc * cf + cc * sf).astype(jnp.bfloat16)


def lag_bases(core, half, blocks):
    block_index = jnp.concatenate(
        [core * half + jnp.arange(half, dtype=jnp.int32), jnp.full((1,), blocks - 1, jnp.int32)]
    )
    bins = (K0 + block_index[:, None] * LANES + jnp.arange(LANES, dtype=jnp.int32)).reshape(-1)

    def base(lags):
        angles = (lags[:, None] * bins[None, :] % NFFT).astype(jnp.float32) * (2.0 * math.pi / NFFT)
        return jnp.stack([jnp.cos(angles), -jnp.sin(angles)])

    coarse = base(jnp.arange(LAGS // FINE, dtype=jnp.int32) * FINE - LAGS // 2)
    fine = base(jnp.arange(FINE, dtype=jnp.int32))
    return coarse, fine


def lag_table(coarse, fine):
    width = fine.shape[2]
    half = width // LANES - 1
    step = 8
    return pl.pallas_call(
        table_kernel,
        name="lagtable",
        grid=(LAGS // FINE // step,),
        out_shape=(
            jax.ShapeDtypeStruct((LAGS, 16 * LANES), jnp.bfloat16),
            jax.ShapeDtypeStruct((LAGS, 2 * (half + 1 - 8) * LANES), jnp.bfloat16),
        ),
        in_specs=[
            pl.BlockSpec((2, step, width), lambda u: (0, u, 0)),
            pl.BlockSpec((2, FINE, width), lambda u: (0, 0, 0)),
        ],
        out_specs=(
            pl.BlockSpec((step * FINE, 16 * LANES), lambda u: (u, 0)),
            pl.BlockSpec((step * FINE, 2 * (half + 1 - 8) * LANES), lambda u: (u, 0)),
        ),
        compiler_params=params(),
        cost_estimate=pl.CostEstimate(
            flops=LAGS * width * 6, bytes_accessed=LAGS * width * 4, transcendentals=0
        ),
    )(coarse, fine)


def dot_nt(a, b):
    return lax.dot_general(a, b, (((1,), (1,)), ((), ())), preferred_element_type=jnp.float32)


def scratch(bufs, pairs, each, depth):
    slots = sum(buf.shape[0] for buf in bufs)
    shapes = (
        ((slots,) + bufs[0].shape[1:], jnp.float32),
        ((pairs * each, LANES), jnp.float32),
        ((pairs, depth), jnp.bfloat16),
    )
    return dict(
        scratch_shapes=[pltpu.VMEM(*s) for s in shapes],
        compiler_params=params(*(size(*s) for s in shapes), roomy=len(bufs) == 1),
    )


def stack_cost(lags, depth, pairs):
    return pl.CostEstimate(
        flops=2 * lags * depth * pairs,
        bytes_accessed=2 * lags * depth + 4 * lags * pairs,
        transcendentals=0,
    )


def stack_small_kernel(count, tile, first_ref, second_ref, *refs):
    bufs = refs[:count]
    lag_ref, acc_ref, table, rows, cross = refs[count:]
    cross_small(first_ref, second_ref, bufs, table, rows, cross)
    for t in range(acc_ref.shape[0] // tile):
        at = slice(t * tile, (t + 1) * tile)
        acc_ref[at, :] = dot_nt(lag_ref[at, :], cross[...])


def stack_small(first, second, bufs, lag_table, tile):
    lags, depth = lag_table.shape
    pairs = first.shape[0]
    return pl.pallas_call(
        functools.partial(stack_small_kernel, len(bufs), tile),
        name="stack0",
        out_shape=jax.ShapeDtypeStruct((lags, pairs), jnp.float32),
        in_specs=[SMEM, SMEM] + [VMEM] * (len(bufs) + 1),
        out_specs=VMEM,
        cost_estimate=stack_cost(lags, depth, pairs),
        **scratch(bufs, pairs, SMALL_ROWS, depth),
    )(first, second, *bufs, lag_table)


def stack_big_kernel(count, start, core_ref, first_ref, second_ref, *refs):
    bufs = refs[:count]
    lag_ref, acc_ref, send_ref, keep_ref, table, rows, cross = refs[count:]
    cross_big(start, first_ref, second_ref, bufs, table, rows, cross)
    core = core_ref[0]
    outer, tile, pairs = send_ref.shape
    for mine in range(2):
        for at in range(outer):
            group = 2 * at + (core if mine else 1 - core)
            lags = pl.ds(pl.multiple_of(group * tile, tile), tile)
            value = acc_ref[lags, start : start + pairs] + dot_nt(lag_ref[lags, :], cross[...])
            if mine:
                keep_ref[at] = value
            else:
                send_ref[at] = value.astype(send_ref.dtype)


def stack_big(core, first, second, bufs, lag_table, acc, groups, part, parts):
    lags, depth = lag_table.shape
    pairs = acc.shape[1] // parts
    shape = (groups // 2, lags // groups, pairs)
    return pl.pallas_call(
        functools.partial(stack_big_kernel, len(bufs), part * pairs),
        name="stack1",
        in_specs=[SMEM] * 3 + [VMEM] * (len(bufs) + 2),
        out_specs=[VMEM] * 2,
        out_shape=[
            jax.ShapeDtypeStruct(shape, jnp.bfloat16),
            jax.ShapeDtypeStruct(shape, jnp.float32),
        ],
        cost_estimate=stack_cost(lags, depth, pairs),
        **scratch(bufs, pairs, BIG_ROWS, depth),
    )(core, first, second, *bufs, lag_table, acc)


def away_kernel(place_ref, keep_ref, near_ref, *outs):
    for d, out in enumerate(outs):
        at = place_ref[0] ^ (d + 1)
        out[...] = (keep_ref[at] + near_ref[at].astype(jnp.float32)).astype(out.dtype)


def sum_away(place, keep, near):
    outer, lags, pairs = keep.shape
    return pl.pallas_call(
        away_kernel,
        name="away",
        out_shape=[jax.ShapeDtypeStruct((lags, pairs), near.dtype)] * (outer - 1),
        in_specs=[SMEM, VMEM, VMEM],
        out_specs=[VMEM] * (outer - 1),
        compiler_params=params(2 * size(keep.shape, jnp.float32)),
        cost_estimate=pl.CostEstimate(
            flops=keep.size, bytes_accessed=6 * keep.size, transcendentals=0
        ),
    )(place, keep, near)


def result_kernel(scale, parts, place_ref, *refs):
    out = refs[-1]
    each = (len(refs) - 1) // parts
    place = place_ref[0]
    for part in range(parts):
        keep, near, *far = refs[part * each : (part + 1) * each]
        total = keep[place] + near[place].astype(jnp.float32)
        for ref in far:
            total = total + ref[...].astype(jnp.float32)
        pairs = total.shape[1]
        out[:, part * pairs : (part + 1) * pairs] = scale * total


def result(place, pieces, scale):
    operands = [x for piece in pieces for x in piece]
    _, lags, pairs = pieces[0][0].shape
    return pl.pallas_call(
        functools.partial(result_kernel, scale, len(pieces)),
        name="result",
        out_shape=jax.ShapeDtypeStruct((lags, pairs * len(pieces)), jnp.float32),
        in_specs=[SMEM] + [VMEM] * len(operands),
        out_specs=VMEM,
        compiler_params=params(2 * size((lags, pairs * len(pieces)), jnp.float32)),
        cost_estimate=pl.CostEstimate(
            flops=lags * pairs * 4, bytes_accessed=lags * pairs * 16, transcendentals=0
        ),
    )(place, *operands)


def swap(x, axis, mask):
    return lax.ppermute(x, axis, [(i, i ^ mask) for i in range(lax.axis_size(axis))])


def swap_both(x, mask_pairs, mask_win):
    groups = lax.axis_size("win")
    perm = [
        (p * groups + w, (p ^ mask_pairs) * groups + (w ^ mask_win))
        for p in range(lax.axis_size("pairs"))
        for w in range(groups)
    ]
    return lax.ppermute(x, ("pairs", "win"), perm)


def after(x, *earlier):
    return lax.optimization_barrier((x,) + earlier)[0]


def local(spectra, requests, pair_first, pair_second):
    stations, windows, _, bins = spectra.shape
    sources = lax.axis_size("pairs")
    groups = lax.axis_size("win")
    cap = requests.shape[2]
    me = lax.axis_index("pairs").astype(jnp.int32)
    group = lax.axis_index("win").astype(jnp.int32)
    core = group & 1
    blocks = bins // LANES
    half = blocks // 2
    assert windows == 2 and blocks == 2 * half + 1 and half == 12 and groups % 2 == 0
    assert stations % 2 == 0

    keep_big, keep_small, give_big, give_small = whiten(core[None], spectra)
    near_big = swap(give_big, "win", 1)
    near_small = swap(give_small, "win", 1)

    slots = sources * cap
    wanted = requests[0]
    if two_stage(sources):
        far = sources // 2
        asked = [wanted] + [swap(wanted, "pairs", d) for d in range(1, sources)]
        outs = select(me[None], asked, (keep_big, near_big), cap, False)
        big = [outs[0]] + [swap(outs[d], "pairs", d) for d in range(1, sources)]
        chunks = (
            keep_small, near_small, swap(keep_small, "pairs", far), swap_both(give_small, far, 1)
        )
        core_table = after(core, outs[0])
        outs = select(me[None], asked[:far], chunks, cap, True)
        small = [outs[0]] + [swap(outs[d], "pairs", d) for d in range(1, far)]

        def row_of_big(slot):
            return ((slot // cap) ^ me) * cap + slot % cap

        def row_of_small(slot):
            apart = (slot // cap) ^ me
            return (apart % far) * (2 * cap) + (apart // far) * cap + slot % cap

    else:
        asked_rows = lax.all_to_all(wanted, "pairs", split_axis=0, concat_axis=0, tiled=True)

        def exchange(chunk):
            outgoing = chunk[jnp.maximum(asked_rows, 0)]
            arrived = lax.all_to_all(outgoing, "pairs", split_axis=0, concat_axis=0, tiled=True)
            return [arrived.reshape((slots,) + chunk.shape[1:])]

        big = exchange(join(keep_big, near_big, False))
        small = exchange(join(keep_small, near_small, True))
        core_table = core

        def row_of_big(slot):
            return slot

        row_of_small = row_of_big

    coarse, fine = lag_bases(core_table, half, blocks)
    table_big, table_small = lag_table(coarse, fine)
    acc = stack_small(
        row_of_small(pair_first), row_of_small(pair_second), small, table_small, LAGS // groups
    )

    place = (group >> 1)[None]
    parts = 2
    first = row_of_big(pair_first)
    second = row_of_big(pair_second)
    pieces = []
    for part in range(parts):
        send, keep = stack_big(core[None], first, second, big, table_big, acc, groups, part, parts)
        near = swap(send, "win", 1)
        away = sum_away(place, keep, near)
        pieces.append([keep, near] + [swap(x, "win", 2 * (d + 1)) for d, x in enumerate(away)])
    return result(place, pieces, 1.0 / math.sqrt(bins * windows * groups))


def two_stage(sources):
    return sources & (sources - 1) == 0 and 4 <= sources <= 16


def solution(mesh):
    step = jax.shard_map(
        local,
        mesh=mesh,
        in_specs=(P("pairs", "win", None, None), P("pairs", None, None), P("pairs"), P("pairs")),
        out_specs=P("win", "pairs"),
        check_vma=False,
    )
    sources = mesh.shape["pairs"]
    if not two_stage(sources):
        return step
    return step
```

```python
import functools
import math

import jax
import jax.numpy as jnp
from jax import lax
from jax.experimental import pallas as pl
from jax.experimental.pallas import tpu as pltpu
from jax.sharding import PartitionSpec as P


LAGS = 2048
NFFT = 18000
K0 = 360
LANES = 128
EPS = 1e-06
FINE = 32
VMEM = pl.BlockSpec(memory_space=pltpu.VMEM)
SMEM = pl.BlockSpec(memory_space=pltpu.SMEM)


def params(*nbytes, roomy=False):
    limit = 60 if roomy else sum(nbytes) // 1024**2 + 5
    return pltpu.CompilerParams(vmem_limit_bytes=limit * 1024**2)


def size(shape, dtype):
    return math.prod(shape) * jnp.dtype(dtype).itemsize


def whiten_kernel(core_ref, raw_ref, keep_big, keep_small, give_big, give_small, tmp):
    stations, windows, _, bins = raw_ref.shape
    blocks = bins // LANES
    half = blocks // 2
    core = core_ref[0]

    def white(re, im):
        power = jnp.sum(re * re + im * im, axis=1, keepdims=True) * (1.0 / (2 * LANES))
        scale = lax.rsqrt(power + EPS)
        return re * scale, im * scale

    def station(s, slot):
        for w in range(windows):
            for b in range(blocks):
                value = raw_ref[s, w, :, b * LANES : (b + 1) * LANES]
                side, at = divmod(b, half)
                if side == 2:
                    row = 96 + w
                elif at < 8:
                    row = side * 48 + w * 16 + at
                else:
                    row = side * 48 + 32 + w * 4 + at - 8
                tmp[slot, pl.ds(row, 2, stride=8), :] = value
        for mine, big, small in ((True, keep_big, keep_small), (False, give_big, give_small)):
            base = pl.multiple_of((core if mine else 1 - core) * 48, 16)
            for g in range(3):
                re = tmp[slot, pl.ds(base + g * 16, 8), :]
                im = tmp[slot, pl.ds(base + g * 16 + 8, 8), :]
                rows = jnp.concatenate(white(re, im), axis=0).astype(jnp.bfloat16)
                if g < 2:
                    big[s, g * 16 : g * 16 + 16, :] = rows
                else:
                    small[s, 0:16, :] = rows
        re, im = white(tmp[slot, 96:104, :], tmp[slot, 104:112, :])
        tmp[slot, 112:114, :] = re[0:windows]
        tmp[slot, 114:116, :] = im[0:windows]
        keep_small[s, 16:24, :] = tmp[slot, 112:120, :].astype(jnp.bfloat16)

    tmp[...] = jnp.zeros_like(tmp)

    def several(i, carry):
        for slot in range(2):
            station(2 * i + slot, slot)
        return carry

    lax.fori_loop(0, stations // 2, several, 0)


def whiten(core, raw):
    stations = raw.shape[0]
    rows = (32, 24, 32, 16)
    return pl.pallas_call(
        whiten_kernel,
        name="whiten",
        out_shape=tuple(jax.ShapeDtypeStruct((stations, r, LANES), jnp.bfloat16) for r in rows),
        in_specs=[SMEM, VMEM],
        out_specs=(VMEM,) * 4,
        scratch_shapes=[pltpu.VMEM((2, 120, LANES), jnp.float32)],
        compiler_params=params(size(raw.shape, raw.dtype)),
        cost_estimate=pl.CostEstimate(flops=2_000_000, bytes_accessed=2_000_000, transcendentals=0),
    )(core, raw)


def join(keep, got, small):
    if small:
        return jnp.concatenate([keep[:, :16], got, keep[:, 16:]], axis=1)
    return jnp.concatenate([keep, got], axis=1)


def select_kernel(peers, stages, sources, cap, small, me_ref, *refs):
    asked = refs[:peers]
    chunks = refs[peers : peers + 2 * stages]
    outs = refs[peers + 2 * stages :]
    me = me_ref[0]
    for d in range(peers):
        for h in range(stages):
            source = me ^ (h * (sources // 2))
            keep, got = chunks[2 * h : 2 * h + 2]
            for c in range(cap):
                row = jnp.maximum(asked[d][source, c], 0)
                out = outs[d].at[h * cap + c]
                if small:
                    out[0:16] = keep[row, 0:16]
                    out[16:32] = got[row]
                    out[32:40] = keep[row, 16:24]
                else:
                    out[0:32] = keep[row]
                    out[32:64] = got[row]


def select(me, asked, chunks, cap, small):
    peers = len(asked)
    stages = len(chunks) // 2
    sources = asked[0].shape[0]
    rows = chunks[0].shape[1] + chunks[1].shape[1]
    out = jax.ShapeDtypeStruct((stages * cap, rows, LANES), chunks[0].dtype)
    return pl.pallas_call(
        functools.partial(select_kernel, peers, stages, sources, cap, small),
        name="select",
        out_shape=(out,) * peers,
        in_specs=[SMEM] * (1 + peers) + [VMEM] * len(chunks),
        out_specs=(VMEM,) * peers,
        compiler_params=params(2 * (peers + 2) * size(out.shape, out.dtype)),
        cost_estimate=pl.CostEstimate(flops=0, bytes_accessed=1_000_000, transcendentals=0),
    )(me, *asked, *chunks)


def load_table(bufs, table):
    at = 0
    for buf in bufs:

        def copy(i, carry, buf=buf, at=at):
            table[at + i] = buf[i].astype(jnp.float32)
            return carry

        lax.fori_loop(0, buf.shape[0], copy, 0, unroll=4)
        at += buf.shape[0]


def products(table, i, j, groups):
    re = im = None
    for g in range(groups):
        ar = table[i, g * 16 : g * 16 + 8, :]
        ai = table[i, g * 16 + 8 : g * 16 + 16, :]
        br = table[j, g * 16 : g * 16 + 8, :]
        bi = table[j, g * 16 + 8 : g * 16 + 16, :]
        r = ar * br + ai * bi
        m = ai * br - ar * bi
        re = r if re is None else re + r
        im = m if im is None else im + m
    return re, im


BIG_ROWS = 17
SMALL_ROWS = 25


def cross_big(first_ref, second_ref, bufs, table, cross, out):
    pairs = out.shape[0]
    load_table(bufs, table)

    def pair(p, carry):
        re, im = products(table, first_ref[p], second_ref[p], 4)
        cross[pl.ds(p * BIG_ROWS, 8), :] = re
        cross[pl.ds(p * BIG_ROWS + 8, 8), :] = im
        return carry

    lax.fori_loop(0, pairs, pair, 0, unroll=8)
    for k in range(16):
        out[:, k * LANES : (k + 1) * LANES] = cross[pl.ds(k, pairs, stride=BIG_ROWS), :].astype(
            jnp.bfloat16
        )


def cross_small(first_ref, second_ref, bufs, table, cross, out):
    pairs = out.shape[0]
    load_table(bufs, table)

    def pair(p, carry):
        i = first_ref[p]
        j = second_ref[p]
        re, im = products(table, i, j, 2)
        at = p * SMALL_ROWS
        cross[pl.ds(at, 8), :] = re
        cross[pl.ds(at + 8, 8), :] = im
        a = table[i, 32:40, :]
        b = table[j, 32:40, :]
        cross[pl.ds(at + 16, 2), :] = a[0:2] * b[0:2] + a[2:4] * b[2:4]
        cross[pl.ds(at + 18, 2), :] = a[2:4] * b[0:2] - a[0:2] * b[2:4]
        return carry

    lax.fori_loop(0, pairs, pair, 0, unroll=8)

    def column(row):
        return cross[pl.ds(row, pairs, stride=SMALL_ROWS), :]

    for k in range(8):
        row = (k // 4) * 8 + k % 4
        out[:, k * LANES : (k + 1) * LANES] = (column(row) + column(row + 4)).astype(jnp.bfloat16)
    for k in range(2):
        row = 16 + 2 * k
        out[:, (8 + k) * LANES : (9 + k) * LANES] = (column(row) + column(row + 1)).astype(
            jnp.bfloat16
        )


def table_kernel(coarse_ref, fine_ref, big_ref, small_ref):
    half = fine_ref.shape[2] // LANES - 1
    for g in range(half + 1):
        at = slice(g * LANES, (g + 1) * LANES)
        cf = fine_ref[0, :, at]
        sf = fine_ref[1, :, at]
        if g < 8:
            ref, re, im = big_ref, g, g + 8
        elif g < half:
            ref, re, im = small_ref, g - 8, g - 8 + half - 8
        else:
            ref, re, im = small_ref, 2 * (half - 8), 2 * (half - 8) + 1
        for u in range(coarse_ref.shape[1]):
            cc = coarse_ref[0, u : u + 1, at]
            sc = coarse_ref[1, u : u + 1, at]
            rows = slice(u * FINE, (u + 1) * FINE)
            ref[rows, re * LANES : (re + 1) * LANES] = (cc * cf - sc * sf).astype(jnp.bfloat16)
            ref[rows, im * LANES : (im + 1) * LANES] = (sc * cf + cc * sf).astype(jnp.bfloat16)


def lag_bases(core, half, blocks):
    block_index = jnp.concatenate(
        [core * half + jnp.arange(half, dtype=jnp.int32), jnp.full((1,), blocks - 1, jnp.int32)]
    )
    bins = (K0 + block_index[:, None] * LANES + jnp.arange(LANES, dtype=jnp.int32)).reshape(-1)

    def base(lags):
        angles = (lags[:, None] * bins[None, :] % NFFT).astype(jnp.float32) * (2.0 * math.pi / NFFT)
        return jnp.stack([jnp.cos(angles), -jnp.sin(angles)])

    coarse = base(jnp.arange(LAGS // FINE, dtype=jnp.int32) * FINE - LAGS // 2)
    fine = base(jnp.arange(FINE, dtype=jnp.int32))
    return coarse, fine


def lag_table(coarse, fine):
    width = fine.shape[2]
    half = width // LANES - 1
    step = 8
    return pl.pallas_call(
        table_kernel,
        name="lagtable",
        grid=(LAGS // FINE // step,),
        out_shape=(
            jax.ShapeDtypeStruct((LAGS, 16 * LANES), jnp.bfloat16),
            jax.ShapeDtypeStruct((LAGS, 2 * (half + 1 - 8) * LANES), jnp.bfloat16),
        ),
        in_specs=[
            pl.BlockSpec((2, step, width), lambda u: (0, u, 0)),
            pl.BlockSpec((2, FINE, width), lambda u: (0, 0, 0)),
        ],
        out_specs=(
            pl.BlockSpec((step * FINE, 16 * LANES), lambda u: (u, 0)),
            pl.BlockSpec((step * FINE, 2 * (half + 1 - 8) * LANES), lambda u: (u, 0)),
        ),
        compiler_params=params(),
        cost_estimate=pl.CostEstimate(
            flops=LAGS * width * 6, bytes_accessed=LAGS * width * 4, transcendentals=0
        ),
    )(coarse, fine)


def dot_nt(a, b):
    return lax.dot_general(a, b, (((1,), (1,)), ((), ())), preferred_element_type=jnp.float32)


def scratch(bufs, pairs, each, *more):
    slots = sum(buf.shape[0] for buf in bufs)
    shapes = (
        ((slots,) + bufs[0].shape[1:], jnp.float32),
        ((pairs * each, LANES), jnp.float32),
    ) + more
    return dict(
        scratch_shapes=[pltpu.VMEM(*s) for s in shapes],
        compiler_params=params(*(size(*s) for s in shapes), roomy=len(bufs) == 1),
    )


def stack_cost(lags, depth, pairs):
    return pl.CostEstimate(
        flops=2 * lags * depth * pairs,
        bytes_accessed=2 * lags * depth + 4 * lags * pairs,
        transcendentals=0,
    )


CHUNKS = {"big": (cross_big, BIG_ROWS), "small": (cross_small, SMALL_ROWS)}


def stack_all_kernel(chunk, count, tile, first_ref, second_ref, *refs):
    bufs = refs[:count]
    lag_ref, acc_ref, table, rows, cross = refs[count:]
    CHUNKS[chunk][0](first_ref, second_ref, bufs, table, rows, cross)
    for t in range(acc_ref.shape[0] // tile):
        at = slice(t * tile, (t + 1) * tile)
        acc_ref[at, :] = dot_nt(lag_ref[at, :], cross[...])


def stack_all(chunk, first, second, bufs, lag_table, tile):
    lags, depth = lag_table.shape
    pairs = first.shape[0]
    return pl.pallas_call(
        functools.partial(stack_all_kernel, chunk, len(bufs), tile),
        name="stack0",
        out_shape=jax.ShapeDtypeStruct((lags, pairs), jnp.float32),
        in_specs=[SMEM, SMEM] + [VMEM] * (len(bufs) + 1),
        out_specs=VMEM,
        cost_estimate=stack_cost(lags, depth, pairs),
        **scratch(bufs, pairs, CHUNKS[chunk][1], ((pairs, depth), jnp.bfloat16)),
    )(first, second, *bufs, lag_table)


def finish(part, core, lag_ref, acc_ref, cross, send_ref, keep_ref):
    outer, tile, _ = send_ref.shape
    group_rows = lag_ref.shape[0] // (2 * outer)
    for mine in range(2):
        for at in range(outer):
            group = 2 * at + (core if mine else 1 - core)
            lags = pl.ds(pl.multiple_of(group * group_rows + part * tile, tile), tile)
            value = acc_ref[lags, :] + dot_nt(lag_ref[lags, :], cross[...])
            if mine:
                keep_ref[at] = value
            else:
                send_ref[at] = value.astype(send_ref.dtype)


def stack_outputs(acc, groups, parts):
    lags, pairs = acc.shape
    shape = (groups // 2, lags // groups // parts, pairs)
    return [jax.ShapeDtypeStruct(shape, jnp.bfloat16), jax.ShapeDtypeStruct(shape, jnp.float32)]


def stack_first_kernel(chunk, count, core_ref, first_ref, second_ref, *refs):
    bufs = refs[:count]
    lag_ref, acc_ref, send_ref, keep_ref, cross, table, rows = refs[count:]
    CHUNKS[chunk][0](first_ref, second_ref, bufs, table, rows, cross)
    finish(0, core_ref[0], lag_ref, acc_ref, cross, send_ref, keep_ref)


def stack_first(chunk, core, first, second, bufs, lag_table, acc, groups, parts):
    lags, depth = lag_table.shape
    pairs = acc.shape[1]
    return pl.pallas_call(
        functools.partial(stack_first_kernel, chunk, len(bufs)),
        name="stack1",
        in_specs=[SMEM] * 3 + [VMEM] * (len(bufs) + 2),
        out_specs=[VMEM] * 3,
        out_shape=stack_outputs(acc, groups, parts)
        + [jax.ShapeDtypeStruct((pairs, depth), jnp.bfloat16)],
        cost_estimate=stack_cost(lags // parts, depth, pairs),
        **scratch(bufs, pairs, CHUNKS[chunk][1]),
    )(core, first, second, *bufs, lag_table, acc)


def stack_next_kernel(part, core_ref, lag_ref, acc_ref, cross, send_ref, keep_ref):
    finish(part, core_ref[0], lag_ref, acc_ref, cross, send_ref, keep_ref)


def stack_next(core, lag_table, acc, cross, groups, part, parts):
    lags, depth = lag_table.shape
    return pl.pallas_call(
        functools.partial(stack_next_kernel, part),
        name="stack2",
        in_specs=[SMEM] + [VMEM] * 3,
        out_specs=[VMEM] * 2,
        out_shape=stack_outputs(acc, groups, parts),
        compiler_params=params(),
        cost_estimate=stack_cost(lags // parts, depth, acc.shape[1]),
    )(core, lag_table, acc, cross)


def away_kernel(place_ref, keep_ref, near_ref, *outs):
    for d, out in enumerate(outs):
        at = place_ref[0] ^ (d + 1)
        out[...] = (keep_ref[at] + near_ref[at].astype(jnp.float32)).astype(out.dtype)


def sum_away(place, keep, near):
    outer, lags, pairs = keep.shape
    return pl.pallas_call(
        away_kernel,
        name="away",
        out_shape=[jax.ShapeDtypeStruct((lags, pairs), near.dtype)] * (outer - 1),
        in_specs=[SMEM, VMEM, VMEM],
        out_specs=[VMEM] * (outer - 1),
        compiler_params=params(2 * size(keep.shape, jnp.float32)),
        cost_estimate=pl.CostEstimate(
            flops=keep.size, bytes_accessed=6 * keep.size, transcendentals=0
        ),
    )(place, keep, near)


def result_kernel(scale, parts, place_ref, *refs):
    out = refs[-1]
    each = (len(refs) - 1) // parts
    place = place_ref[0]
    for part in range(parts):
        keep, near, *far = refs[part * each : (part + 1) * each]
        total = keep[place] + near[place].astype(jnp.float32)
        for ref in far:
            total = total + ref[...].astype(jnp.float32)
        lags = total.shape[0]
        out[part * lags : (part + 1) * lags, :] = scale * total


def result(place, pieces, scale):
    operands = [x for piece in pieces for x in piece]
    _, lags, pairs = pieces[0][0].shape
    return pl.pallas_call(
        functools.partial(result_kernel, scale, len(pieces)),
        name="result",
        out_shape=jax.ShapeDtypeStruct((lags * len(pieces), pairs), jnp.float32),
        in_specs=[SMEM] + [VMEM] * len(operands),
        out_specs=VMEM,
        compiler_params=params(2 * size((lags * len(pieces), pairs), jnp.float32)),
        cost_estimate=pl.CostEstimate(
            flops=lags * pairs * 4, bytes_accessed=lags * pairs * 16, transcendentals=0
        ),
    )(place, *operands)


def swap(x, axis, mask):
    return lax.ppermute(x, axis, [(i, i ^ mask) for i in range(lax.axis_size(axis))])


def swap_both(x, mask_pairs, mask_win):
    groups = lax.axis_size("win")
    perm = [
        (p * groups + w, (p ^ mask_pairs) * groups + (w ^ mask_win))
        for p in range(lax.axis_size("pairs"))
        for w in range(groups)
    ]
    return lax.ppermute(x, ("pairs", "win"), perm)


def local(spectra, requests, pair_first, pair_second):
    stations, windows, _, bins = spectra.shape
    sources = lax.axis_size("pairs")
    groups = lax.axis_size("win")
    cap = requests.shape[2]
    me = lax.axis_index("pairs").astype(jnp.int32)
    group = lax.axis_index("win").astype(jnp.int32)
    core = group & 1
    blocks = bins // LANES
    half = blocks // 2
    assert windows == 2 and blocks == 2 * half + 1 and half == 12 and groups % 2 == 0
    assert stations % 2 == 0

    keep_big, keep_small, give_big, give_small = whiten(core[None], spectra)
    near_big = swap(give_big, "win", 1)
    near_small = swap(give_small, "win", 1)

    slots = sources * cap
    wanted = requests[0]
    if two_stage(sources):
        far = sources // 2
        chunks = {
            "big": [keep_big, near_big, swap(keep_big, "pairs", far), swap_both(give_big, far, 1)],
            "small": [
                keep_small,
                near_small,
                swap(keep_small, "pairs", far),
                swap_both(give_small, far, 1),
            ],
        }
        asked = [wanted] + [swap(wanted, "pairs", d) for d in range(1, far)]
        arrived = {}
        for name, chunk in chunks.items():
            outs = select(me[None], asked, chunk, cap, name == "small")
            arrived[name] = [outs[0]] + [swap(outs[d], "pairs", d) for d in range(1, far)]
        small, big = arrived["small"], arrived["big"]
        core_table = core

        def row_of(slot):
            apart = (slot // cap) ^ me
            return (apart % far) * (2 * cap) + (apart // far) * cap + slot % cap

    else:
        asked_rows = lax.all_to_all(wanted, "pairs", split_axis=0, concat_axis=0, tiled=True)

        def exchange(chunk):
            outgoing = chunk[jnp.maximum(asked_rows, 0)]
            arrived = lax.all_to_all(outgoing, "pairs", split_axis=0, concat_axis=0, tiled=True)
            return [arrived.reshape((slots,) + chunk.shape[1:])]

        big = exchange(join(keep_big, near_big, False))
        small = exchange(join(keep_small, near_small, True))
        core_table = core

        def row_of(slot):
            return slot

    coarse, fine = lag_bases(core_table, half, blocks)
    table_big, table_small = lag_table(coarse, fine)
    first = row_of(pair_first)
    second = row_of(pair_second)
    acc = stack_all("big", first, second, big, table_big, LAGS // groups)

    place = (group >> 1)[None]
    parts = 2
    pieces = []
    send, keep, cross = stack_first(
        "small", core[None], first, second, small, table_small, acc, groups, parts
    )
    for part in range(parts):
        if part > 0:
            send, keep = stack_next(core[None], table_small, acc, cross, groups, part, parts)
        near = swap(send, "win", 1)
        away = sum_away(place, keep, near)
        pieces.append([keep, near] + [swap(x, "win", 2 * (d + 1)) for d, x in enumerate(away)])
    return result(place, pieces, 1.0 / math.sqrt(bins * windows * groups))


def two_stage(sources):
    return sources & (sources - 1) == 0 and 4 <= sources <= 16


def solution(mesh):
    step = jax.shard_map(
        local,
        mesh=mesh,
        in_specs=(P("pairs", "win", None, None), P("pairs", None, None), P("pairs"), P("pairs")),
        out_specs=P("win", "pairs"),
        check_vma=False,
    )
    sources = mesh.shape["pairs"]
    if not two_stage(sources):
        return step
    return step
```

```python
import functools
import math

import jax
import jax.numpy as jnp
from jax import lax
from jax.experimental import pallas as pl
from jax.experimental.pallas import tpu as pltpu
from jax.sharding import PartitionSpec as P


LAGS = 2048
NFFT = 18000
K0 = 360
LANES = 128
EPS = 1e-06
FINE = 32
VMEM = pl.BlockSpec(memory_space=pltpu.VMEM)
SMEM = pl.BlockSpec(memory_space=pltpu.SMEM)


def params(*nbytes, roomy=False):
    limit = 60 if roomy else sum(nbytes) // 1024**2 + 5
    return pltpu.CompilerParams(vmem_limit_bytes=limit * 1024**2)


def size(shape, dtype):
    return math.prod(shape) * jnp.dtype(dtype).itemsize


def whiten_kernel(core_ref, raw_ref, keep_big, keep_small, give_big, give_small, tmp):
    stations, windows, _, bins = raw_ref.shape
    blocks = bins // LANES
    half = blocks // 2
    core = core_ref[0]

    def white(re, im):
        power = jnp.sum(re * re + im * im, axis=1, keepdims=True) * (1.0 / (2 * LANES))
        scale = lax.rsqrt(power + EPS)
        return re * scale, im * scale

    def station(s, slot):
        for w in range(windows):
            for b in range(blocks):
                value = raw_ref[s, w, :, b * LANES : (b + 1) * LANES]
                side, at = divmod(b, half)
                if side == 2:
                    row = 96 + w
                elif at < 8:
                    row = side * 48 + w * 16 + at
                else:
                    row = side * 48 + 32 + w * 4 + at - 8
                tmp[slot, pl.ds(row, 2, stride=8), :] = value
        for mine, big, small in ((True, keep_big, keep_small), (False, give_big, give_small)):
            base = pl.multiple_of((core if mine else 1 - core) * 48, 16)
            for g in range(3):
                re = tmp[slot, pl.ds(base + g * 16, 8), :]
                im = tmp[slot, pl.ds(base + g * 16 + 8, 8), :]
                rows = jnp.concatenate(white(re, im), axis=0).astype(jnp.bfloat16)
                if g < 2:
                    big[s, g * 16 : g * 16 + 16, :] = rows
                else:
                    small[s, 0:16, :] = rows
        re, im = white(tmp[slot, 96:104, :], tmp[slot, 104:112, :])
        tmp[slot, 112:114, :] = re[0:windows]
        tmp[slot, 114:116, :] = im[0:windows]
        keep_small[s, 16:24, :] = tmp[slot, 112:120, :].astype(jnp.bfloat16)

    tmp[...] = jnp.zeros_like(tmp)

    def several(i, carry):
        for slot in range(2):
            station(2 * i + slot, slot)
        return carry

    lax.fori_loop(0, stations // 2, several, 0)


def whiten(core, raw):
    stations = raw.shape[0]
    rows = (32, 24, 32, 16)
    return pl.pallas_call(
        whiten_kernel,
        name="whiten",
        out_shape=tuple(jax.ShapeDtypeStruct((stations, r, LANES), jnp.bfloat16) for r in rows),
        in_specs=[SMEM, VMEM],
        out_specs=(VMEM,) * 4,
        scratch_shapes=[pltpu.VMEM((2, 120, LANES), jnp.float32)],
        compiler_params=params(size(raw.shape, raw.dtype)),
        cost_estimate=pl.CostEstimate(flops=2_000_000, bytes_accessed=2_000_000, transcendentals=0),
    )(core, raw)


def join(keep, got, small):
    if small:
        return jnp.concatenate([keep[:, :16], got, keep[:, 16:]], axis=1)
    return jnp.concatenate([keep, got], axis=1)


def select_kernel(peers, stages, sources, cap, small, me_ref, *refs):
    asked = refs[:peers]
    chunks = refs[peers : peers + 2 * stages]
    outs = refs[peers + 2 * stages :]
    me = me_ref[0]
    for d in range(peers):
        for h in range(stages):
            source = me ^ (h * (sources // 2))
            keep, got = chunks[2 * h : 2 * h + 2]
            for c in range(cap):
                row = jnp.maximum(asked[d][source, c], 0)
                out = outs[d].at[h * cap + c]
                if small:
                    out[0:16] = keep[row, 0:16]
                    out[16:32] = got[row]
                    out[32:40] = keep[row, 16:24]
                else:
                    out[0:32] = keep[row]
                    out[32:64] = got[row]


def select(me, asked, chunks, cap, small):
    peers = len(asked)
    stages = len(chunks) // 2
    sources = asked[0].shape[0]
    rows = chunks[0].shape[1] + chunks[1].shape[1]
    out = jax.ShapeDtypeStruct((stages * cap, rows, LANES), chunks[0].dtype)
    return pl.pallas_call(
        functools.partial(select_kernel, peers, stages, sources, cap, small),
        name="select",
        out_shape=(out,) * peers,
        in_specs=[SMEM] * (1 + peers) + [VMEM] * len(chunks),
        out_specs=(VMEM,) * peers,
        compiler_params=params(2 * (peers + 2) * size(out.shape, out.dtype)),
        cost_estimate=pl.CostEstimate(flops=0, bytes_accessed=1_000_000, transcendentals=0),
    )(me, *asked, *chunks)


def load_table(bufs, table):
    at = 0
    for buf in bufs:

        def copy(i, carry, buf=buf, at=at):
            table[at + i] = buf[i].astype(jnp.float32)
            return carry

        lax.fori_loop(0, buf.shape[0], copy, 0, unroll=4)
        at += buf.shape[0]


def products(table, i, j, groups):
    re = im = None
    for g in range(groups):
        ar = table[i, g * 16 : g * 16 + 8, :]
        ai = table[i, g * 16 + 8 : g * 16 + 16, :]
        br = table[j, g * 16 : g * 16 + 8, :]
        bi = table[j, g * 16 + 8 : g * 16 + 16, :]
        r = ar * br + ai * bi
        m = ai * br - ar * bi
        re = r if re is None else re + r
        im = m if im is None else im + m
    return re, im


BIG_ROWS = 17
SMALL_ROWS = 25


def cross_big(first_ref, second_ref, bufs, table, cross, out):
    pairs = out.shape[0]
    load_table(bufs, table)

    def pair(p, carry):
        re, im = products(table, first_ref[p], second_ref[p], 4)
        cross[pl.ds(p * BIG_ROWS, 8), :] = re
        cross[pl.ds(p * BIG_ROWS + 8, 8), :] = im
        return carry

    lax.fori_loop(0, pairs, pair, 0, unroll=8)
    for k in range(16):
        out[:, k * LANES : (k + 1) * LANES] = cross[pl.ds(k, pairs, stride=BIG_ROWS), :].astype(
            jnp.bfloat16
        )


def cross_small(first_ref, second_ref, bufs, table, cross, out):
    pairs = out.shape[0]
    load_table(bufs, table)

    def pair(p, carry):
        i = first_ref[p]
        j = second_ref[p]
        re, im = products(table, i, j, 2)
        at = p * SMALL_ROWS
        cross[pl.ds(at, 8), :] = re
        cross[pl.ds(at + 8, 8), :] = im
        a = table[i, 32:40, :]
        b = table[j, 32:40, :]
        cross[pl.ds(at + 16, 2), :] = a[0:2] * b[0:2] + a[2:4] * b[2:4]
        cross[pl.ds(at + 18, 2), :] = a[2:4] * b[0:2] - a[0:2] * b[2:4]
        return carry

    lax.fori_loop(0, pairs, pair, 0, unroll=8)

    def column(row):
        return cross[pl.ds(row, pairs, stride=SMALL_ROWS), :]

    for k in range(8):
        row = (k // 4) * 8 + k % 4
        out[:, k * LANES : (k + 1) * LANES] = (column(row) + column(row + 4)).astype(jnp.bfloat16)
    for k in range(2):
        row = 16 + 2 * k
        out[:, (8 + k) * LANES : (9 + k) * LANES] = (column(row) + column(row + 1)).astype(
            jnp.bfloat16
        )


def table_kernel(coarse_ref, fine_ref, big_ref, small_ref):
    half = fine_ref.shape[2] // LANES - 1
    for g in range(half + 1):
        at = slice(g * LANES, (g + 1) * LANES)
        cf = fine_ref[0, :, at]
        sf = fine_ref[1, :, at]
        if g < 8:
            ref, re, im = big_ref, g, g + 8
        elif g < half:
            ref, re, im = small_ref, g - 8, g - 8 + half - 8
        else:
            ref, re, im = small_ref, 2 * (half - 8), 2 * (half - 8) + 1
        for u in range(coarse_ref.shape[1]):
            cc = coarse_ref[0, u : u + 1, at]
            sc = coarse_ref[1, u : u + 1, at]
            rows = slice(u * FINE, (u + 1) * FINE)
            ref[rows, re * LANES : (re + 1) * LANES] = (cc * cf - sc * sf).astype(jnp.bfloat16)
            ref[rows, im * LANES : (im + 1) * LANES] = (sc * cf + cc * sf).astype(jnp.bfloat16)


def lag_bases(core, half, blocks):
    block_index = jnp.concatenate(
        [core * half + jnp.arange(half, dtype=jnp.int32), jnp.full((1,), blocks - 1, jnp.int32)]
    )
    bins = (K0 + block_index[:, None] * LANES + jnp.arange(LANES, dtype=jnp.int32)).reshape(-1)

    def base(lags):
        angles = (lags[:, None] * bins[None, :] % NFFT).astype(jnp.float32) * (2.0 * math.pi / NFFT)
        return jnp.stack([jnp.cos(angles), -jnp.sin(angles)])

    coarse = base(jnp.arange(LAGS // FINE, dtype=jnp.int32) * FINE - LAGS // 2)
    fine = base(jnp.arange(FINE, dtype=jnp.int32))
    return coarse, fine


def lag_table(coarse, fine):
    width = fine.shape[2]
    half = width // LANES - 1
    step = 8
    return pl.pallas_call(
        table_kernel,
        name="lagtable",
        grid=(LAGS // FINE // step,),
        out_shape=(
            jax.ShapeDtypeStruct((LAGS, 16 * LANES), jnp.bfloat16),
            jax.ShapeDtypeStruct((LAGS, 2 * (half + 1 - 8) * LANES), jnp.bfloat16),
        ),
        in_specs=[
            pl.BlockSpec((2, step, width), lambda u: (0, u, 0)),
            pl.BlockSpec((2, FINE, width), lambda u: (0, 0, 0)),
        ],
        out_specs=(
            pl.BlockSpec((step * FINE, 16 * LANES), lambda u: (u, 0)),
            pl.BlockSpec((step * FINE, 2 * (half + 1 - 8) * LANES), lambda u: (u, 0)),
        ),
        compiler_params=params(),
        cost_estimate=pl.CostEstimate(
            flops=LAGS * width * 6, bytes_accessed=LAGS * width * 4, transcendentals=0
        ),
    )(coarse, fine)


def dot_nt(a, b):
    return lax.dot_general(a, b, (((1,), (1,)), ((), ())), preferred_element_type=jnp.float32)


def scratch(bufs, pairs, each, *more):
    slots = sum(buf.shape[0] for buf in bufs)
    shapes = (
        ((slots,) + bufs[0].shape[1:], jnp.float32),
        ((pairs * each, LANES), jnp.float32),
    ) + more
    return dict(
        scratch_shapes=[pltpu.VMEM(*s) for s in shapes],
        compiler_params=params(*(size(*s) for s in shapes), roomy=len(bufs) == 1),
    )


def stack_cost(lags, depth, pairs):
    return pl.CostEstimate(
        flops=2 * lags * depth * pairs,
        bytes_accessed=2 * lags * depth + 4 * lags * pairs,
        transcendentals=0,
    )


def stack_small_kernel(count, tile, first_ref, second_ref, *refs):
    bufs = refs[:count]
    lag_ref, acc_ref, table, rows, cross = refs[count:]
    cross_small(first_ref, second_ref, bufs, table, rows, cross)
    for t in range(acc_ref.shape[0] // tile):
        at = slice(t * tile, (t + 1) * tile)
        acc_ref[at, :] = dot_nt(lag_ref[at, :], cross[...])


def stack_small(first, second, bufs, lag_table, tile):
    lags, depth = lag_table.shape
    pairs = first.shape[0]
    return pl.pallas_call(
        functools.partial(stack_small_kernel, len(bufs), tile),
        name="stack0",
        out_shape=jax.ShapeDtypeStruct((lags, pairs), jnp.float32),
        in_specs=[SMEM, SMEM] + [VMEM] * (len(bufs) + 1),
        out_specs=VMEM,
        cost_estimate=stack_cost(lags, depth, pairs),
        **scratch(bufs, pairs, SMALL_ROWS, ((pairs, depth), jnp.bfloat16)),
    )(first, second, *bufs, lag_table)


def finish(part, core, lag_ref, acc_ref, cross, send_ref, keep_ref):
    outer, tile, _ = send_ref.shape
    group_rows = lag_ref.shape[0] // (2 * outer)
    for mine in range(2):
        for at in range(outer):
            group = 2 * at + (core if mine else 1 - core)
            lags = pl.ds(pl.multiple_of(group * group_rows + part * tile, tile), tile)
            value = acc_ref[lags, :] + dot_nt(lag_ref[lags, :], cross[...])
            if mine:
                keep_ref[at] = value
            else:
                send_ref[at] = value.astype(send_ref.dtype)


def stack_outputs(acc, groups, parts):
    lags, pairs = acc.shape
    shape = (groups // 2, lags // groups // parts, pairs)
    return [jax.ShapeDtypeStruct(shape, jnp.bfloat16), jax.ShapeDtypeStruct(shape, jnp.float32)]


def stack_first_kernel(count, core_ref, first_ref, second_ref, *refs):
    bufs = refs[:count]
    lag_ref, acc_ref, send_ref, keep_ref, cross, table, rows = refs[count:]
    cross_big(first_ref, second_ref, bufs, table, rows, cross)
    finish(0, core_ref[0], lag_ref, acc_ref, cross, send_ref, keep_ref)


def stack_first(core, first, second, bufs, lag_table, acc, groups, parts):
    lags, depth = lag_table.shape
    pairs = acc.shape[1]
    return pl.pallas_call(
        functools.partial(stack_first_kernel, len(bufs)),
        name="stack1",
        in_specs=[SMEM] * 3 + [VMEM] * (len(bufs) + 2),
        out_specs=[VMEM] * 3,
        out_shape=stack_outputs(acc, groups, parts)
        + [jax.ShapeDtypeStruct((pairs, depth), jnp.bfloat16)],
        cost_estimate=stack_cost(lags // parts, depth, pairs),
        **scratch(bufs, pairs, BIG_ROWS),
    )(core, first, second, *bufs, lag_table, acc)


def stack_next_kernel(part, core_ref, lag_ref, acc_ref, cross, send_ref, keep_ref):
    finish(part, core_ref[0], lag_ref, acc_ref, cross, send_ref, keep_ref)


def stack_next(core, lag_table, acc, cross, groups, part, parts):
    lags, depth = lag_table.shape
    return pl.pallas_call(
        functools.partial(stack_next_kernel, part),
        name="stack2",
        in_specs=[SMEM] + [VMEM] * 3,
        out_specs=[VMEM] * 2,
        out_shape=stack_outputs(acc, groups, parts),
        compiler_params=params(),
        cost_estimate=stack_cost(lags // parts, depth, acc.shape[1]),
    )(core, lag_table, acc, cross)


def away_kernel(place_ref, keep_ref, near_ref, *outs):
    for d, out in enumerate(outs):
        at = place_ref[0] ^ (d + 1)
        out[...] = (keep_ref[at] + near_ref[at].astype(jnp.float32)).astype(out.dtype)


def sum_away(place, keep, near):
    outer, lags, pairs = keep.shape
    return pl.pallas_call(
        away_kernel,
        name="away",
        out_shape=[jax.ShapeDtypeStruct((lags, pairs), near.dtype)] * (outer - 1),
        in_specs=[SMEM, VMEM, VMEM],
        out_specs=[VMEM] * (outer - 1),
        compiler_params=params(2 * size(keep.shape, jnp.float32)),
        cost_estimate=pl.CostEstimate(
            flops=keep.size, bytes_accessed=6 * keep.size, transcendentals=0
        ),
    )(place, keep, near)


def result_kernel(scale, parts, place_ref, *refs):
    out = refs[-1]
    each = (len(refs) - 1) // parts
    place = place_ref[0]
    for part in range(parts):
        keep, near, *far = refs[part * each : (part + 1) * each]
        total = keep[place] + near[place].astype(jnp.float32)
        for ref in far:
            total = total + ref[...].astype(jnp.float32)
        lags = total.shape[0]
        out[part * lags : (part + 1) * lags, :] = scale * total


def result(place, pieces, scale):
    operands = [x for piece in pieces for x in piece]
    _, lags, pairs = pieces[0][0].shape
    return pl.pallas_call(
        functools.partial(result_kernel, scale, len(pieces)),
        name="result",
        out_shape=jax.ShapeDtypeStruct((lags * len(pieces), pairs), jnp.float32),
        in_specs=[SMEM] + [VMEM] * len(operands),
        out_specs=VMEM,
        compiler_params=params(2 * size((lags * len(pieces), pairs), jnp.float32)),
        cost_estimate=pl.CostEstimate(
            flops=lags * pairs * 4, bytes_accessed=lags * pairs * 16, transcendentals=0
        ),
    )(place, *operands)


def swap(x, axis, mask):
    return lax.ppermute(x, axis, [(i, i ^ mask) for i in range(lax.axis_size(axis))])


def swap_both(x, mask_pairs, mask_win):
    groups = lax.axis_size("win")
    perm = [
        (p * groups + w, (p ^ mask_pairs) * groups + (w ^ mask_win))
        for p in range(lax.axis_size("pairs"))
        for w in range(groups)
    ]
    return lax.ppermute(x, ("pairs", "win"), perm)


def after(x, *earlier):
    return lax.optimization_barrier((x,) + earlier)[0]


def local(spectra, requests, pair_first, pair_second):
    stations, windows, _, bins = spectra.shape
    sources = lax.axis_size("pairs")
    groups = lax.axis_size("win")
    cap = requests.shape[2]
    me = lax.axis_index("pairs").astype(jnp.int32)
    group = lax.axis_index("win").astype(jnp.int32)
    core = group & 1
    blocks = bins // LANES
    half = blocks // 2
    assert windows == 2 and blocks == 2 * half + 1 and half == 12 and groups % 2 == 0
    assert stations % 2 == 0

    keep_big, keep_small, give_big, give_small = whiten(core[None], spectra)
    near_big = swap(give_big, "win", 1)
    near_small = swap(give_small, "win", 1)

    slots = sources * cap
    wanted = requests[0]
    if two_stage(sources):
        far = sources // 2
        chunks = {
            "small": [
                keep_small,
                near_small,
                swap(keep_small, "pairs", far),
                swap_both(give_small, far, 1),
            ],
            "big": [keep_big, near_big, swap(keep_big, "pairs", far), swap_both(give_big, far, 1)],
        }
        wanted = after(wanted, keep_small)
        asked = [wanted] + [swap(wanted, "pairs", d) for d in range(1, far)]
        arrived = {}
        for name, chunk in chunks.items():
            outs = select(me[None], asked, chunk, cap, name == "small")
            arrived[name] = [outs[0]] + [swap(outs[d], "pairs", d) for d in range(1, far)]
        small, big = arrived["small"], arrived["big"]
        core_table = core

        def row_of(slot):
            apart = (slot // cap) ^ me
            return (apart % far) * (2 * cap) + (apart // far) * cap + slot % cap

    else:
        asked_rows = lax.all_to_all(wanted, "pairs", split_axis=0, concat_axis=0, tiled=True)

        def exchange(chunk):
            outgoing = chunk[jnp.maximum(asked_rows, 0)]
            arrived = lax.all_to_all(outgoing, "pairs", split_axis=0, concat_axis=0, tiled=True)
            return [arrived.reshape((slots,) + chunk.shape[1:])]

        big = exchange(join(keep_big, near_big, False))
        small = exchange(join(keep_small, near_small, True))
        core_table = core

        def row_of(slot):
            return slot

    coarse, fine = lag_bases(core_table, half, blocks)
    table_big, table_small = lag_table(coarse, fine)
    first = row_of(pair_first)
    second = row_of(pair_second)
    acc = stack_small(first, second, small, table_small, LAGS // groups)

    place = (group >> 1)[None]
    parts = 2
    pieces = []
    send, keep, cross = stack_first(core[None], first, second, big, table_big, acc, groups, parts)
    for part in range(parts):
        if part > 0:
            send, keep = stack_next(core[None], table_big, acc, cross, groups, part, parts)
        near = swap(send, "win", 1)
        away = sum_away(place, keep, near)
        pieces.append([keep, near] + [swap(x, "win", 2 * (d + 1)) for d, x in enumerate(away)])
    return result(place, pieces, 1.0 / math.sqrt(bins * windows * groups))


def two_stage(sources):
    return sources & (sources - 1) == 0 and 4 <= sources <= 16


def solution(mesh):
    step = jax.shard_map(
        local,
        mesh=mesh,
        in_specs=(P("pairs", "win", None, None), P("pairs", None, None), P("pairs"), P("pairs")),
        out_specs=P("win", "pairs"),
        check_vma=False,
    )
    sources = mesh.shape["pairs"]
    if not two_stage(sources):
        return step
    return step
```

```python
import functools
import math

import jax
import jax.numpy as jnp
from jax import lax
from jax.experimental import pallas as pl
from jax.experimental.pallas import tpu as pltpu
from jax.sharding import PartitionSpec as P


LAGS = 2048
NFFT = 18000
K0 = 360
LANES = 128
EPS = 1e-06
FINE = 32
VMEM = pl.BlockSpec(memory_space=pltpu.VMEM)
SMEM = pl.BlockSpec(memory_space=pltpu.SMEM)


def params(*nbytes, roomy=False):
    limit = 60 if roomy else sum(nbytes) // 1024**2 + 5
    return pltpu.CompilerParams(vmem_limit_bytes=limit * 1024**2)


def size(shape, dtype):
    return math.prod(shape) * jnp.dtype(dtype).itemsize


def whiten_kernel(core_ref, raw_ref, keep_ref, give_ref, tmp):
    stations, windows, _, bins = raw_ref.shape
    blocks = bins // LANES
    half = blocks // 2
    core = core_ref[0]

    def white(re, im):
        power = jnp.sum(re * re + im * im, axis=1, keepdims=True) * (1.0 / (2 * LANES))
        scale = lax.rsqrt(power + EPS)
        return re * scale, im * scale

    def station(s, slot):
        for w in range(windows):
            for b in range(blocks):
                value = raw_ref[s, w, :, b * LANES : (b + 1) * LANES]
                side, at = divmod(b, half)
                if side == 2:
                    row = 96 + w
                elif at < 8:
                    row = side * 48 + w * 16 + at
                else:
                    row = side * 48 + 32 + w * 4 + at - 8
                tmp[slot, pl.ds(row, 2, stride=8), :] = value
        for mine, out in ((True, keep_ref), (False, give_ref)):
            base = pl.multiple_of((core if mine else 1 - core) * 48, 16)
            for g in range(3):
                re = tmp[slot, pl.ds(base + g * 16, 8), :]
                im = tmp[slot, pl.ds(base + g * 16 + 8, 8), :]
                rows = jnp.concatenate(white(re, im), axis=0).astype(jnp.bfloat16)
                out[s, g * 16 : g * 16 + 16, :] = rows
        re, im = white(tmp[slot, 96:104, :], tmp[slot, 104:112, :])
        tmp[slot, 112:114, :] = re[0:windows]
        tmp[slot, 114:116, :] = im[0:windows]
        keep_ref[s, 48:56, :] = tmp[slot, 112:120, :].astype(jnp.bfloat16)

    tmp[...] = jnp.zeros_like(tmp)

    def several(i, carry):
        for slot in range(2):
            station(2 * i + slot, slot)
        return carry

    lax.fori_loop(0, stations // 2, several, 0)


def whiten(core, raw):
    stations = raw.shape[0]
    return pl.pallas_call(
        whiten_kernel,
        name="whiten",
        out_shape=tuple(jax.ShapeDtypeStruct((stations, r, LANES), jnp.bfloat16) for r in (56, 48)),
        in_specs=[SMEM, VMEM],
        out_specs=(VMEM,) * 2,
        scratch_shapes=[pltpu.VMEM((2, 120, LANES), jnp.float32)],
        compiler_params=params(size(raw.shape, raw.dtype)),
        cost_estimate=pl.CostEstimate(flops=2_000_000, bytes_accessed=2_000_000, transcendentals=0),
    )(core, raw)


BIG_PIECES = ((0, 0, 0, 32), (32, 1, 0, 32))
SMALL_PIECES = ((0, 0, 32, 16), (16, 1, 32, 16), (32, 0, 48, 8))
ALL_PIECES = BIG_PIECES + tuple(
    (64 + at, which, start, rows) for at, which, start, rows in SMALL_PIECES
)


def join(keep, got):
    return jnp.concatenate(
        [(keep, got)[which][:, start : start + rows] for _, which, start, rows in ALL_PIECES], axis=1
    )


def select_kernel(pieces, flip, cap, me_ref, *refs):
    peers = (len(refs) - 2) // 2
    asked = refs[:peers]
    chunk = refs[peers : peers + 2]
    source = me_ref[0] ^ flip
    for d, out in enumerate(refs[peers + 2 :]):
        for c in range(cap):
            row = jnp.maximum(asked[d][source, c], 0)
            for at, which, start, rows in pieces:
                out[c, at : at + rows] = chunk[which][row, start : start + rows]


def select(me, asked, keep, got, flip, pieces):
    peers = len(asked)
    cap = asked[0].shape[1]
    rows = sum(piece[3] for piece in pieces)
    out = jax.ShapeDtypeStruct((cap, rows, LANES), keep.dtype)
    return pl.pallas_call(
        functools.partial(select_kernel, pieces, flip, cap),
        name="select",
        out_shape=(out,) * peers,
        in_specs=[SMEM] * (1 + peers) + [VMEM] * 2,
        out_specs=(VMEM,) * peers,
        compiler_params=params(),
        cost_estimate=pl.CostEstimate(flops=0, bytes_accessed=1_000_000, transcendentals=0),
    )(me, *asked, keep, got)


def load_table(bufs, table, lo):
    rows = table.shape[1]
    at = 0
    for buf in bufs:
        start = lo if buf.shape[1] > rows else 0

        def copy(i, carry, buf=buf, at=at, start=start):
            table[at + i] = buf[i, start : start + rows].astype(jnp.float32)
            return carry

        lax.fori_loop(0, buf.shape[0], copy, 0, unroll=4)
        at += buf.shape[0]


def products(table, i, j, groups):
    re = im = None
    for g in range(groups):
        ar = table[i, g * 16 : g * 16 + 8, :]
        ai = table[i, g * 16 + 8 : g * 16 + 16, :]
        br = table[j, g * 16 : g * 16 + 8, :]
        bi = table[j, g * 16 + 8 : g * 16 + 16, :]
        r = ar * br + ai * bi
        m = ai * br - ar * bi
        re = r if re is None else re + r
        im = m if im is None else im + m
    return re, im


BIG_ROWS = 17
SMALL_ROWS = 25


def cross_big(first_ref, second_ref, bufs, table, cross, out):
    pairs = out.shape[0]
    load_table(bufs, table, 0)

    def pair(p, carry):
        re, im = products(table, first_ref[p], second_ref[p], 4)
        cross[pl.ds(p * BIG_ROWS, 8), :] = re
        cross[pl.ds(p * BIG_ROWS + 8, 8), :] = im
        return carry

    lax.fori_loop(0, pairs, pair, 0, unroll=8)
    for k in range(16):
        out[:, k * LANES : (k + 1) * LANES] = cross[pl.ds(k, pairs, stride=BIG_ROWS), :].astype(
            jnp.bfloat16
        )


def cross_small(first_ref, second_ref, bufs, table, cross, out):
    pairs = out.shape[0]
    load_table(bufs, table, 64)

    def pair(p, carry):
        i = first_ref[p]
        j = second_ref[p]
        re, im = products(table, i, j, 2)
        at = p * SMALL_ROWS
        cross[pl.ds(at, 8), :] = re
        cross[pl.ds(at + 8, 8), :] = im
        a = table[i, 32:40, :]
        b = table[j, 32:40, :]
        cross[pl.ds(at + 16, 2), :] = a[0:2] * b[0:2] + a[2:4] * b[2:4]
        cross[pl.ds(at + 18, 2), :] = a[2:4] * b[0:2] - a[0:2] * b[2:4]
        return carry

    lax.fori_loop(0, pairs, pair, 0, unroll=8)

    def column(row):
        return cross[pl.ds(row, pairs, stride=SMALL_ROWS), :]

    for k in range(8):
        row = (k // 4) * 8 + k % 4
        out[:, k * LANES : (k + 1) * LANES] = (column(row) + column(row + 4)).astype(jnp.bfloat16)
    for k in range(2):
        row = 16 + 2 * k
        out[:, (8 + k) * LANES : (9 + k) * LANES] = (column(row) + column(row + 1)).astype(
            jnp.bfloat16
        )


def table_kernel(coarse_ref, fine_ref, big_ref, small_ref):
    half = fine_ref.shape[2] // LANES - 1
    for g in range(half + 1):
        at = slice(g * LANES, (g + 1) * LANES)
        cf = fine_ref[0, :, at]
        sf = fine_ref[1, :, at]
        if g < 8:
            ref, re, im = big_ref, g, g + 8
        elif g < half:
            ref, re, im = small_ref, g - 8, g - 8 + half - 8
        else:
            ref, re, im = small_ref, 2 * (half - 8), 2 * (half - 8) + 1
        for u in range(coarse_ref.shape[1]):
            cc = coarse_ref[0, u : u + 1, at]
            sc = coarse_ref[1, u : u + 1, at]
            rows = slice(u * FINE, (u + 1) * FINE)
            ref[rows, re * LANES : (re + 1) * LANES] = (cc * cf - sc * sf).astype(jnp.bfloat16)
            ref[rows, im * LANES : (im + 1) * LANES] = (sc * cf + cc * sf).astype(jnp.bfloat16)


def lag_bases(core, half, blocks):
    block_index = jnp.concatenate(
        [core * half + jnp.arange(half, dtype=jnp.int32), jnp.full((1,), blocks - 1, jnp.int32)]
    )
    bins = (K0 + block_index[:, None] * LANES + jnp.arange(LANES, dtype=jnp.int32)).reshape(-1)

    def base(lags):
        angles = (lags[:, None] * bins[None, :] % NFFT).astype(jnp.float32) * (2.0 * math.pi / NFFT)
        return jnp.stack([jnp.cos(angles), -jnp.sin(angles)])

    coarse = base(jnp.arange(LAGS // FINE, dtype=jnp.int32) * FINE - LAGS // 2)
    fine = base(jnp.arange(FINE, dtype=jnp.int32))
    return coarse, fine


def lag_table(coarse, fine):
    width = fine.shape[2]
    half = width // LANES - 1
    step = 8
    return pl.pallas_call(
        table_kernel,
        name="lagtable",
        grid=(LAGS // FINE // step,),
        out_shape=(
            jax.ShapeDtypeStruct((LAGS, 16 * LANES), jnp.bfloat16),
            jax.ShapeDtypeStruct((LAGS, 2 * (half + 1 - 8) * LANES), jnp.bfloat16),
        ),
        in_specs=[
            pl.BlockSpec((2, step, width), lambda u: (0, u, 0)),
            pl.BlockSpec((2, FINE, width), lambda u: (0, 0, 0)),
        ],
        out_specs=(
            pl.BlockSpec((step * FINE, 16 * LANES), lambda u: (u, 0)),
            pl.BlockSpec((step * FINE, 2 * (half + 1 - 8) * LANES), lambda u: (u, 0)),
        ),
        compiler_params=params(),
        cost_estimate=pl.CostEstimate(
            flops=LAGS * width * 6, bytes_accessed=LAGS * width * 4, transcendentals=0
        ),
    )(coarse, fine)


def dot_nt(a, b):
    return lax.dot_general(a, b, (((1,), (1,)), ((), ())), preferred_element_type=jnp.float32)


def scratch(chunk, bufs, pairs, *more):
    slots = sum(buf.shape[0] for buf in bufs)
    _, each, rows = CHUNKS[chunk]
    shapes = (
        ((slots, rows, LANES), jnp.float32),
        ((pairs * each, LANES), jnp.float32),
    ) + more
    return dict(
        scratch_shapes=[pltpu.VMEM(*s) for s in shapes],
        compiler_params=params(*(size(*s) for s in shapes), roomy=len(bufs) == 1),
    )


def stack_cost(lags, depth, pairs):
    return pl.CostEstimate(
        flops=2 * lags * depth * pairs,
        bytes_accessed=2 * lags * depth + 4 * lags * pairs,
        transcendentals=0,
    )


CHUNKS = {"big": (cross_big, BIG_ROWS, 64), "small": (cross_small, SMALL_ROWS, 40)}


def stack_all_kernel(chunk, count, tile, first_ref, second_ref, *refs):
    bufs = refs[:count]
    lag_ref, acc_ref, table, rows, cross = refs[count:]
    CHUNKS[chunk][0](first_ref, second_ref, bufs, table, rows, cross)
    for t in range(acc_ref.shape[0] // tile):
        at = slice(t * tile, (t + 1) * tile)
        acc_ref[at, :] = dot_nt(lag_ref[at, :], cross[...])


def stack_all(chunk, first, second, bufs, lag_table, tile):
    lags, depth = lag_table.shape
    pairs = first.shape[0]
    return pl.pallas_call(
        functools.partial(stack_all_kernel, chunk, len(bufs), tile),
        name="stack0",
        out_shape=jax.ShapeDtypeStruct((lags, pairs), jnp.float32),
        in_specs=[SMEM, SMEM] + [VMEM] * (len(bufs) + 1),
        out_specs=VMEM,
        cost_estimate=stack_cost(lags, depth, pairs),
        **scratch(chunk, bufs, pairs, ((pairs, depth), jnp.bfloat16)),
    )(first, second, *bufs, lag_table)


def finish(part, core, lag_ref, acc_ref, cross, send_ref, keep_ref):
    outer, tile, _ = send_ref.shape
    group_rows = lag_ref.shape[0] // (2 * outer)
    for mine in range(2):
        for at in range(outer):
            group = 2 * at + (core if mine else 1 - core)
            lags = pl.ds(pl.multiple_of(group * group_rows + part * tile, tile), tile)
            value = acc_ref[lags, :] + dot_nt(lag_ref[lags, :], cross[...])
            if mine:
                keep_ref[at] = value
            else:
                send_ref[at] = value.astype(send_ref.dtype)


def stack_outputs(acc, groups, parts):
    lags, pairs = acc.shape
    shape = (groups // 2, lags // groups // parts, pairs)
    return [jax.ShapeDtypeStruct(shape, jnp.bfloat16), jax.ShapeDtypeStruct(shape, jnp.float32)]


def stack_first_kernel(chunk, count, core_ref, first_ref, second_ref, *refs):
    bufs = refs[:count]
    lag_ref, acc_ref, send_ref, keep_ref, cross, table, rows = refs[count:]
    CHUNKS[chunk][0](first_ref, second_ref, bufs, table, rows, cross)
    finish(0, core_ref[0], lag_ref, acc_ref, cross, send_ref, keep_ref)


def stack_first(chunk, core, first, second, bufs, lag_table, acc, groups, parts):
    lags, depth = lag_table.shape
    pairs = acc.shape[1]
    return pl.pallas_call(
        functools.partial(stack_first_kernel, chunk, len(bufs)),
        name="stack1",
        in_specs=[SMEM] * 3 + [VMEM] * (len(bufs) + 2),
        out_specs=[VMEM] * 3,
        out_shape=stack_outputs(acc, groups, parts)
        + [jax.ShapeDtypeStruct((pairs, depth), jnp.bfloat16)],
        cost_estimate=stack_cost(lags // parts, depth, pairs),
        **scratch(chunk, bufs, pairs),
    )(core, first, second, *bufs, lag_table, acc)


def stack_next_kernel(part, core_ref, lag_ref, acc_ref, cross, send_ref, keep_ref):
    finish(part, core_ref[0], lag_ref, acc_ref, cross, send_ref, keep_ref)


def stack_next(core, lag_table, acc, cross, groups, part, parts):
    lags, depth = lag_table.shape
    return pl.pallas_call(
        functools.partial(stack_next_kernel, part),
        name="stack2",
        in_specs=[SMEM] + [VMEM] * 3,
        out_specs=[VMEM] * 2,
        out_shape=stack_outputs(acc, groups, parts),
        compiler_params=params(),
        cost_estimate=stack_cost(lags // parts, depth, acc.shape[1]),
    )(core, lag_table, acc, cross)


def away_kernel(place_ref, keep_ref, near_ref, *outs):
    for d, out in enumerate(outs):
        at = place_ref[0] ^ (d + 1)
        out[...] = (keep_ref[at] + near_ref[at].astype(jnp.float32)).astype(out.dtype)


def sum_away(place, keep, near):
    outer, lags, pairs = keep.shape
    return pl.pallas_call(
        away_kernel,
        name="away",
        out_shape=[jax.ShapeDtypeStruct((lags, pairs), near.dtype)] * (outer - 1),
        in_specs=[SMEM, VMEM, VMEM],
        out_specs=[VMEM] * (outer - 1),
        compiler_params=params(2 * size(keep.shape, jnp.float32)),
        cost_estimate=pl.CostEstimate(
            flops=keep.size, bytes_accessed=6 * keep.size, transcendentals=0
        ),
    )(place, keep, near)


def result_kernel(scale, parts, place_ref, *refs):
    out = refs[-1]
    each = (len(refs) - 1) // parts
    place = place_ref[0]
    for part in range(parts):
        keep, near, *far = refs[part * each : (part + 1) * each]
        total = keep[place] + near[place].astype(jnp.float32)
        for ref in far:
            total = total + ref[...].astype(jnp.float32)
        lags = total.shape[0]
        out[part * lags : (part + 1) * lags, :] = scale * total


def result(place, pieces, scale):
    operands = [x for piece in pieces for x in piece]
    _, lags, pairs = pieces[0][0].shape
    return pl.pallas_call(
        functools.partial(result_kernel, scale, len(pieces)),
        name="result",
        out_shape=jax.ShapeDtypeStruct((lags * len(pieces), pairs), jnp.float32),
        in_specs=[SMEM] + [VMEM] * len(operands),
        out_specs=VMEM,
        compiler_params=params(2 * size((lags * len(pieces), pairs), jnp.float32)),
        cost_estimate=pl.CostEstimate(
            flops=lags * pairs * 4, bytes_accessed=lags * pairs * 16, transcendentals=0
        ),
    )(place, *operands)


def swap(x, axis, mask):
    return lax.ppermute(x, axis, [(i, i ^ mask) for i in range(lax.axis_size(axis))])


def swap_both(x, mask_pairs, mask_win):
    groups = lax.axis_size("win")
    perm = [
        (p * groups + w, (p ^ mask_pairs) * groups + (w ^ mask_win))
        for p in range(lax.axis_size("pairs"))
        for w in range(groups)
    ]
    return lax.ppermute(x, ("pairs", "win"), perm)


def after(x, *earlier):
    return lax.optimization_barrier((x,) + earlier)[0]


def local(spectra, requests, pair_first, pair_second):
    stations, windows, _, bins = spectra.shape
    sources = lax.axis_size("pairs")
    groups = lax.axis_size("win")
    cap = requests.shape[2]
    me = lax.axis_index("pairs").astype(jnp.int32)
    group = lax.axis_index("win").astype(jnp.int32)
    core = group & 1
    blocks = bins // LANES
    half = blocks // 2
    assert windows == 2 and blocks == 2 * half + 1 and half == 12 and groups % 2 == 0
    assert stations % 2 == 0

    keep, give = whiten(core[None], spectra)
    near = swap(give, "win", 1)

    wanted = requests[0]
    if two_stage(sources):
        far = sources // 2
        wanted = after(wanted, keep)
        asked = [wanted] + [swap(wanted, "pairs", d) for d in range(1, far)]
        far_keep = swap(keep, "pairs", far)
        far_give = swap_both(give, far, 1)

        def to_half(outs):
            return [outs[0]] + [swap(outs[d], "pairs", d) for d in range(1, far)]

        own = select(me[None], asked, keep, near, 0, ALL_PIECES)
        own = to_half(own)
        big = select(me[None], asked, far_keep, far_give, far, BIG_PIECES)
        big = own + to_half(big)
        small = select(me[None], asked, far_keep, far_give, far, SMALL_PIECES)
        small = own + to_half(small)

        def row_of(slot):
            return ((slot // cap) ^ me) * cap + slot % cap

    else:
        asked_rows = lax.all_to_all(wanted, "pairs", split_axis=0, concat_axis=0, tiled=True)
        outgoing = join(keep, near)[jnp.maximum(asked_rows, 0)]
        arrived = lax.all_to_all(outgoing, "pairs", split_axis=0, concat_axis=0, tiled=True)
        big = small = [arrived.reshape((sources * cap,) + outgoing.shape[2:])]

        def row_of(slot):
            return slot

    coarse, fine = lag_bases(core, half, blocks)
    table_big, table_small = lag_table(coarse, fine)
    first = row_of(pair_first)
    second = row_of(pair_second)
    acc = stack_all("big", first, second, big, table_big, LAGS // groups)

    place = (group >> 1)[None]
    parts = 2
    pieces = []
    send, kept, cross = stack_first(
        "small", core[None], first, second, small, table_small, acc, groups, parts
    )
    for part in range(parts):
        if part > 0:
            send, kept = stack_next(core[None], table_small, acc, cross, groups, part, parts)
        summed = swap(send, "win", 1)
        away = sum_away(place, kept, summed)
        pieces.append([kept, summed] + [swap(x, "win", 2 * (d + 1)) for d, x in enumerate(away)])
    return result(place, pieces, 1.0 / math.sqrt(bins * windows * groups))


def two_stage(sources):
    return sources & (sources - 1) == 0 and 4 <= sources <= 16


def solution(mesh):
    step = jax.shard_map(
        local,
        mesh=mesh,
        in_specs=(P("pairs", "win", None, None), P("pairs", None, None), P("pairs"), P("pairs")),
        out_specs=P("win", "pairs"),
        check_vma=False,
    )
    sources = mesh.shape["pairs"]
    if not two_stage(sources):
        return step
    return step
```

```python
import functools
import math

import jax
import jax.numpy as jnp
from jax import lax
from jax.experimental import pallas as pl
from jax.experimental.pallas import tpu as pltpu
from jax.sharding import PartitionSpec as P


LAGS = 2048
NFFT = 18000
K0 = 360
LANES = 128
EPS = 1e-06
FINE = 32
VMEM = pl.BlockSpec(memory_space=pltpu.VMEM)
SMEM = pl.BlockSpec(memory_space=pltpu.SMEM)


def params(*nbytes, roomy=False):
    limit = 60 if roomy else sum(nbytes) // 1024**2 + 5
    return pltpu.CompilerParams(vmem_limit_bytes=limit * 1024**2)


def size(shape, dtype):
    return math.prod(shape) * jnp.dtype(dtype).itemsize


def whiten_kernel(core_ref, raw_ref, keep_big, keep_small, give_big, give_small, tmp):
    stations, windows, _, bins = raw_ref.shape
    blocks = bins // LANES
    half = blocks // 2
    core = core_ref[0]

    def white(re, im):
        power = jnp.sum(re * re + im * im, axis=1, keepdims=True) * (1.0 / (2 * LANES))
        scale = lax.rsqrt(power + EPS)
        return re * scale, im * scale

    def station(s, slot):
        for w in range(windows):
            for b in range(blocks):
                value = raw_ref[s, w, :, b * LANES : (b + 1) * LANES]
                side, at = divmod(b, half)
                if side == 2:
                    row = 96 + w
                elif at < 8:
                    row = side * 48 + w * 16 + at
                else:
                    row = side * 48 + 32 + w * 4 + at - 8
                tmp[slot, pl.ds(row, 2, stride=8), :] = value
        for mine, big, small in ((True, keep_big, keep_small), (False, give_big, give_small)):
            base = pl.multiple_of((core if mine else 1 - core) * 48, 16)
            for g in range(3):
                re = tmp[slot, pl.ds(base + g * 16, 8), :]
                im = tmp[slot, pl.ds(base + g * 16 + 8, 8), :]
                rows = jnp.concatenate(white(re, im), axis=0).astype(jnp.bfloat16)
                if g < 2:
                    big[s, g * 16 : g * 16 + 16, :] = rows
                else:
                    small[s, 0:16, :] = rows
        re, im = white(tmp[slot, 96:104, :], tmp[slot, 104:112, :])
        tmp[slot, 112:114, :] = re[0:windows]
        tmp[slot, 114:116, :] = im[0:windows]
        keep_small[s, 16:24, :] = tmp[slot, 112:120, :].astype(jnp.bfloat16)

    tmp[...] = jnp.zeros_like(tmp)

    def several(i, carry):
        for slot in range(2):
            station(2 * i + slot, slot)
        return carry

    lax.fori_loop(0, stations // 2, several, 0)


def whiten(core, raw):
    stations = raw.shape[0]
    rows = (32, 24, 32, 16)
    return pl.pallas_call(
        whiten_kernel,
        name="whiten",
        out_shape=tuple(jax.ShapeDtypeStruct((stations, r, LANES), jnp.bfloat16) for r in rows),
        in_specs=[SMEM, VMEM],
        out_specs=(VMEM,) * 4,
        scratch_shapes=[pltpu.VMEM((2, 120, LANES), jnp.float32)],
        compiler_params=params(size(raw.shape, raw.dtype)),
        cost_estimate=pl.CostEstimate(flops=2_000_000, bytes_accessed=2_000_000, transcendentals=0),
    )(core, raw)


def join(keep, got, small):
    if small:
        return jnp.concatenate([keep[:, :16], got, keep[:, 16:]], axis=1)
    return jnp.concatenate([keep, got], axis=1)


def select_kernel(peers, stages, sources, cap, small, me_ref, *refs):
    asked = refs[:peers]
    chunks = refs[peers : peers + 2 * stages]
    outs = refs[peers + 2 * stages :]
    me = me_ref[0]
    for d in range(peers):
        for h in range(stages):
            source = me ^ (h * (sources // 2))
            keep, got = chunks[2 * h : 2 * h + 2]
            for c in range(cap):
                row = asked[d][source, c]
                out = outs[d].at[h * cap + c]
                if small:
                    out[0:16] = keep[row, 0:16]
                    out[16:32] = got[row]
                    out[32:40] = keep[row, 16:24]
                else:
                    out[0:32] = keep[row]
                    out[32:64] = got[row]


def select(me, asked, chunks, cap, small):
    peers = len(asked)
    stages = len(chunks) // 2
    sources = asked[0].shape[0]
    rows = chunks[0].shape[1] + chunks[1].shape[1]
    out = jax.ShapeDtypeStruct((stages * cap, rows, LANES), chunks[0].dtype)
    return pl.pallas_call(
        functools.partial(select_kernel, peers, stages, sources, cap, small),
        name="select",
        out_shape=(out,) * peers,
        in_specs=[SMEM] * (1 + peers) + [VMEM] * len(chunks),
        out_specs=(VMEM,) * peers,
        compiler_params=params(2 * (peers + 2) * size(out.shape, out.dtype)),
        cost_estimate=pl.CostEstimate(flops=0, bytes_accessed=1_000_000, transcendentals=0),
    )(me, *asked, *chunks)


def load_table(bufs, table):
    at = 0
    for buf in bufs:

        def copy(i, carry, buf=buf, at=at):
            table[at + i] = buf[i].astype(jnp.float32)
            return carry

        lax.fori_loop(0, buf.shape[0], copy, 0, unroll=4)
        at += buf.shape[0]


def products(table, i, j, groups):
    re = im = None
    for g in range(groups):
        ar = table[i, g * 16 : g * 16 + 8, :]
        ai = table[i, g * 16 + 8 : g * 16 + 16, :]
        br = table[j, g * 16 : g * 16 + 8, :]
        bi = table[j, g * 16 + 8 : g * 16 + 16, :]
        r = ar * br + ai * bi
        m = ai * br - ar * bi
        re = r if re is None else re + r
        im = m if im is None else im + m
    return re, im


BIG_ROWS = 17
SMALL_ROWS = 25


def cross_big(first_ref, second_ref, bufs, table, cross, out):
    pairs = out.shape[0]
    load_table(bufs, table)

    def pair(p, carry):
        re, im = products(table, first_ref[p], second_ref[p], 4)
        cross[pl.ds(p * BIG_ROWS, 8), :] = re
        cross[pl.ds(p * BIG_ROWS + 8, 8), :] = im
        return carry

    lax.fori_loop(0, pairs, pair, 0, unroll=8)
    for k in range(16):
        out[:, k * LANES : (k + 1) * LANES] = cross[pl.ds(k, pairs, stride=BIG_ROWS), :].astype(
            jnp.bfloat16
        )


def cross_small(first_ref, second_ref, bufs, table, cross, out):
    pairs = out.shape[0]
    load_table(bufs, table)

    def pair(p, carry):
        i = first_ref[p]
        j = second_ref[p]
        re, im = products(table, i, j, 2)
        at = p * SMALL_ROWS
        cross[pl.ds(at, 8), :] = re
        cross[pl.ds(at + 8, 8), :] = im
        a = table[i, 32:40, :]
        b = table[j, 32:40, :]
        cross[pl.ds(at + 16, 2), :] = a[0:2] * b[0:2] + a[2:4] * b[2:4]
        cross[pl.ds(at + 18, 2), :] = a[2:4] * b[0:2] - a[0:2] * b[2:4]
        return carry

    lax.fori_loop(0, pairs, pair, 0, unroll=8)

    def column(row):
        return cross[pl.ds(row, pairs, stride=SMALL_ROWS), :]

    for k in range(8):
        row = (k // 4) * 8 + k % 4
        out[:, k * LANES : (k + 1) * LANES] = (column(row) + column(row + 4)).astype(jnp.bfloat16)
    for k in range(2):
        row = 16 + 2 * k
        out[:, (8 + k) * LANES : (9 + k) * LANES] = (column(row) + column(row + 1)).astype(
            jnp.bfloat16
        )


def table_kernel(coarse_ref, fine_ref, big_ref, small_ref):
    half = fine_ref.shape[2] // LANES - 1
    for g in range(half + 1):
        at = slice(g * LANES, (g + 1) * LANES)
        cf = fine_ref[0, :, at]
        sf = fine_ref[1, :, at]
        if g < 8:
            ref, re, im = big_ref, g, g + 8
        elif g < half:
            ref, re, im = small_ref, g - 8, g - 8 + half - 8
        else:
            ref, re, im = small_ref, 2 * (half - 8), 2 * (half - 8) + 1
        for u in range(coarse_ref.shape[1]):
            cc = coarse_ref[0, u : u + 1, at]
            sc = coarse_ref[1, u : u + 1, at]
            rows = slice(u * FINE, (u + 1) * FINE)
            ref[rows, re * LANES : (re + 1) * LANES] = (cc * cf - sc * sf).astype(jnp.bfloat16)
            ref[rows, im * LANES : (im + 1) * LANES] = (sc * cf + cc * sf).astype(jnp.bfloat16)


def lag_bases(core, half, blocks):
    block_index = jnp.concatenate(
        [core * half + jnp.arange(half, dtype=jnp.int32), jnp.full((1,), blocks - 1, jnp.int32)]
    )
    bins = (K0 + block_index[:, None] * LANES + jnp.arange(LANES, dtype=jnp.int32)).reshape(-1)

    def base(lags):
        angles = (lags[:, None] * bins[None, :] % NFFT).astype(jnp.float32) * (2.0 * math.pi / NFFT)
        return jnp.stack([jnp.cos(angles), -jnp.sin(angles)])

    coarse = base(jnp.arange(LAGS // FINE, dtype=jnp.int32) * FINE - LAGS // 2)
    fine = base(jnp.arange(FINE, dtype=jnp.int32))
    return coarse, fine


def lag_table(coarse, fine):
    width = fine.shape[2]
    half = width // LANES - 1
    step = 8
    return pl.pallas_call(
        table_kernel,
        name="lagtable",
        grid=(LAGS // FINE // step,),
        out_shape=(
            jax.ShapeDtypeStruct((LAGS, 16 * LANES), jnp.bfloat16),
            jax.ShapeDtypeStruct((LAGS, 2 * (half + 1 - 8) * LANES), jnp.bfloat16),
        ),
        in_specs=[
            pl.BlockSpec((2, step, width), lambda u: (0, u, 0)),
            pl.BlockSpec((2, FINE, width), lambda u: (0, 0, 0)),
        ],
        out_specs=(
            pl.BlockSpec((step * FINE, 16 * LANES), lambda u: (u, 0)),
            pl.BlockSpec((step * FINE, 2 * (half + 1 - 8) * LANES), lambda u: (u, 0)),
        ),
        compiler_params=params(),
        cost_estimate=pl.CostEstimate(
            flops=LAGS * width * 6, bytes_accessed=LAGS * width * 4, transcendentals=0
        ),
    )(coarse, fine)


def dot_nt(a, b):
    return lax.dot_general(a, b, (((1,), (1,)), ((), ())), preferred_element_type=jnp.float32)


def scratch(bufs, pairs, each, *more):
    slots = sum(buf.shape[0] for buf in bufs)
    shapes = (
        ((slots,) + bufs[0].shape[1:], jnp.float32),
        ((pairs * each, LANES), jnp.float32),
    ) + more
    return dict(
        scratch_shapes=[pltpu.VMEM(*s) for s in shapes],
        compiler_params=params(*(size(*s) for s in shapes), roomy=len(bufs) == 1),
    )


def stack_cost(lags, depth, pairs):
    return pl.CostEstimate(
        flops=2 * lags * depth * pairs,
        bytes_accessed=2 * lags * depth + 4 * lags * pairs,
        transcendentals=0,
    )


def stack_small_kernel(count, tile, first_ref, second_ref, *refs):
    bufs = refs[:count]
    lag_ref, acc_ref, table, rows, cross = refs[count:]
    cross_small(first_ref, second_ref, bufs, table, rows, cross)
    for t in range(acc_ref.shape[0] // tile):
        at = slice(t * tile, (t + 1) * tile)
        acc_ref[at, :] = dot_nt(lag_ref[at, :], cross[...])


def stack_small(first, second, bufs, lag_table, tile):
    lags, depth = lag_table.shape
    pairs = first.shape[0]
    return pl.pallas_call(
        functools.partial(stack_small_kernel, len(bufs), tile),
        name="stack0",
        out_shape=jax.ShapeDtypeStruct((lags, pairs), jnp.float32),
        in_specs=[SMEM, SMEM] + [VMEM] * (len(bufs) + 1),
        out_specs=VMEM,
        cost_estimate=stack_cost(lags, depth, pairs),
        **scratch(bufs, pairs, SMALL_ROWS, ((pairs, depth), jnp.bfloat16)),
    )(first, second, *bufs, lag_table)


def finish(part, core, lag_ref, acc_ref, cross, send_ref, keep_ref):
    outer, tile, _ = send_ref.shape
    group_rows = lag_ref.shape[0] // (2 * outer)
    for mine in range(2):
        for at in range(outer):
            group = 2 * at + (core if mine else 1 - core)
            lags = pl.ds(pl.multiple_of(group * group_rows + part * tile, tile), tile)
            value = acc_ref[lags, :] + dot_nt(lag_ref[lags, :], cross[...])
            if mine:
                keep_ref[at] = value
            else:
                send_ref[at] = value.astype(send_ref.dtype)


def stack_outputs(acc, groups, parts):
    lags, pairs = acc.shape
    shape = (groups // 2, lags // groups // parts, pairs)
    return [jax.ShapeDtypeStruct(shape, jnp.bfloat16), jax.ShapeDtypeStruct(shape, jnp.float32)]


def stack_first_kernel(count, core_ref, first_ref, second_ref, *refs):
    bufs = refs[:count]
    lag_ref, acc_ref, send_ref, keep_ref, cross, table, rows = refs[count:]
    cross_big(first_ref, second_ref, bufs, table, rows, cross)
    finish(0, core_ref[0], lag_ref, acc_ref, cross, send_ref, keep_ref)


def stack_first(core, first, second, bufs, lag_table, acc, groups, parts):
    lags, depth = lag_table.shape
    pairs = acc.shape[1]
    return pl.pallas_call(
        functools.partial(stack_first_kernel, len(bufs)),
        name="stack1",
        in_specs=[SMEM] * 3 + [VMEM] * (len(bufs) + 2),
        out_specs=[VMEM] * 3,
        out_shape=stack_outputs(acc, groups, parts)
        + [jax.ShapeDtypeStruct((pairs, depth), jnp.bfloat16)],
        cost_estimate=stack_cost(lags // parts, depth, pairs),
        **scratch(bufs, pairs, BIG_ROWS),
    )(core, first, second, *bufs, lag_table, acc)


def stack_next_kernel(part, core_ref, lag_ref, acc_ref, cross, send_ref, keep_ref):
    finish(part, core_ref[0], lag_ref, acc_ref, cross, send_ref, keep_ref)


def stack_next(core, lag_table, acc, cross, groups, part, parts):
    lags, depth = lag_table.shape
    return pl.pallas_call(
        functools.partial(stack_next_kernel, part),
        name="stack2",
        in_specs=[SMEM] + [VMEM] * 3,
        out_specs=[VMEM] * 2,
        out_shape=stack_outputs(acc, groups, parts),
        compiler_params=params(),
        cost_estimate=stack_cost(lags // parts, depth, acc.shape[1]),
    )(core, lag_table, acc, cross)


def away_kernel(place_ref, keep_ref, near_ref, *outs):
    for d, out in enumerate(outs):
        at = place_ref[0] ^ (d + 1)
        out[...] = (keep_ref[at] + near_ref[at].astype(jnp.float32)).astype(out.dtype)


def sum_away(place, keep, near):
    outer, lags, pairs = keep.shape
    return pl.pallas_call(
        away_kernel,
        name="away",
        out_shape=[jax.ShapeDtypeStruct((lags, pairs), near.dtype)] * (outer - 1),
        in_specs=[SMEM, VMEM, VMEM],
        out_specs=[VMEM] * (outer - 1),
        compiler_params=params(2 * size(keep.shape, jnp.float32)),
        cost_estimate=pl.CostEstimate(
            flops=keep.size, bytes_accessed=6 * keep.size, transcendentals=0
        ),
    )(place, keep, near)


def result_kernel(scale, count, place_ref, *refs):
    keep, near, *far = refs[:count]
    place = place_ref[0]
    total = keep[place] + near[place].astype(jnp.float32)
    for ref in far:
        total = total + ref[...].astype(jnp.float32)
    refs[-1][...] = scale * total


def result(place, pieces, scale, part, parts, before):
    _, lags, pairs = pieces[0].shape
    specs = [pl.BlockSpec(x.shape, lambda i, n=x.ndim: (0,) * n) for x in pieces]
    operands = (place, *pieces)
    aliases = {}
    if before is not None:
        operands += (before,)
        specs.append(pl.BlockSpec(memory_space=pl.ANY))
        aliases = {len(operands) - 1: 0}
    return pl.pallas_call(
        functools.partial(result_kernel, scale, len(pieces)),
        name="result",
        grid=(1,),
        out_shape=jax.ShapeDtypeStruct((lags * parts, pairs), jnp.float32),
        in_specs=[SMEM] + specs,
        out_specs=pl.BlockSpec((lags, pairs), lambda i: (part, 0)),
        input_output_aliases=aliases,
        compiler_params=params(
            *(2 * size(x.shape, x.dtype) for x in pieces), 2 * size((lags, pairs), jnp.float32)
        ),
        cost_estimate=pl.CostEstimate(
            flops=lags * pairs * 4, bytes_accessed=lags * pairs * 16, transcendentals=0
        ),
    )(*operands)


def swap(x, axis, mask):
    return lax.ppermute(x, axis, [(i, i ^ mask) for i in range(lax.axis_size(axis))])


def swap_both(x, mask_pairs, mask_win):
    groups = lax.axis_size("win")
    perm = [
        (p * groups + w, (p ^ mask_pairs) * groups + (w ^ mask_win))
        for p in range(lax.axis_size("pairs"))
        for w in range(groups)
    ]
    return lax.ppermute(x, ("pairs", "win"), perm)


def after(x, *earlier):
    return lax.optimization_barrier((x,) + earlier)[0]


def local(spectra, requests, pair_first, pair_second):
    stations, windows, _, bins = spectra.shape
    sources = lax.axis_size("pairs")
    groups = lax.axis_size("win")
    cap = requests.shape[2]
    me = lax.axis_index("pairs").astype(jnp.int32)
    group = lax.axis_index("win").astype(jnp.int32)
    core = group & 1
    blocks = bins // LANES
    half = blocks // 2
    assert windows == 2 and blocks == 2 * half + 1 and half == 12 and groups % 2 == 0
    assert stations % 2 == 0

    keep_big, keep_small, give_big, give_small = whiten(core[None], spectra)
    near_big = swap(give_big, "win", 1)
    near_small = swap(give_small, "win", 1)

    slots = sources * cap
    wanted = jnp.maximum(requests[0], 0)
    if two_stage(sources):
        far = sources // 2
        chunks = {
            "small": [
                keep_small,
                near_small,
                swap(keep_small, "pairs", far),
                swap_both(give_small, far, 1),
            ],
            "big": [keep_big, near_big, swap(keep_big, "pairs", far), swap_both(give_big, far, 1)],
        }
        wanted = after(wanted, keep_small)
        asked = [wanted] + [swap(wanted, "pairs", d) for d in range(1, far)]
        arrived = {}
        for name, chunk in chunks.items():
            outs = select(me[None], asked, chunk, cap, name == "small")
            arrived[name] = [outs[0]] + [swap(outs[d], "pairs", d) for d in range(1, far)]
        small, big = arrived["small"], arrived["big"]
        core_table = core

        def row_of(slot):
            apart = (slot // cap) ^ me
            return (apart % far) * (2 * cap) + (apart // far) * cap + slot % cap

    else:
        asked_rows = lax.all_to_all(wanted, "pairs", split_axis=0, concat_axis=0, tiled=True)

        def exchange(chunk):
            outgoing = chunk[asked_rows]
            arrived = lax.all_to_all(outgoing, "pairs", split_axis=0, concat_axis=0, tiled=True)
            return [arrived.reshape((slots,) + chunk.shape[1:])]

        big = exchange(join(keep_big, near_big, False))
        small = exchange(join(keep_small, near_small, True))
        core_table = core

        def row_of(slot):
            return slot

    coarse, fine = lag_bases(core_table, half, blocks)
    table_big, table_small = lag_table(coarse, fine)
    first = row_of(pair_first)
    second = row_of(pair_second)
    acc = stack_small(first, second, small, table_small, LAGS // groups)

    place = (group >> 1)[None]
    parts = 2
    out = None
    norm_scale = 1.0 / math.sqrt(bins * windows * groups)
    send, keep, cross = stack_first(core[None], first, second, big, table_big, acc, groups, parts)
    for part in range(parts):
        if part > 0:
            send, keep = stack_next(core[None], table_big, acc, cross, groups, part, parts)
        near = swap(send, "win", 1)
        away = sum_away(place, keep, near)
        pieces = [keep, near] + [swap(x, "win", 2 * (d + 1)) for d, x in enumerate(away)]
        out = result(place, pieces, norm_scale, part, parts, out)
    return out


def two_stage(sources):
    return sources & (sources - 1) == 0 and 4 <= sources <= 16


def solution(mesh):
    step = jax.shard_map(
        local,
        mesh=mesh,
        in_specs=(P("pairs", "win", None, None), P("pairs", None, None), P("pairs"), P("pairs")),
        out_specs=P("win", "pairs"),
        check_vma=False,
    )
    sources = mesh.shape["pairs"]
    if not two_stage(sources):
        return step
    return step
```

```python
import functools
import math

import jax
import jax.numpy as jnp
from jax import lax
from jax.experimental import pallas as pl
from jax.experimental.pallas import tpu as pltpu
from jax.sharding import PartitionSpec as P


LAGS = 2048
NFFT = 18000
K0 = 360
LANES = 128
EPS = 1e-06
FINE = 32
VMEM = pl.BlockSpec(memory_space=pltpu.VMEM)
SMEM = pl.BlockSpec(memory_space=pltpu.SMEM)


def params(*nbytes, roomy=False):
    limit = 60 if roomy else sum(nbytes) // 1024**2 + 5
    return pltpu.CompilerParams(vmem_limit_bytes=limit * 1024**2)


def size(shape, dtype):
    return math.prod(shape) * jnp.dtype(dtype).itemsize


def whiten_kernel(core_ref, raw_ref, keep_ref, give_ref, tmp):
    stations, windows, _, bins = raw_ref.shape
    blocks = bins // LANES
    half = blocks // 2
    core = core_ref[0]

    def white(re, im):
        power = jnp.sum(re * re + im * im, axis=1, keepdims=True) * (1.0 / (2 * LANES))
        scale = lax.rsqrt(power + EPS)
        return re * scale, im * scale

    def station(s, slot):
        for w in range(windows):
            for b in range(blocks):
                value = raw_ref[s, w, :, b * LANES : (b + 1) * LANES]
                side, at = divmod(b, half)
                if side == 2:
                    row = 96 + w
                elif at < 8:
                    row = side * 48 + w * 16 + at
                else:
                    row = side * 48 + 32 + w * 4 + at - 8
                tmp[slot, pl.ds(row, 2, stride=8), :] = value
        for mine, out in ((True, keep_ref), (False, give_ref)):
            base = pl.multiple_of((core if mine else 1 - core) * 48, 16)
            for g in range(3):
                re = tmp[slot, pl.ds(base + g * 16, 8), :]
                im = tmp[slot, pl.ds(base + g * 16 + 8, 8), :]
                rows = jnp.concatenate(white(re, im), axis=0).astype(jnp.bfloat16)
                out[s, g * 16 : g * 16 + 16, :] = rows
        re, im = white(tmp[slot, 96:104, :], tmp[slot, 104:112, :])
        tmp[slot, 112:114, :] = re[0:windows]
        tmp[slot, 114:116, :] = im[0:windows]
        keep_ref[s, 48:56, :] = tmp[slot, 112:120, :].astype(jnp.bfloat16)

    tmp[...] = jnp.zeros_like(tmp)

    def several(i, carry):
        for slot in range(2):
            station(2 * i + slot, slot)
        return carry

    lax.fori_loop(0, stations // 2, several, 0)


def whiten(core, raw):
    stations = raw.shape[0]
    return pl.pallas_call(
        whiten_kernel,
        name="whiten",
        out_shape=tuple(jax.ShapeDtypeStruct((stations, r, LANES), jnp.bfloat16) for r in (56, 48)),
        in_specs=[SMEM, VMEM],
        out_specs=(VMEM,) * 2,
        scratch_shapes=[pltpu.VMEM((2, 120, LANES), jnp.float32)],
        compiler_params=params(size(raw.shape, raw.dtype)),
        cost_estimate=pl.CostEstimate(flops=2_000_000, bytes_accessed=2_000_000, transcendentals=0),
    )(core, raw)


BIG_PIECES = ((0, 0, 0, 32), (32, 1, 0, 32))
SMALL_PIECES = ((0, 0, 32, 16), (16, 1, 32, 16), (32, 0, 48, 8))
ALL_PIECES = BIG_PIECES + tuple(
    (64 + at, which, start, rows) for at, which, start, rows in SMALL_PIECES
)


def join(keep, got):
    return jnp.concatenate(
        [(keep, got)[which][:, start : start + rows] for _, which, start, rows in ALL_PIECES], axis=1
    )


def select_kernel(pieces, flip, cap, me_ref, *refs):
    peers = (len(refs) - 2) // 2
    asked = refs[:peers]
    chunk = refs[peers : peers + 2]
    source = me_ref[0] ^ flip
    for d, out in enumerate(refs[peers + 2 :]):
        for c in range(cap):
            row = asked[d][source, c]
            for at, which, start, rows in pieces:
                out[c, at : at + rows] = chunk[which][row, start : start + rows]


def select(me, asked, keep, got, flip, pieces):
    peers = len(asked)
    cap = asked[0].shape[1]
    rows = sum(piece[3] for piece in pieces)
    out = jax.ShapeDtypeStruct((cap, rows, LANES), keep.dtype)
    return pl.pallas_call(
        functools.partial(select_kernel, pieces, flip, cap),
        name="select",
        out_shape=(out,) * peers,
        in_specs=[SMEM] * (1 + peers) + [VMEM] * 2,
        out_specs=(VMEM,) * peers,
        compiler_params=params(),
        cost_estimate=pl.CostEstimate(flops=0, bytes_accessed=1_000_000, transcendentals=0),
    )(me, *asked, keep, got)


def load_table(bufs, table, lo):
    rows = table.shape[1]
    at = 0
    for buf in bufs:
        start = lo if buf.shape[1] > rows else 0

        def copy(i, carry, buf=buf, at=at, start=start):
            table[at + i] = buf[i, start : start + rows].astype(jnp.float32)
            return carry

        lax.fori_loop(0, buf.shape[0], copy, 0, unroll=4)
        at += buf.shape[0]


def products(table, i, j, groups):
    re = im = None
    for g in range(groups):
        ar = table[i, g * 16 : g * 16 + 8, :]
        ai = table[i, g * 16 + 8 : g * 16 + 16, :]
        br = table[j, g * 16 : g * 16 + 8, :]
        bi = table[j, g * 16 + 8 : g * 16 + 16, :]
        r = ar * br + ai * bi
        m = ai * br - ar * bi
        re = r if re is None else re + r
        im = m if im is None else im + m
    return re, im


BIG_ROWS = 17
SMALL_ROWS = 25


def cross_big(first_ref, second_ref, bufs, table, cross, out):
    pairs = out.shape[0]
    load_table(bufs, table, 0)

    def pair(p, carry):
        re, im = products(table, first_ref[p], second_ref[p], 4)
        cross[pl.ds(p * BIG_ROWS, 8), :] = re
        cross[pl.ds(p * BIG_ROWS + 8, 8), :] = im
        return carry

    lax.fori_loop(0, pairs, pair, 0, unroll=8)
    for k in range(16):
        out[:, k * LANES : (k + 1) * LANES] = cross[pl.ds(k, pairs, stride=BIG_ROWS), :].astype(
            jnp.bfloat16
        )


def cross_small(first_ref, second_ref, bufs, table, cross, out):
    pairs = out.shape[0]
    load_table(bufs, table, 64)

    def pair(p, carry):
        i = first_ref[p]
        j = second_ref[p]
        re, im = products(table, i, j, 2)
        at = p * SMALL_ROWS
        cross[pl.ds(at, 8), :] = re
        cross[pl.ds(at + 8, 8), :] = im
        a = table[i, 32:40, :]
        b = table[j, 32:40, :]
        cross[pl.ds(at + 16, 2), :] = a[0:2] * b[0:2] + a[2:4] * b[2:4]
        cross[pl.ds(at + 18, 2), :] = a[2:4] * b[0:2] - a[0:2] * b[2:4]
        return carry

    lax.fori_loop(0, pairs, pair, 0, unroll=8)

    def column(row):
        return cross[pl.ds(row, pairs, stride=SMALL_ROWS), :]

    for k in range(8):
        row = (k // 4) * 8 + k % 4
        out[:, k * LANES : (k + 1) * LANES] = (column(row) + column(row + 4)).astype(jnp.bfloat16)
    for k in range(2):
        row = 16 + 2 * k
        out[:, (8 + k) * LANES : (9 + k) * LANES] = (column(row) + column(row + 1)).astype(
            jnp.bfloat16
        )


def table_kernel(coarse_ref, fine_ref, big_ref, small_ref):
    half = fine_ref.shape[2] // LANES - 1
    for g in range(half + 1):
        at = slice(g * LANES, (g + 1) * LANES)
        cf = fine_ref[0, :, at]
        sf = fine_ref[1, :, at]
        if g < 8:
            ref, re, im = big_ref, g, g + 8
        elif g < half:
            ref, re, im = small_ref, g - 8, g - 8 + half - 8
        else:
            ref, re, im = small_ref, 2 * (half - 8), 2 * (half - 8) + 1
        for u in range(coarse_ref.shape[1]):
            cc = coarse_ref[0, u : u + 1, at]
            sc = coarse_ref[1, u : u + 1, at]
            rows = slice(u * FINE, (u + 1) * FINE)
            ref[rows, re * LANES : (re + 1) * LANES] = (cc * cf - sc * sf).astype(jnp.bfloat16)
            ref[rows, im * LANES : (im + 1) * LANES] = (sc * cf + cc * sf).astype(jnp.bfloat16)


def lag_bases(core, half, blocks):
    block_index = jnp.concatenate(
        [core * half + jnp.arange(half, dtype=jnp.int32), jnp.full((1,), blocks - 1, jnp.int32)]
    )
    bins = (K0 + block_index[:, None] * LANES + jnp.arange(LANES, dtype=jnp.int32)).reshape(-1)

    def base(lags):
        angles = (lags[:, None] * bins[None, :] % NFFT).astype(jnp.float32) * (2.0 * math.pi / NFFT)
        return jnp.stack([jnp.cos(angles), -jnp.sin(angles)])

    coarse = base(jnp.arange(LAGS // FINE, dtype=jnp.int32) * FINE - LAGS // 2)
    fine = base(jnp.arange(FINE, dtype=jnp.int32))
    return coarse, fine


def lag_table(coarse, fine):
    width = fine.shape[2]
    half = width // LANES - 1
    step = 8
    return pl.pallas_call(
        table_kernel,
        name="lagtable",
        grid=(LAGS // FINE // step,),
        out_shape=(
            jax.ShapeDtypeStruct((LAGS, 16 * LANES), jnp.bfloat16),
            jax.ShapeDtypeStruct((LAGS, 2 * (half + 1 - 8) * LANES), jnp.bfloat16),
        ),
        in_specs=[
            pl.BlockSpec((2, step, width), lambda u: (0, u, 0)),
            pl.BlockSpec((2, FINE, width), lambda u: (0, 0, 0)),
        ],
        out_specs=(
            pl.BlockSpec((step * FINE, 16 * LANES), lambda u: (u, 0)),
            pl.BlockSpec((step * FINE, 2 * (half + 1 - 8) * LANES), lambda u: (u, 0)),
        ),
        compiler_params=params(),
        cost_estimate=pl.CostEstimate(
            flops=LAGS * width * 6, bytes_accessed=LAGS * width * 4, transcendentals=0
        ),
    )(coarse, fine)


def dot_nt(a, b):
    return lax.dot_general(a, b, (((1,), (1,)), ((), ())), preferred_element_type=jnp.float32)


def scratch(chunk, bufs, pairs, *more):
    slots = sum(buf.shape[0] for buf in bufs)
    _, each, rows = CHUNKS[chunk]
    shapes = (
        ((slots, rows, LANES), jnp.float32),
        ((pairs * each, LANES), jnp.float32),
    ) + more
    return dict(
        scratch_shapes=[pltpu.VMEM(*s) for s in shapes],
        compiler_params=params(*(size(*s) for s in shapes), roomy=len(bufs) == 1),
    )


def stack_cost(lags, depth, pairs):
    return pl.CostEstimate(
        flops=2 * lags * depth * pairs,
        bytes_accessed=2 * lags * depth + 4 * lags * pairs,
        transcendentals=0,
    )


CHUNKS = {"big": (cross_big, BIG_ROWS, 64), "small": (cross_small, SMALL_ROWS, 40)}


def stack_all_kernel(chunk, count, tile, first_ref, second_ref, *refs):
    bufs = refs[:count]
    lag_ref, acc_ref, table, rows, cross = refs[count:]
    CHUNKS[chunk][0](first_ref, second_ref, bufs, table, rows, cross)
    for t in range(acc_ref.shape[0] // tile):
        at = slice(t * tile, (t + 1) * tile)
        acc_ref[at, :] = dot_nt(lag_ref[at, :], cross[...])


def stack_all(chunk, first, second, bufs, lag_table, tile):
    lags, depth = lag_table.shape
    pairs = first.shape[0]
    return pl.pallas_call(
        functools.partial(stack_all_kernel, chunk, len(bufs), tile),
        name="stack0",
        out_shape=jax.ShapeDtypeStruct((lags, pairs), jnp.float32),
        in_specs=[SMEM, SMEM] + [VMEM] * (len(bufs) + 1),
        out_specs=VMEM,
        cost_estimate=stack_cost(lags, depth, pairs),
        **scratch(chunk, bufs, pairs, ((pairs, depth), jnp.bfloat16)),
    )(first, second, *bufs, lag_table)


def finish(part, core, lag_ref, acc_ref, cross, send_ref, keep_ref):
    outer, tile, _ = send_ref.shape
    group_rows = lag_ref.shape[0] // (2 * outer)
    for mine in range(2):
        for at in range(outer):
            group = 2 * at + (core if mine else 1 - core)
            lags = pl.ds(pl.multiple_of(group * group_rows + part * tile, tile), tile)
            value = acc_ref[lags, :] + dot_nt(lag_ref[lags, :], cross[...])
            if mine:
                keep_ref[at] = value
            else:
                send_ref[at] = value.astype(send_ref.dtype)


def stack_outputs(acc, groups, parts):
    lags, pairs = acc.shape
    shape = (groups // 2, lags // groups // parts, pairs)
    return [jax.ShapeDtypeStruct(shape, jnp.bfloat16), jax.ShapeDtypeStruct(shape, jnp.float32)]


def stack_first_kernel(chunk, count, core_ref, first_ref, second_ref, *refs):
    bufs = refs[:count]
    lag_ref, acc_ref, send_ref, keep_ref, cross, table, rows = refs[count:]
    CHUNKS[chunk][0](first_ref, second_ref, bufs, table, rows, cross)
    finish(0, core_ref[0], lag_ref, acc_ref, cross, send_ref, keep_ref)


def stack_first(chunk, core, first, second, bufs, lag_table, acc, groups, parts):
    lags, depth = lag_table.shape
    pairs = acc.shape[1]
    return pl.pallas_call(
        functools.partial(stack_first_kernel, chunk, len(bufs)),
        name="stack1",
        in_specs=[SMEM] * 3 + [VMEM] * (len(bufs) + 2),
        out_specs=[VMEM] * 3,
        out_shape=stack_outputs(acc, groups, parts)
        + [jax.ShapeDtypeStruct((pairs, depth), jnp.bfloat16)],
        cost_estimate=stack_cost(lags // parts, depth, pairs),
        **scratch(chunk, bufs, pairs),
    )(core, first, second, *bufs, lag_table, acc)


def stack_next_kernel(part, core_ref, lag_ref, acc_ref, cross, send_ref, keep_ref):
    finish(part, core_ref[0], lag_ref, acc_ref, cross, send_ref, keep_ref)


def stack_next(core, lag_table, acc, cross, groups, part, parts):
    lags, depth = lag_table.shape
    return pl.pallas_call(
        functools.partial(stack_next_kernel, part),
        name="stack2",
        in_specs=[SMEM] + [VMEM] * 3,
        out_specs=[VMEM] * 2,
        out_shape=stack_outputs(acc, groups, parts),
        compiler_params=params(),
        cost_estimate=stack_cost(lags // parts, depth, acc.shape[1]),
    )(core, lag_table, acc, cross)


def away_kernel(place_ref, keep_ref, near_ref, *outs):
    for d, out in enumerate(outs):
        at = place_ref[0] ^ (d + 1)
        out[...] = (keep_ref[at] + near_ref[at].astype(jnp.float32)).astype(out.dtype)


def sum_away(place, keep, near):
    outer, lags, pairs = keep.shape
    return pl.pallas_call(
        away_kernel,
        name="away",
        out_shape=[jax.ShapeDtypeStruct((lags, pairs), near.dtype)] * (outer - 1),
        in_specs=[SMEM, VMEM, VMEM],
        out_specs=[VMEM] * (outer - 1),
        compiler_params=params(2 * size(keep.shape, jnp.float32)),
        cost_estimate=pl.CostEstimate(
            flops=keep.size, bytes_accessed=6 * keep.size, transcendentals=0
        ),
    )(place, keep, near)


def result_kernel(scale, count, place_ref, *refs):
    keep, near, *far = refs[:count]
    place = place_ref[0]
    total = keep[place] + near[place].astype(jnp.float32)
    for ref in far:
        total = total + ref[...].astype(jnp.float32)
    refs[-1][...] = scale * total


def result(place, pieces, scale, part, parts, before):
    _, lags, pairs = pieces[0].shape
    specs = [pl.BlockSpec(x.shape, lambda i, n=x.ndim: (0,) * n) for x in pieces]
    operands = (place, *pieces)
    aliases = {}
    if before is not None:
        operands += (before,)
        specs.append(pl.BlockSpec(memory_space=pl.ANY))
        aliases = {len(operands) - 1: 0}
    return pl.pallas_call(
        functools.partial(result_kernel, scale, len(pieces)),
        name="result",
        grid=(1,),
        out_shape=jax.ShapeDtypeStruct((lags * parts, pairs), jnp.float32),
        in_specs=[SMEM] + specs,
        out_specs=pl.BlockSpec((lags, pairs), lambda i: (part, 0)),
        input_output_aliases=aliases,
        compiler_params=params(
            *(2 * size(x.shape, x.dtype) for x in pieces), 2 * size((lags, pairs), jnp.float32)
        ),
        cost_estimate=pl.CostEstimate(
            flops=lags * pairs * 4, bytes_accessed=lags * pairs * 16, transcendentals=0
        ),
    )(*operands)


def swap(x, axis, mask):
    return lax.ppermute(x, axis, [(i, i ^ mask) for i in range(lax.axis_size(axis))])


def swap_both(x, mask_pairs, mask_win):
    groups = lax.axis_size("win")
    perm = [
        (p * groups + w, (p ^ mask_pairs) * groups + (w ^ mask_win))
        for p in range(lax.axis_size("pairs"))
        for w in range(groups)
    ]
    return lax.ppermute(x, ("pairs", "win"), perm)


def local(spectra, requests, pair_first, pair_second):
    stations, windows, _, bins = spectra.shape
    sources = lax.axis_size("pairs")
    groups = lax.axis_size("win")
    cap = requests.shape[2]
    me = lax.axis_index("pairs").astype(jnp.int32)
    group = lax.axis_index("win").astype(jnp.int32)
    core = group & 1
    blocks = bins // LANES
    half = blocks // 2
    assert windows == 2 and blocks == 2 * half + 1 and half == 12 and groups % 2 == 0
    assert stations % 2 == 0

    keep, give = whiten(core[None], spectra)
    near = swap(give, "win", 1)

    wanted = jnp.maximum(requests[0], 0)
    if two_stage(sources):
        far = sources // 2
        asked = [wanted] + [swap(wanted, "pairs", d) for d in range(1, far)]
        far_keep = swap(keep, "pairs", far)
        far_give = swap_both(give, far, 1)

        def to_half(outs):
            return [outs[0]] + [swap(outs[d], "pairs", d) for d in range(1, far)]

        own = select(me[None], asked, keep, near, 0, ALL_PIECES)
        own = to_half(own)
        big = select(me[None], asked, far_keep, far_give, far, BIG_PIECES)
        big = own + to_half(big)
        small = select(me[None], asked, far_keep, far_give, far, SMALL_PIECES)
        small = own + to_half(small)

        def row_of(slot):
            return ((slot // cap) ^ me) * cap + slot % cap

    else:
        asked_rows = lax.all_to_all(wanted, "pairs", split_axis=0, concat_axis=0, tiled=True)
        outgoing = join(keep, near)[asked_rows]
        arrived = lax.all_to_all(outgoing, "pairs", split_axis=0, concat_axis=0, tiled=True)
        big = small = [arrived.reshape((sources * cap,) + outgoing.shape[2:])]

        def row_of(slot):
            return slot

    coarse, fine = lag_bases(core, half, blocks)
    table_big, table_small = lag_table(coarse, fine)
    first = row_of(pair_first)
    second = row_of(pair_second)
    acc = stack_all("big", first, second, big, table_big, LAGS // groups)

    place = (group >> 1)[None]
    parts = 2
    out = None
    norm_scale = 1.0 / math.sqrt(bins * windows * groups)
    send, kept, cross = stack_first(
        "small", core[None], first, second, small, table_small, acc, groups, parts
    )
    for part in range(parts):
        if part > 0:
            send, kept = stack_next(core[None], table_small, acc, cross, groups, part, parts)
        summed = swap(send, "win", 1)
        away = sum_away(place, kept, summed)
        pieces = [kept, summed] + [swap(x, "win", 2 * (d + 1)) for d, x in enumerate(away)]
        out = result(place, pieces, norm_scale, part, parts, out)
    return out


def two_stage(sources):
    return sources & (sources - 1) == 0 and 4 <= sources <= 16


def solution(mesh):
    step = jax.shard_map(
        local,
        mesh=mesh,
        in_specs=(P("pairs", "win", None, None), P("pairs", None, None), P("pairs"), P("pairs")),
        out_specs=P("win", "pairs"),
        check_vma=False,
    )
    sources = mesh.shape["pairs"]
    if not two_stage(sources):
        return step
    return step
```

```python
import functools
import math

import jax
import jax.numpy as jnp
from jax import lax
from jax.experimental import pallas as pl
from jax.experimental.pallas import tpu as pltpu
from jax.sharding import PartitionSpec as P


LAGS = 2048
NFFT = 18000
K0 = 360
LANES = 128
EPS = 1e-06
FINE = 32
VMEM = pl.BlockSpec(memory_space=pltpu.VMEM)
SMEM = pl.BlockSpec(memory_space=pltpu.SMEM)


def params(*nbytes, roomy=False):
    limit = 60 if roomy else sum(nbytes) // 1024**2 + 5
    return pltpu.CompilerParams(vmem_limit_bytes=limit * 1024**2)


def size(shape, dtype):
    return math.prod(shape) * jnp.dtype(dtype).itemsize


def white(re, im):
    power = jnp.sum(re * re + im * im, axis=1, keepdims=True) * (1.0 / (2 * LANES))
    scale = lax.rsqrt(power + EPS)
    return re * scale, im * scale


def white_rows(tmp, slot, at):
    re = tmp[slot, pl.ds(at, 8), :]
    im = tmp[slot, pl.ds(at + 8, 8), :]
    return jnp.concatenate(white(re, im), axis=0).astype(jnp.bfloat16)


def gather_rows(raw_ref, tmp, s, slot, w, b, row):
    tmp[slot, pl.ds(row, 2, stride=8), :] = raw_ref[s, w, :, b * LANES : (b + 1) * LANES]


def by_twos(stations, station):
    def several(i, carry):
        for slot in range(2):
            station(2 * i + slot, slot)
        return carry

    lax.fori_loop(0, stations // 2, several, 0)


def whiten_big_kernel(core_ref, raw_ref, keep_ref, give_ref, tmp):
    stations, windows, _, bins = raw_ref.shape
    half = bins // LANES // 2
    core = core_ref[0]

    def station(s, slot):
        for w in range(windows):
            for side in range(2):
                for at in range(8):
                    gather_rows(raw_ref, tmp, s, slot, w, side * half + at, side * 32 + w * 16 + at)
        for side, out in ((core, keep_ref), (1 - core, give_ref)):
            base = pl.multiple_of(side * 32, 16)
            for w in range(windows):
                out[s, w * 16 : w * 16 + 16, :] = white_rows(tmp, slot, base + w * 16)

    by_twos(stations, station)


def whiten_small_kernel(core_ref, raw_ref, keep_ref, give_ref, tmp):
    stations, windows, _, bins = raw_ref.shape
    half = bins // LANES // 2
    core = core_ref[0]

    def station(s, slot):
        for w in range(windows):
            for side in range(2):
                for at in range(8, half):
                    gather_rows(raw_ref, tmp, s, slot, w, side * half + at, side * 16 + w * 4 + at - 8)
            gather_rows(raw_ref, tmp, s, slot, w, 2 * half, 32 + w)
        keep_ref[s, 0:16, :] = white_rows(tmp, slot, pl.multiple_of(core * 16, 16))
        give_ref[s, 0:16, :] = white_rows(tmp, slot, pl.multiple_of((1 - core) * 16, 16))
        re, im = white(tmp[slot, 32:40, :], tmp[slot, 40:48, :])
        tmp[slot, 48:50, :] = re[0:windows]
        tmp[slot, 50:52, :] = im[0:windows]
        keep_ref[s, 16:24, :] = tmp[slot, 48:56, :].astype(jnp.bfloat16)

    tmp[...] = jnp.zeros_like(tmp)
    by_twos(stations, station)


def whiten(kernel, rows, core, raw):
    stations = raw.shape[0]
    return pl.pallas_call(
        kernel,
        out_shape=tuple(jax.ShapeDtypeStruct((stations, r, LANES), jnp.bfloat16) for r in rows),
        in_specs=[SMEM, VMEM],
        out_specs=(VMEM,) * 2,
        scratch_shapes=[pltpu.VMEM((2, 64, LANES), jnp.float32)],
        compiler_params=params(size(raw.shape, raw.dtype)),
        cost_estimate=pl.CostEstimate(flops=2_000_000, bytes_accessed=2_000_000, transcendentals=0),
    )(core, raw)


def join(keep, got, small):
    if small:
        return jnp.concatenate([keep[:, :16], got, keep[:, 16:]], axis=1)
    return jnp.concatenate([keep, got], axis=1)


def select_kernel(peers, stages, sources, cap, small, me_ref, *refs):
    asked = refs[:peers]
    chunks = refs[peers : peers + 2 * stages]
    outs = refs[peers + 2 * stages :]
    me = me_ref[0]
    for d in range(peers):
        for h in range(stages):
            source = me ^ (h * (sources // 2))
            keep, got = chunks[2 * h : 2 * h + 2]
            for c in range(cap):
                row = asked[d][source, c]
                out = outs[d].at[h * cap + c]
                if small:
                    out[0:16] = keep[row, 0:16]
                    out[16:32] = got[row]
                    out[32:40] = keep[row, 16:24]
                else:
                    out[0:32] = keep[row]
                    out[32:64] = got[row]


def select(me, asked, chunks, cap, small):
    peers = len(asked)
    stages = len(chunks) // 2
    sources = asked[0].shape[0]
    rows = chunks[0].shape[1] + chunks[1].shape[1]
    out = jax.ShapeDtypeStruct((stages * cap, rows, LANES), chunks[0].dtype)
    return pl.pallas_call(
        functools.partial(select_kernel, peers, stages, sources, cap, small),
        name="select",
        out_shape=(out,) * peers,
        in_specs=[SMEM] * (1 + peers) + [VMEM] * len(chunks),
        out_specs=(VMEM,) * peers,
        compiler_params=params(2 * (peers + 2) * size(out.shape, out.dtype)),
        cost_estimate=pl.CostEstimate(flops=0, bytes_accessed=1_000_000, transcendentals=0),
    )(me, *asked, *chunks)


def load_table(bufs, table):
    at = 0
    for buf in bufs:

        def copy(i, carry, buf=buf, at=at):
            table[at + i] = buf[i].astype(jnp.float32)
            return carry

        lax.fori_loop(0, buf.shape[0], copy, 0, unroll=4)
        at += buf.shape[0]


def products(table, i, j, groups):
    re = im = None
    for g in range(groups):
        ar = table[i, g * 16 : g * 16 + 8, :]
        ai = table[i, g * 16 + 8 : g * 16 + 16, :]
        br = table[j, g * 16 : g * 16 + 8, :]
        bi = table[j, g * 16 + 8 : g * 16 + 16, :]
        r = ar * br + ai * bi
        m = ai * br - ar * bi
        re = r if re is None else re + r
        im = m if im is None else im + m
    return re, im


BIG_ROWS = 17
SMALL_ROWS = 25


def cross_big(first_ref, second_ref, bufs, table, cross, out):
    pairs = out.shape[0]
    load_table(bufs, table)

    def pair(p, carry):
        re, im = products(table, first_ref[p], second_ref[p], 4)
        cross[pl.ds(p * BIG_ROWS, 8), :] = re
        cross[pl.ds(p * BIG_ROWS + 8, 8), :] = im
        return carry

    lax.fori_loop(0, pairs, pair, 0, unroll=8)
    for k in range(16):
        out[:, k * LANES : (k + 1) * LANES] = cross[pl.ds(k, pairs, stride=BIG_ROWS), :].astype(
            jnp.bfloat16
        )


def cross_small(first_ref, second_ref, bufs, table, cross, out):
    pairs = out.shape[0]
    load_table(bufs, table)

    def pair(p, carry):
        i = first_ref[p]
        j = second_ref[p]
        re, im = products(table, i, j, 2)
        at = p * SMALL_ROWS
        cross[pl.ds(at, 8), :] = re
        cross[pl.ds(at + 8, 8), :] = im
        a = table[i, 32:40, :]
        b = table[j, 32:40, :]
        cross[pl.ds(at + 16, 2), :] = a[0:2] * b[0:2] + a[2:4] * b[2:4]
        cross[pl.ds(at + 18, 2), :] = a[2:4] * b[0:2] - a[0:2] * b[2:4]
        return carry

    lax.fori_loop(0, pairs, pair, 0, unroll=8)

    def column(row):
        return cross[pl.ds(row, pairs, stride=SMALL_ROWS), :]

    for k in range(8):
        row = (k // 4) * 8 + k % 4
        out[:, k * LANES : (k + 1) * LANES] = (column(row) + column(row + 4)).astype(jnp.bfloat16)
    for k in range(2):
        row = 16 + 2 * k
        out[:, (8 + k) * LANES : (9 + k) * LANES] = (column(row) + column(row + 1)).astype(
            jnp.bfloat16
        )


def table_kernel(coarse_ref, fine_ref, big_ref, small_ref):
    half = fine_ref.shape[2] // LANES - 1
    for g in range(half + 1):
        at = slice(g * LANES, (g + 1) * LANES)
        cf = fine_ref[0, :, at]
        sf = fine_ref[1, :, at]
        if g < 8:
            ref, re, im = big_ref, g, g + 8
        elif g < half:
            ref, re, im = small_ref, g - 8, g - 8 + half - 8
        else:
            ref, re, im = small_ref, 2 * (half - 8), 2 * (half - 8) + 1
        for u in range(coarse_ref.shape[1]):
            cc = coarse_ref[0, u : u + 1, at]
            sc = coarse_ref[1, u : u + 1, at]
            rows = slice(u * FINE, (u + 1) * FINE)
            ref[rows, re * LANES : (re + 1) * LANES] = (cc * cf - sc * sf).astype(jnp.bfloat16)
            ref[rows, im * LANES : (im + 1) * LANES] = (sc * cf + cc * sf).astype(jnp.bfloat16)


def lag_bases(core, half, blocks):
    block_index = jnp.concatenate(
        [core * half + jnp.arange(half, dtype=jnp.int32), jnp.full((1,), blocks - 1, jnp.int32)]
    )
    bins = (K0 + block_index[:, None] * LANES + jnp.arange(LANES, dtype=jnp.int32)).reshape(-1)

    def base(lags):
        angles = (lags[:, None] * bins[None, :] % NFFT).astype(jnp.float32) * (2.0 * math.pi / NFFT)
        return jnp.stack([jnp.cos(angles), -jnp.sin(angles)])

    coarse = base(jnp.arange(LAGS // FINE, dtype=jnp.int32) * FINE - LAGS // 2)
    fine = base(jnp.arange(FINE, dtype=jnp.int32))
    return coarse, fine


def lag_table(coarse, fine):
    width = fine.shape[2]
    half = width // LANES - 1
    step = 8
    return pl.pallas_call(
        table_kernel,
        name="lagtable",
        grid=(LAGS // FINE // step,),
        out_shape=(
            jax.ShapeDtypeStruct((LAGS, 16 * LANES), jnp.bfloat16),
            jax.ShapeDtypeStruct((LAGS, 2 * (half + 1 - 8) * LANES), jnp.bfloat16),
        ),
        in_specs=[
            pl.BlockSpec((2, step, width), lambda u: (0, u, 0)),
            pl.BlockSpec((2, FINE, width), lambda u: (0, 0, 0)),
        ],
        out_specs=(
            pl.BlockSpec((step * FINE, 16 * LANES), lambda u: (u, 0)),
            pl.BlockSpec((step * FINE, 2 * (half + 1 - 8) * LANES), lambda u: (u, 0)),
        ),
        compiler_params=params(),
        cost_estimate=pl.CostEstimate(
            flops=LAGS * width * 6, bytes_accessed=LAGS * width * 4, transcendentals=0
        ),
    )(coarse, fine)


def dot_nt(a, b):
    return lax.dot_general(a, b, (((1,), (1,)), ((), ())), preferred_element_type=jnp.float32)


def scratch(bufs, pairs, each, *more):
    slots = sum(buf.shape[0] for buf in bufs)
    shapes = (
        ((slots,) + bufs[0].shape[1:], jnp.float32),
        ((pairs * each, LANES), jnp.float32),
    ) + more
    return dict(
        scratch_shapes=[pltpu.VMEM(*s) for s in shapes],
        compiler_params=params(*(size(*s) for s in shapes), roomy=len(bufs) == 1),
    )


def stack_cost(lags, depth, pairs):
    return pl.CostEstimate(
        flops=2 * lags * depth * pairs,
        bytes_accessed=2 * lags * depth + 4 * lags * pairs,
        transcendentals=0,
    )


def stack_small_kernel(count, tile, first_ref, second_ref, *refs):
    bufs = refs[:count]
    lag_ref, acc_ref, table, rows, cross = refs[count:]
    cross_small(first_ref, second_ref, bufs, table, rows, cross)
    for t in range(acc_ref.shape[0] // tile):
        at = slice(t * tile, (t + 1) * tile)
        acc_ref[at, :] = dot_nt(lag_ref[at, :], cross[...])


def stack_small(first, second, bufs, lag_table, tile):
    lags, depth = lag_table.shape
    pairs = first.shape[0]
    return pl.pallas_call(
        functools.partial(stack_small_kernel, len(bufs), tile),
        name="stack0",
        out_shape=jax.ShapeDtypeStruct((lags, pairs), jnp.float32),
        in_specs=[SMEM, SMEM] + [VMEM] * (len(bufs) + 1),
        out_specs=VMEM,
        cost_estimate=stack_cost(lags, depth, pairs),
        **scratch(bufs, pairs, SMALL_ROWS, ((pairs, depth), jnp.bfloat16)),
    )(first, second, *bufs, lag_table)


def finish(part, core, lag_ref, acc_ref, cross, send_ref, keep_ref):
    outer, tile, _ = send_ref.shape
    group_rows = lag_ref.shape[0] // (2 * outer)
    for mine in range(2):
        for at in range(outer):
            group = 2 * at + (core if mine else 1 - core)
            lags = pl.ds(pl.multiple_of(group * group_rows + part * tile, tile), tile)
            value = acc_ref[lags, :] + dot_nt(lag_ref[lags, :], cross[...])
            if mine:
                keep_ref[at] = value
            else:
                send_ref[at] = value.astype(send_ref.dtype)


def stack_outputs(acc, groups, parts):
    lags, pairs = acc.shape
    shape = (groups // 2, lags // groups // parts, pairs)
    return [jax.ShapeDtypeStruct(shape, jnp.bfloat16), jax.ShapeDtypeStruct(shape, jnp.float32)]


def stack_first_kernel(count, core_ref, first_ref, second_ref, *refs):
    bufs = refs[:count]
    lag_ref, acc_ref, send_ref, keep_ref, cross, table, rows = refs[count:]
    cross_big(first_ref, second_ref, bufs, table, rows, cross)
    finish(0, core_ref[0], lag_ref, acc_ref, cross, send_ref, keep_ref)


def stack_first(core, first, second, bufs, lag_table, acc, groups, parts):
    lags, depth = lag_table.shape
    pairs = acc.shape[1]
    return pl.pallas_call(
        functools.partial(stack_first_kernel, len(bufs)),
        name="stack1",
        in_specs=[SMEM] * 3 + [VMEM] * (len(bufs) + 2),
        out_specs=[VMEM] * 3,
        out_shape=stack_outputs(acc, groups, parts)
        + [jax.ShapeDtypeStruct((pairs, depth), jnp.bfloat16)],
        cost_estimate=stack_cost(lags // parts, depth, pairs),
        **scratch(bufs, pairs, BIG_ROWS),
    )(core, first, second, *bufs, lag_table, acc)


def stack_next_kernel(part, core_ref, lag_ref, acc_ref, cross, send_ref, keep_ref):
    finish(part, core_ref[0], lag_ref, acc_ref, cross, send_ref, keep_ref)


def stack_next(core, lag_table, acc, cross, groups, part, parts):
    lags, depth = lag_table.shape
    return pl.pallas_call(
        functools.partial(stack_next_kernel, part),
        name="stack2",
        in_specs=[SMEM] + [VMEM] * 3,
        out_specs=[VMEM] * 2,
        out_shape=stack_outputs(acc, groups, parts),
        compiler_params=params(),
        cost_estimate=stack_cost(lags // parts, depth, acc.shape[1]),
    )(core, lag_table, acc, cross)


def away_kernel(place_ref, keep_ref, near_ref, *outs):
    for d, out in enumerate(outs):
        at = place_ref[0] ^ (d + 1)
        out[...] = (keep_ref[at] + near_ref[at].astype(jnp.float32)).astype(out.dtype)


def sum_away(place, keep, near):
    outer, lags, pairs = keep.shape
    return pl.pallas_call(
        away_kernel,
        name="away",
        out_shape=[jax.ShapeDtypeStruct((lags, pairs), near.dtype)] * (outer - 1),
        in_specs=[SMEM, VMEM, VMEM],
        out_specs=[VMEM] * (outer - 1),
        compiler_params=params(2 * size(keep.shape, jnp.float32)),
        cost_estimate=pl.CostEstimate(
            flops=keep.size, bytes_accessed=6 * keep.size, transcendentals=0
        ),
    )(place, keep, near)


def result_kernel(scale, count, place_ref, *refs):
    keep, near, *far = refs[:count]
    place = place_ref[0]
    total = keep[place] + near[place].astype(jnp.float32)
    for ref in far:
        total = total + ref[...].astype(jnp.float32)
    refs[-1][...] = scale * total


def result(place, pieces, scale, part, parts, before):
    _, lags, pairs = pieces[0].shape
    specs = [pl.BlockSpec(x.shape, lambda i, n=x.ndim: (0,) * n) for x in pieces]
    operands = (place, *pieces)
    aliases = {}
    if before is not None:
        operands += (before,)
        specs.append(pl.BlockSpec(memory_space=pl.ANY))
        aliases = {len(operands) - 1: 0}
    return pl.pallas_call(
        functools.partial(result_kernel, scale, len(pieces)),
        name="result",
        grid=(1,),
        out_shape=jax.ShapeDtypeStruct((lags * parts, pairs), jnp.float32),
        in_specs=[SMEM] + specs,
        out_specs=pl.BlockSpec((lags, pairs), lambda i: (part, 0)),
        input_output_aliases=aliases,
        compiler_params=params(
            *(2 * size(x.shape, x.dtype) for x in pieces), 2 * size((lags, pairs), jnp.float32)
        ),
        cost_estimate=pl.CostEstimate(
            flops=lags * pairs * 4, bytes_accessed=lags * pairs * 16, transcendentals=0
        ),
    )(*operands)


def swap(x, axis, mask):
    return lax.ppermute(x, axis, [(i, i ^ mask) for i in range(lax.axis_size(axis))])


def swap_both(x, mask_pairs, mask_win):
    groups = lax.axis_size("win")
    perm = [
        (p * groups + w, (p ^ mask_pairs) * groups + (w ^ mask_win))
        for p in range(lax.axis_size("pairs"))
        for w in range(groups)
    ]
    return lax.ppermute(x, ("pairs", "win"), perm)


def after(x, *earlier):
    return lax.optimization_barrier((x,) + earlier)[0]


def local(spectra, requests, pair_first, pair_second):
    stations, windows, _, bins = spectra.shape
    sources = lax.axis_size("pairs")
    groups = lax.axis_size("win")
    cap = requests.shape[2]
    me = lax.axis_index("pairs").astype(jnp.int32)
    group = lax.axis_index("win").astype(jnp.int32)
    core = group & 1
    blocks = bins // LANES
    half = blocks // 2
    assert windows == 2 and blocks == 2 * half + 1 and half == 12 and groups % 2 == 0
    assert stations % 2 == 0

    keep_small, give_small = whiten(whiten_small_kernel, (24, 16), core[None], spectra)
    keep_big, give_big = whiten(whiten_big_kernel, (32, 32), core[None], spectra)
    near_big = swap(give_big, "win", 1)
    near_small = swap(give_small, "win", 1)

    slots = sources * cap
    wanted = jnp.maximum(requests[0], 0)
    if two_stage(sources):
        far = sources // 2
        chunks = {
            "small": [
                keep_small,
                near_small,
                swap(keep_small, "pairs", far),
                swap_both(give_small, far, 1),
            ],
            "big": [keep_big, near_big, swap(keep_big, "pairs", far), swap_both(give_big, far, 1)],
        }
        wanted = after(wanted, keep_small)
        asked = [wanted] + [swap(wanted, "pairs", d) for d in range(1, far)]
        arrived = {}
        for name, chunk in chunks.items():
            outs = select(me[None], asked, chunk, cap, name == "small")
            arrived[name] = [outs[0]] + [swap(outs[d], "pairs", d) for d in range(1, far)]
        small, big = arrived["small"], arrived["big"]
        core_table = core

        def row_of(slot):
            apart = (slot // cap) ^ me
            return (apart % far) * (2 * cap) + (apart // far) * cap + slot % cap

    else:
        asked_rows = lax.all_to_all(wanted, "pairs", split_axis=0, concat_axis=0, tiled=True)

        def exchange(chunk):
            outgoing = chunk[asked_rows]
            arrived = lax.all_to_all(outgoing, "pairs", split_axis=0, concat_axis=0, tiled=True)
            return [arrived.reshape((slots,) + chunk.shape[1:])]

        big = exchange(join(keep_big, near_big, False))
        small = exchange(join(keep_small, near_small, True))
        core_table = core

        def row_of(slot):
            return slot

    coarse, fine = lag_bases(core_table, half, blocks)
    table_big, table_small = lag_table(coarse, fine)
    first = row_of(pair_first)
    second = row_of(pair_second)
    acc = stack_small(first, second, small, table_small, LAGS // groups)

    place = (group >> 1)[None]
    parts = 2
    out = None
    norm_scale = 1.0 / math.sqrt(bins * windows * groups)
    send, keep, cross = stack_first(core[None], first, second, big, table_big, acc, groups, parts)
    for part in range(parts):
        if part > 0:
            send, keep = stack_next(core[None], table_big, acc, cross, groups, part, parts)
        near = swap(send, "win", 1)
        away = sum_away(place, keep, near)
        pieces = [keep, near] + [swap(x, "win", 2 * (d + 1)) for d, x in enumerate(away)]
        out = result(place, pieces, norm_scale, part, parts, out)
    return out


def two_stage(sources):
    return sources & (sources - 1) == 0 and 4 <= sources <= 16


def solution(mesh):
    step = jax.shard_map(
        local,
        mesh=mesh,
        in_specs=(P("pairs", "win", None, None), P("pairs", None, None), P("pairs"), P("pairs")),
        out_specs=P("win", "pairs"),
        check_vma=False,
    )
    sources = mesh.shape["pairs"]
    if not two_stage(sources):
        return step
    return step
```

```python
import functools
import math

import jax
import jax.numpy as jnp
from jax import lax
from jax.experimental import pallas as pl
from jax.experimental.pallas import tpu as pltpu
from jax.sharding import PartitionSpec as P


LAGS = 2048
NFFT = 18000
K0 = 360
LANES = 128
EPS = 1e-06
FINE = 32
VMEM = pl.BlockSpec(memory_space=pltpu.VMEM)
SMEM = pl.BlockSpec(memory_space=pltpu.SMEM)


def params(*nbytes, roomy=False):
    limit = 60 if roomy else sum(nbytes) // 1024**2 + 5
    return pltpu.CompilerParams(vmem_limit_bytes=limit * 1024**2)


def size(shape, dtype):
    return math.prod(shape) * jnp.dtype(dtype).itemsize


def whiten_kernel(core_ref, raw_ref, keep_big, keep_small, give_big, give_small, tmp):
    stations, windows, _, bins = raw_ref.shape
    blocks = bins // LANES
    half = blocks // 2
    core = core_ref[0]

    def white(re, im):
        power = jnp.sum(re * re + im * im, axis=1, keepdims=True) * (1.0 / (2 * LANES))
        scale = lax.rsqrt(power + EPS)
        return re * scale, im * scale

    def station(s, slot):
        for w in range(windows):
            for b in range(blocks):
                value = raw_ref[s, w, :, b * LANES : (b + 1) * LANES]
                side, at = divmod(b, half)
                if side == 2:
                    row = 96 + w
                elif at < 8:
                    row = side * 48 + w * 16 + at
                else:
                    row = side * 48 + 32 + w * 4 + at - 8
                tmp[slot, pl.ds(row, 2, stride=8), :] = value
        for mine, big, small in ((True, keep_big, keep_small), (False, give_big, give_small)):
            base = pl.multiple_of((core if mine else 1 - core) * 48, 16)
            for g in range(3):
                re = tmp[slot, pl.ds(base + g * 16, 8), :]
                im = tmp[slot, pl.ds(base + g * 16 + 8, 8), :]
                rows = jnp.concatenate(white(re, im), axis=0).astype(jnp.bfloat16)
                if g < 2:
                    big[s, g * 16 : g * 16 + 16, :] = rows
                else:
                    small[s, 0:16, :] = rows
        re, im = white(tmp[slot, 96:104, :], tmp[slot, 104:112, :])
        tmp[slot, 112:114, :] = re[0:windows]
        tmp[slot, 114:116, :] = im[0:windows]
        keep_small[s, 16:24, :] = tmp[slot, 112:120, :].astype(jnp.bfloat16)

    tmp[...] = jnp.zeros_like(tmp)

    def several(i, carry):
        for slot in range(2):
            station(2 * i + slot, slot)
        return carry

    lax.fori_loop(0, stations // 2, several, 0)


def whiten(core, raw):
    stations = raw.shape[0]
    rows = (32, 24, 32, 16)
    return pl.pallas_call(
        whiten_kernel,
        name="whiten",
        out_shape=tuple(jax.ShapeDtypeStruct((stations, r, LANES), jnp.bfloat16) for r in rows),
        in_specs=[SMEM, VMEM],
        out_specs=(VMEM,) * 4,
        scratch_shapes=[pltpu.VMEM((2, 120, LANES), jnp.float32)],
        compiler_params=params(size(raw.shape, raw.dtype)),
        cost_estimate=pl.CostEstimate(flops=2_000_000, bytes_accessed=2_000_000, transcendentals=0),
    )(core, raw)


def join(keep, got, small):
    if small:
        return jnp.concatenate([keep[:, :16], got, keep[:, 16:]], axis=1)
    return jnp.concatenate([keep, got], axis=1)


def copy_row(out, at, keep, got, row, small):
    if small:
        out[at : at + 16] = keep[row, 0:16]
        out[at + 16 : at + 32] = got[row]
        out[at + 32 : at + 40] = keep[row, 16:24]
    else:
        out[at : at + 32] = keep[row]
        out[at + 32 : at + 64] = got[row]


def select_kernel(sources, cap, small, early, me_ref, *refs):
    peers = (len(refs) - 4) // 2
    asked = refs[:peers]
    chunks = refs[peers : peers + 4]
    me = me_ref[0]
    for d, out in enumerate(refs[peers + 4 :]):
        for h in range(1 if d in early else 0, 2):
            source = me ^ (h * (sources // 2))
            keep, got = chunks[2 * h : 2 * h + 2]
            for c in range(cap):
                at = c if d in early else h * cap + c
                copy_row(out.at[at], 0, keep, got, asked[d][source, c], small)


def select(me, asked, chunks, cap, small, early):
    sources = asked[0].shape[0]
    rows = chunks[0].shape[1] + chunks[1].shape[1]
    outs = [
        jax.ShapeDtypeStruct(((1 if d in early else 2) * cap, rows, LANES), chunks[0].dtype)
        for d in range(len(asked))
    ]
    return pl.pallas_call(
        functools.partial(select_kernel, sources, cap, small, early),
        name="select",
        out_shape=outs,
        in_specs=[SMEM] * (1 + len(asked)) + [VMEM] * 4,
        out_specs=[VMEM] * len(asked),
        compiler_params=params(),
        cost_estimate=pl.CostEstimate(flops=0, bytes_accessed=1_000_000, transcendentals=0),
    )(me, *asked, *chunks)


def early_kernel(me_ref, asked, keep_big, got_big, keep_small, got_small, out):
    for c in range(out.shape[0]):
        row = asked[me_ref[0], c]
        copy_row(out.at[c], 0, keep_big, got_big, row, False)
        copy_row(out.at[c], 64, keep_small, got_small, row, True)


def select_early(me, asked, keep_big, got_big, keep_small, got_small):
    return pl.pallas_call(
        early_kernel,
        name="selectearly",
        out_shape=jax.ShapeDtypeStruct((asked.shape[1], 104, LANES), keep_big.dtype),
        in_specs=[SMEM] * 2 + [VMEM] * 4,
        out_specs=VMEM,
        compiler_params=params(),
        cost_estimate=pl.CostEstimate(flops=0, bytes_accessed=500_000, transcendentals=0),
    )(me, asked, keep_big, got_big, keep_small, got_small)


def load_table(bufs, table, lo):
    rows = table.shape[1]
    at = 0
    for buf in bufs:
        start = lo if buf.shape[1] > rows else 0

        def copy(i, carry, buf=buf, at=at, start=start):
            table[at + i] = buf[i, start : start + rows].astype(jnp.float32)
            return carry

        lax.fori_loop(0, buf.shape[0], copy, 0, unroll=4)
        at += buf.shape[0]


def products(table, i, j, groups):
    re = im = None
    for g in range(groups):
        ar = table[i, g * 16 : g * 16 + 8, :]
        ai = table[i, g * 16 + 8 : g * 16 + 16, :]
        br = table[j, g * 16 : g * 16 + 8, :]
        bi = table[j, g * 16 + 8 : g * 16 + 16, :]
        r = ar * br + ai * bi
        m = ai * br - ar * bi
        re = r if re is None else re + r
        im = m if im is None else im + m
    return re, im


BIG_ROWS = 17
SMALL_ROWS = 25


def cross_big(first_ref, second_ref, bufs, table, cross, out):
    pairs = out.shape[0]
    load_table(bufs, table, 0)

    def pair(p, carry):
        re, im = products(table, first_ref[p], second_ref[p], 4)
        cross[pl.ds(p * BIG_ROWS, 8), :] = re
        cross[pl.ds(p * BIG_ROWS + 8, 8), :] = im
        return carry

    lax.fori_loop(0, pairs, pair, 0, unroll=8)
    for k in range(16):
        out[:, k * LANES : (k + 1) * LANES] = cross[pl.ds(k, pairs, stride=BIG_ROWS), :].astype(
            jnp.bfloat16
        )


def cross_small(first_ref, second_ref, bufs, table, cross, out):
    pairs = out.shape[0]
    load_table(bufs, table, 64)

    def pair(p, carry):
        i = first_ref[p]
        j = second_ref[p]
        re, im = products(table, i, j, 2)
        at = p * SMALL_ROWS
        cross[pl.ds(at, 8), :] = re
        cross[pl.ds(at + 8, 8), :] = im
        a = table[i, 32:40, :]
        b = table[j, 32:40, :]
        cross[pl.ds(at + 16, 2), :] = a[0:2] * b[0:2] + a[2:4] * b[2:4]
        cross[pl.ds(at + 18, 2), :] = a[2:4] * b[0:2] - a[0:2] * b[2:4]
        return carry

    lax.fori_loop(0, pairs, pair, 0, unroll=8)

    def column(row):
        return cross[pl.ds(row, pairs, stride=SMALL_ROWS), :]

    for k in range(8):
        row = (k // 4) * 8 + k % 4
        out[:, k * LANES : (k + 1) * LANES] = (column(row) + column(row + 4)).astype(jnp.bfloat16)
    for k in range(2):
        row = 16 + 2 * k
        out[:, (8 + k) * LANES : (9 + k) * LANES] = (column(row) + column(row + 1)).astype(
            jnp.bfloat16
        )


def table_kernel(coarse_ref, fine_ref, big_ref, small_ref):
    half = fine_ref.shape[2] // LANES - 1
    for g in range(half + 1):
        at = slice(g * LANES, (g + 1) * LANES)
        cf = fine_ref[0, :, at]
        sf = fine_ref[1, :, at]
        if g < 8:
            ref, re, im = big_ref, g, g + 8
        elif g < half:
            ref, re, im = small_ref, g - 8, g - 8 + half - 8
        else:
            ref, re, im = small_ref, 2 * (half - 8), 2 * (half - 8) + 1
        for u in range(coarse_ref.shape[1]):
            cc = coarse_ref[0, u : u + 1, at]
            sc = coarse_ref[1, u : u + 1, at]
            rows = slice(u * FINE, (u + 1) * FINE)
            ref[rows, re * LANES : (re + 1) * LANES] = (cc * cf - sc * sf).astype(jnp.bfloat16)
            ref[rows, im * LANES : (im + 1) * LANES] = (sc * cf + cc * sf).astype(jnp.bfloat16)


def lag_bases(core, half, blocks):
    block_index = jnp.concatenate(
        [core * half + jnp.arange(half, dtype=jnp.int32), jnp.full((1,), blocks - 1, jnp.int32)]
    )
    bins = (K0 + block_index[:, None] * LANES + jnp.arange(LANES, dtype=jnp.int32)).reshape(-1)

    def base(lags):
        angles = (lags[:, None] * bins[None, :] % NFFT).astype(jnp.float32) * (2.0 * math.pi / NFFT)
        return jnp.stack([jnp.cos(angles), -jnp.sin(angles)])

    coarse = base(jnp.arange(LAGS // FINE, dtype=jnp.int32) * FINE - LAGS // 2)
    fine = base(jnp.arange(FINE, dtype=jnp.int32))
    return coarse, fine


def lag_table(coarse, fine):
    width = fine.shape[2]
    half = width // LANES - 1
    step = 8
    return pl.pallas_call(
        table_kernel,
        name="lagtable",
        grid=(LAGS // FINE // step,),
        out_shape=(
            jax.ShapeDtypeStruct((LAGS, 16 * LANES), jnp.bfloat16),
            jax.ShapeDtypeStruct((LAGS, 2 * (half + 1 - 8) * LANES), jnp.bfloat16),
        ),
        in_specs=[
            pl.BlockSpec((2, step, width), lambda u: (0, u, 0)),
            pl.BlockSpec((2, FINE, width), lambda u: (0, 0, 0)),
        ],
        out_specs=(
            pl.BlockSpec((step * FINE, 16 * LANES), lambda u: (u, 0)),
            pl.BlockSpec((step * FINE, 2 * (half + 1 - 8) * LANES), lambda u: (u, 0)),
        ),
        compiler_params=params(),
        cost_estimate=pl.CostEstimate(
            flops=LAGS * width * 6, bytes_accessed=LAGS * width * 4, transcendentals=0
        ),
    )(coarse, fine)


def dot_nt(a, b):
    return lax.dot_general(a, b, (((1,), (1,)), ((), ())), preferred_element_type=jnp.float32)


def scratch(bufs, pairs, each, *more):
    slots = sum(buf.shape[0] for buf in bufs)
    shapes = (
        ((slots,) + bufs[0].shape[1:], jnp.float32),
        ((pairs * each, LANES), jnp.float32),
    ) + more
    return dict(
        scratch_shapes=[pltpu.VMEM(*s) for s in shapes],
        compiler_params=params(*(size(*s) for s in shapes), roomy=len(bufs) == 1),
    )


def stack_cost(lags, depth, pairs):
    return pl.CostEstimate(
        flops=2 * lags * depth * pairs,
        bytes_accessed=2 * lags * depth + 4 * lags * pairs,
        transcendentals=0,
    )


def stack_small_kernel(count, tile, first_ref, second_ref, *refs):
    bufs = refs[:count]
    lag_ref, acc_ref, table, rows, cross = refs[count:]
    cross_small(first_ref, second_ref, bufs, table, rows, cross)
    for t in range(acc_ref.shape[0] // tile):
        at = slice(t * tile, (t + 1) * tile)
        acc_ref[at, :] = dot_nt(lag_ref[at, :], cross[...])


def stack_small(first, second, bufs, lag_table, tile):
    lags, depth = lag_table.shape
    pairs = first.shape[0]
    return pl.pallas_call(
        functools.partial(stack_small_kernel, len(bufs), tile),
        name="stack0",
        out_shape=jax.ShapeDtypeStruct((lags, pairs), jnp.float32),
        in_specs=[SMEM, SMEM] + [VMEM] * (len(bufs) + 1),
        out_specs=VMEM,
        cost_estimate=stack_cost(lags, depth, pairs),
        **scratch(bufs, pairs, SMALL_ROWS, ((pairs, depth), jnp.bfloat16)),
    )(first, second, *bufs, lag_table)


def finish(part, core, lag_ref, acc_ref, cross, send_ref, keep_ref):
    outer, tile, _ = send_ref.shape
    group_rows = lag_ref.shape[0] // (2 * outer)
    for mine in range(2):
        for at in range(outer):
            group = 2 * at + (core if mine else 1 - core)
            lags = pl.ds(pl.multiple_of(group * group_rows + part * tile, tile), tile)
            value = acc_ref[lags, :] + dot_nt(lag_ref[lags, :], cross[...])
            if mine:
                keep_ref[at] = value
            else:
                send_ref[at] = value.astype(send_ref.dtype)


def stack_outputs(acc, groups, parts):
    lags, pairs = acc.shape
    shape = (groups // 2, lags // groups // parts, pairs)
    return [jax.ShapeDtypeStruct(shape, jnp.bfloat16), jax.ShapeDtypeStruct(shape, jnp.float32)]


def stack_first_kernel(count, core_ref, first_ref, second_ref, *refs):
    bufs = refs[:count]
    lag_ref, acc_ref, send_ref, keep_ref, cross, table, rows = refs[count:]
    cross_big(first_ref, second_ref, bufs, table, rows, cross)
    finish(0, core_ref[0], lag_ref, acc_ref, cross, send_ref, keep_ref)


def stack_first(core, first, second, bufs, lag_table, acc, groups, parts):
    lags, depth = lag_table.shape
    pairs = acc.shape[1]
    return pl.pallas_call(
        functools.partial(stack_first_kernel, len(bufs)),
        name="stack1",
        in_specs=[SMEM] * 3 + [VMEM] * (len(bufs) + 2),
        out_specs=[VMEM] * 3,
        out_shape=stack_outputs(acc, groups, parts)
        + [jax.ShapeDtypeStruct((pairs, depth), jnp.bfloat16)],
        cost_estimate=stack_cost(lags // parts, depth, pairs),
        **scratch(bufs, pairs, BIG_ROWS),
    )(core, first, second, *bufs, lag_table, acc)


def stack_next_kernel(part, core_ref, lag_ref, acc_ref, cross, send_ref, keep_ref):
    finish(part, core_ref[0], lag_ref, acc_ref, cross, send_ref, keep_ref)


def stack_next(core, lag_table, acc, cross, groups, part, parts):
    lags, depth = lag_table.shape
    return pl.pallas_call(
        functools.partial(stack_next_kernel, part),
        name="stack2",
        in_specs=[SMEM] + [VMEM] * 3,
        out_specs=[VMEM] * 2,
        out_shape=stack_outputs(acc, groups, parts),
        compiler_params=params(),
        cost_estimate=stack_cost(lags // parts, depth, acc.shape[1]),
    )(core, lag_table, acc, cross)


def away_kernel(place_ref, keep_ref, near_ref, *outs):
    for d, out in enumerate(outs):
        at = place_ref[0] ^ (d + 1)
        out[...] = (keep_ref[at] + near_ref[at].astype(jnp.float32)).astype(out.dtype)


def sum_away(place, keep, near):
    outer, lags, pairs = keep.shape
    return pl.pallas_call(
        away_kernel,
        name="away",
        out_shape=[jax.ShapeDtypeStruct((lags, pairs), near.dtype)] * (outer - 1),
        in_specs=[SMEM, VMEM, VMEM],
        out_specs=[VMEM] * (outer - 1),
        compiler_params=params(2 * size(keep.shape, jnp.float32)),
        cost_estimate=pl.CostEstimate(
            flops=keep.size, bytes_accessed=6 * keep.size, transcendentals=0
        ),
    )(place, keep, near)


def result_kernel(scale, count, place_ref, *refs):
    keep, near, *far = refs[:count]
    place = place_ref[0]
    total = keep[place] + near[place].astype(jnp.float32)
    for ref in far:
        total = total + ref[...].astype(jnp.float32)
    refs[-1][...] = scale * total


def result(place, pieces, scale, part, parts, before):
    _, lags, pairs = pieces[0].shape
    specs = [pl.BlockSpec(x.shape, lambda i, n=x.ndim: (0,) * n) for x in pieces]
    operands = (place, *pieces)
    aliases = {}
    if before is not None:
        operands += (before,)
        specs.append(pl.BlockSpec(memory_space=pl.ANY))
        aliases = {len(operands) - 1: 0}
    return pl.pallas_call(
        functools.partial(result_kernel, scale, len(pieces)),
        name="result",
        grid=(1,),
        out_shape=jax.ShapeDtypeStruct((lags * parts, pairs), jnp.float32),
        in_specs=[SMEM] + specs,
        out_specs=pl.BlockSpec((lags, pairs), lambda i: (part, 0)),
        input_output_aliases=aliases,
        compiler_params=params(
            *(2 * size(x.shape, x.dtype) for x in pieces), 2 * size((lags, pairs), jnp.float32)
        ),
        cost_estimate=pl.CostEstimate(
            flops=lags * pairs * 4, bytes_accessed=lags * pairs * 16, transcendentals=0
        ),
    )(*operands)


def swap(x, axis, mask):
    return lax.ppermute(x, axis, [(i, i ^ mask) for i in range(lax.axis_size(axis))])


def swap_both(x, mask_pairs, mask_win):
    groups = lax.axis_size("win")
    perm = [
        (p * groups + w, (p ^ mask_pairs) * groups + (w ^ mask_win))
        for p in range(lax.axis_size("pairs"))
        for w in range(groups)
    ]
    return lax.ppermute(x, ("pairs", "win"), perm)


def after(x, *earlier):
    return lax.optimization_barrier((x,) + earlier)[0]


def local(spectra, requests, pair_first, pair_second):
    stations, windows, _, bins = spectra.shape
    sources = lax.axis_size("pairs")
    groups = lax.axis_size("win")
    cap = requests.shape[2]
    me = lax.axis_index("pairs").astype(jnp.int32)
    group = lax.axis_index("win").astype(jnp.int32)
    core = group & 1
    blocks = bins // LANES
    half = blocks // 2
    assert windows == 2 and blocks == 2 * half + 1 and half == 12 and groups % 2 == 0
    assert stations % 2 == 0

    keep_big, keep_small, give_big, give_small = whiten(core[None], spectra)
    near_big = swap(give_big, "win", 1)
    near_small = swap(give_small, "win", 1)

    slots = sources * cap
    wanted = jnp.maximum(requests[0], 0)
    if two_stage(sources):
        far = sources // 2
        chunks = {
            "small": [
                keep_small,
                near_small,
                swap(keep_small, "pairs", far),
                swap_both(give_small, far, 1),
            ],
            "big": [keep_big, near_big, swap(keep_big, "pairs", far), swap_both(give_big, far, 1)],
        }
        wanted = after(wanted, keep_small)
        asked = [wanted] + [swap(wanted, "pairs", d) for d in range(1, far)]
        early = select_early(me[None], asked[1], keep_big, near_big, keep_small, near_small)
        early = swap(early, "pairs", 1)
        arrived = {}
        for name, chunk in chunks.items():
            outs = select(me[None], asked, chunk, cap, name == "small", (1,))
            rows = [swap(outs[d], "pairs", d) for d in range(1, far)]
            arrived[name] = [outs[0], early] + rows
        small, big = arrived["small"], arrived["big"]
        core_table = core

        def row_of(slot):
            apart = (slot // cap) ^ me
            return (apart % far) * (2 * cap) + (apart // far) * cap + slot % cap

    else:
        asked_rows = lax.all_to_all(wanted, "pairs", split_axis=0, concat_axis=0, tiled=True)

        def exchange(chunk):
            outgoing = chunk[asked_rows]
            arrived = lax.all_to_all(outgoing, "pairs", split_axis=0, concat_axis=0, tiled=True)
            return [arrived.reshape((slots,) + chunk.shape[1:])]

        big = exchange(join(keep_big, near_big, False))
        small = exchange(join(keep_small, near_small, True))
        core_table = core

        def row_of(slot):
            return slot

    coarse, fine = lag_bases(core_table, half, blocks)
    table_big, table_small = lag_table(coarse, fine)
    first = row_of(pair_first)
    second = row_of(pair_second)
    acc = stack_small(first, second, small, table_small, LAGS // groups)

    place = (group >> 1)[None]
    parts = 2
    out = None
    norm_scale = 1.0 / math.sqrt(bins * windows * groups)
    send, keep, cross = stack_first(core[None], first, second, big, table_big, acc, groups, parts)
    for part in range(parts):
        if part > 0:
            send, keep = stack_next(core[None], table_big, acc, cross, groups, part, parts)
        near = swap(send, "win", 1)
        away = sum_away(place, keep, near)
        pieces = [keep, near] + [swap(x, "win", 2 * (d + 1)) for d, x in enumerate(away)]
        out = result(place, pieces, norm_scale, part, parts, out)
    return out


def two_stage(sources):
    return sources & (sources - 1) == 0 and 4 <= sources <= 16


def solution(mesh):
    step = jax.shard_map(
        local,
        mesh=mesh,
        in_specs=(P("pairs", "win", None, None), P("pairs", None, None), P("pairs"), P("pairs")),
        out_specs=P("win", "pairs"),
        check_vma=False,
    )
    sources = mesh.shape["pairs"]
    if not two_stage(sources):
        return step
    return step
```

```python
import functools
import math

import jax
import jax.numpy as jnp
from jax import lax
from jax.experimental import pallas as pl
from jax.experimental.pallas import tpu as pltpu
from jax.sharding import PartitionSpec as P


LAGS = 2048
NFFT = 18000
K0 = 360
LANES = 128
EPS = 1e-06
FINE = 32
VMEM = pl.BlockSpec(memory_space=pltpu.VMEM)
SMEM = pl.BlockSpec(memory_space=pltpu.SMEM)


def params(*nbytes, roomy=False):
    limit = 60 if roomy else sum(nbytes) // 1024**2 + 5
    return pltpu.CompilerParams(vmem_limit_bytes=limit * 1024**2)


def size(shape, dtype):
    return math.prod(shape) * jnp.dtype(dtype).itemsize


def whiten_kernel(core_ref, raw_ref, keep_big, keep_small, give_big, give_small, tmp):
    stations, windows, _, bins = raw_ref.shape
    blocks = bins // LANES
    half = blocks // 2
    core = core_ref[0]

    def white(re, im):
        power = jnp.sum(re * re + im * im, axis=1, keepdims=True) * (1.0 / (2 * LANES))
        scale = lax.rsqrt(power + EPS)
        return re * scale, im * scale

    def station(s, slot):
        for w in range(windows):
            for b in range(blocks):
                value = raw_ref[s, w, :, b * LANES : (b + 1) * LANES]
                side, at = divmod(b, half)
                if side == 2:
                    row = 96 + w
                elif at < 8:
                    row = side * 48 + w * 16 + at
                else:
                    row = side * 48 + 32 + w * 4 + at - 8
                tmp[slot, pl.ds(row, 2, stride=8), :] = value
        for mine, big, small in ((True, keep_big, keep_small), (False, give_big, give_small)):
            base = pl.multiple_of((core if mine else 1 - core) * 48, 16)
            for g in range(3):
                re = tmp[slot, pl.ds(base + g * 16, 8), :]
                im = tmp[slot, pl.ds(base + g * 16 + 8, 8), :]
                rows = jnp.concatenate(white(re, im), axis=0).astype(jnp.bfloat16)
                if g < 2:
                    big[s, g * 16 : g * 16 + 16, :] = rows
                else:
                    small[s, 0:16, :] = rows
        re, im = white(tmp[slot, 96:104, :], tmp[slot, 104:112, :])
        tmp[slot, 112:114, :] = re[0:windows]
        tmp[slot, 114:116, :] = im[0:windows]
        keep_small[s, 16:24, :] = tmp[slot, 112:120, :].astype(jnp.bfloat16)

    tmp[...] = jnp.zeros_like(tmp)

    def several(i, carry):
        for slot in range(2):
            station(2 * i + slot, slot)
        return carry

    lax.fori_loop(0, stations // 2, several, 0)


def whiten(core, raw):
    stations = raw.shape[0]
    rows = (32, 24, 32, 16)
    return pl.pallas_call(
        whiten_kernel,
        name="whiten",
        out_shape=tuple(jax.ShapeDtypeStruct((stations, r, LANES), jnp.bfloat16) for r in rows),
        in_specs=[SMEM, VMEM],
        out_specs=(VMEM,) * 4,
        scratch_shapes=[pltpu.VMEM((2, 120, LANES), jnp.float32)],
        compiler_params=params(size(raw.shape, raw.dtype)),
        cost_estimate=pl.CostEstimate(flops=2_000_000, bytes_accessed=2_000_000, transcendentals=0),
    )(core, raw)


def join(keep, got, small):
    if small:
        return jnp.concatenate([keep[:, :16], got, keep[:, 16:]], axis=1)
    return jnp.concatenate([keep, got], axis=1)


def copy_row(out, at, keep, got, row, small):
    if small:
        out[at : at + 16] = keep[row, 0:16]
        out[at + 16 : at + 32] = got[row]
        out[at + 32 : at + 40] = keep[row, 16:24]
    else:
        out[at : at + 32] = keep[row]
        out[at + 32 : at + 64] = got[row]


def select_kernel(sources, cap, small, early, me_ref, *refs):
    peers = (len(refs) - 4) // 2
    asked = refs[:peers]
    chunks = refs[peers : peers + 4]
    me = me_ref[0]
    for d, out in enumerate(refs[peers + 4 :]):
        for h in range(1 if d in early else 0, 2):
            source = me ^ (h * (sources // 2))
            keep, got = chunks[2 * h : 2 * h + 2]
            for c in range(cap):
                at = c if d in early else h * cap + c
                copy_row(out.at[at], 0, keep, got, asked[d][source, c], small)


def select(me, asked, chunks, cap, small, early):
    sources = asked[0].shape[0]
    rows = chunks[0].shape[1] + chunks[1].shape[1]
    outs = [
        jax.ShapeDtypeStruct(((1 if d in early else 2) * cap, rows, LANES), chunks[0].dtype)
        for d in range(len(asked))
    ]
    return pl.pallas_call(
        functools.partial(select_kernel, sources, cap, small, early),
        name="select",
        out_shape=outs,
        in_specs=[SMEM] * (1 + len(asked)) + [VMEM] * 4,
        out_specs=[VMEM] * len(asked),
        compiler_params=params(),
        cost_estimate=pl.CostEstimate(flops=0, bytes_accessed=1_000_000, transcendentals=0),
    )(me, *asked, *chunks)


def early_kernel(me_ref, asked, keep_big, got_big, keep_small, got_small, out):
    for c in range(out.shape[0]):
        row = asked[me_ref[0], c]
        copy_row(out.at[c], 0, keep_big, got_big, row, False)
        copy_row(out.at[c], 64, keep_small, got_small, row, True)


def select_early(me, asked, keep_big, got_big, keep_small, got_small):
    return pl.pallas_call(
        early_kernel,
        name="selectearly",
        out_shape=jax.ShapeDtypeStruct((asked.shape[1], 104, LANES), keep_big.dtype),
        in_specs=[SMEM] * 2 + [VMEM] * 4,
        out_specs=VMEM,
        compiler_params=params(),
        cost_estimate=pl.CostEstimate(flops=0, bytes_accessed=500_000, transcendentals=0),
    )(me, asked, keep_big, got_big, keep_small, got_small)


def load_table(bufs, table, lo):
    rows = table.shape[1]
    at = 0
    for buf in bufs:
        start = lo if buf.shape[1] > rows else 0

        def copy(i, carry, buf=buf, at=at, start=start):
            table[at + i] = buf[i, start : start + rows].astype(jnp.float32)
            return carry

        lax.fori_loop(0, buf.shape[0], copy, 0, unroll=4)
        at += buf.shape[0]


def products(table, i, j, groups):
    re = im = None
    for g in range(groups):
        ar = table[i, g * 16 : g * 16 + 8, :]
        ai = table[i, g * 16 + 8 : g * 16 + 16, :]
        br = table[j, g * 16 : g * 16 + 8, :]
        bi = table[j, g * 16 + 8 : g * 16 + 16, :]
        r = ar * br + ai * bi
        m = ai * br - ar * bi
        re = r if re is None else re + r
        im = m if im is None else im + m
    return re, im


BIG_ROWS = 17
SMALL_ROWS = 25


def cross_big(first_ref, second_ref, bufs, table, cross, out):
    pairs = out.shape[0]
    load_table(bufs, table, 0)

    def pair(p, carry):
        re, im = products(table, first_ref[p], second_ref[p], 4)
        cross[pl.ds(p * BIG_ROWS, 8), :] = re
        cross[pl.ds(p * BIG_ROWS + 8, 8), :] = im
        return carry

    lax.fori_loop(0, pairs, pair, 0, unroll=16)
    for k in range(16):
        out[:, k * LANES : (k + 1) * LANES] = cross[pl.ds(k, pairs, stride=BIG_ROWS), :].astype(
            jnp.bfloat16
        )


def cross_small(first_ref, second_ref, bufs, table, cross, out):
    pairs = out.shape[0]
    load_table(bufs, table, 64)

    def pair(p, carry):
        i = first_ref[p]
        j = second_ref[p]
        re, im = products(table, i, j, 2)
        at = p * SMALL_ROWS
        cross[pl.ds(at, 8), :] = re
        cross[pl.ds(at + 8, 8), :] = im
        a = table[i, 32:40, :]
        b = table[j, 32:40, :]
        cross[pl.ds(at + 16, 2), :] = a[0:2] * b[0:2] + a[2:4] * b[2:4]
        cross[pl.ds(at + 18, 2), :] = a[2:4] * b[0:2] - a[0:2] * b[2:4]
        return carry

    lax.fori_loop(0, pairs, pair, 0, unroll=8)

    def column(row):
        return cross[pl.ds(row, pairs, stride=SMALL_ROWS), :]

    for k in range(8):
        row = (k // 4) * 8 + k % 4
        out[:, k * LANES : (k + 1) * LANES] = (column(row) + column(row + 4)).astype(jnp.bfloat16)
    for k in range(2):
        row = 16 + 2 * k
        out[:, (8 + k) * LANES : (9 + k) * LANES] = (column(row) + column(row + 1)).astype(
            jnp.bfloat16
        )


def table_kernel(coarse_ref, fine_ref, big_ref, small_ref):
    half = fine_ref.shape[2] // LANES - 1
    for g in range(half + 1):
        at = slice(g * LANES, (g + 1) * LANES)
        cf = fine_ref[0, :, at]
        sf = fine_ref[1, :, at]
        if g < 8:
            ref, re, im = big_ref, g, g + 8
        elif g < half:
            ref, re, im = small_ref, g - 8, g - 8 + half - 8
        else:
            ref, re, im = small_ref, 2 * (half - 8), 2 * (half - 8) + 1
        for u in range(coarse_ref.shape[1]):
            cc = coarse_ref[0, u : u + 1, at]
            sc = coarse_ref[1, u : u + 1, at]
            rows = slice(u * FINE, (u + 1) * FINE)
            ref[rows, re * LANES : (re + 1) * LANES] = (cc * cf - sc * sf).astype(jnp.bfloat16)
            ref[rows, im * LANES : (im + 1) * LANES] = (sc * cf + cc * sf).astype(jnp.bfloat16)


def lag_bases(core, half, blocks):
    block_index = jnp.concatenate(
        [core * half + jnp.arange(half, dtype=jnp.int32), jnp.full((1,), blocks - 1, jnp.int32)]
    )
    bins = (K0 + block_index[:, None] * LANES + jnp.arange(LANES, dtype=jnp.int32)).reshape(-1)

    def base(lags):
        angles = (lags[:, None] * bins[None, :] % NFFT).astype(jnp.float32) * (2.0 * math.pi / NFFT)
        return jnp.stack([jnp.cos(angles), -jnp.sin(angles)])

    coarse = base(jnp.arange(LAGS // FINE, dtype=jnp.int32) * FINE - LAGS // 2)
    fine = base(jnp.arange(FINE, dtype=jnp.int32))
    return coarse, fine


def lag_table(coarse, fine):
    width = fine.shape[2]
    half = width // LANES - 1
    step = 8
    return pl.pallas_call(
        table_kernel,
        name="lagtable",
        grid=(LAGS // FINE // step,),
        out_shape=(
            jax.ShapeDtypeStruct((LAGS, 16 * LANES), jnp.bfloat16),
            jax.ShapeDtypeStruct((LAGS, 2 * (half + 1 - 8) * LANES), jnp.bfloat16),
        ),
        in_specs=[
            pl.BlockSpec((2, step, width), lambda u: (0, u, 0)),
            pl.BlockSpec((2, FINE, width), lambda u: (0, 0, 0)),
        ],
        out_specs=(
            pl.BlockSpec((step * FINE, 16 * LANES), lambda u: (u, 0)),
            pl.BlockSpec((step * FINE, 2 * (half + 1 - 8) * LANES), lambda u: (u, 0)),
        ),
        compiler_params=params(),
        cost_estimate=pl.CostEstimate(
            flops=LAGS * width * 6, bytes_accessed=LAGS * width * 4, transcendentals=0
        ),
    )(coarse, fine)


def dot_nt(a, b):
    return lax.dot_general(a, b, (((1,), (1,)), ((), ())), preferred_element_type=jnp.float32)


def scratch(bufs, pairs, each, *more):
    slots = sum(buf.shape[0] for buf in bufs)
    shapes = (
        ((slots,) + bufs[0].shape[1:], jnp.float32),
        ((pairs * each, LANES), jnp.float32),
    ) + more
    return dict(
        scratch_shapes=[pltpu.VMEM(*s) for s in shapes],
        compiler_params=params(*(size(*s) for s in shapes), roomy=len(bufs) == 1),
    )


def stack_cost(lags, depth, pairs):
    return pl.CostEstimate(
        flops=2 * lags * depth * pairs,
        bytes_accessed=2 * lags * depth + 4 * lags * pairs,
        transcendentals=0,
    )


def stack_small_kernel(count, tile, first_ref, second_ref, *refs):
    bufs = refs[:count]
    lag_ref, acc_ref, table, rows, cross = refs[count:]
    cross_small(first_ref, second_ref, bufs, table, rows, cross)
    for t in range(acc_ref.shape[0] // tile):
        at = slice(t * tile, (t + 1) * tile)
        acc_ref[at, :] = dot_nt(lag_ref[at, :], cross[...])


def stack_small(first, second, bufs, lag_table, tile):
    lags, depth = lag_table.shape
    pairs = first.shape[0]
    return pl.pallas_call(
        functools.partial(stack_small_kernel, len(bufs), tile),
        name="stack0",
        out_shape=jax.ShapeDtypeStruct((lags, pairs), jnp.float32),
        in_specs=[SMEM, SMEM] + [VMEM] * (len(bufs) + 1),
        out_specs=VMEM,
        cost_estimate=stack_cost(lags, depth, pairs),
        **scratch(bufs, pairs, SMALL_ROWS, ((pairs, depth), jnp.bfloat16)),
    )(first, second, *bufs, lag_table)


def finish(part, core, lag_ref, acc_ref, cross, send_ref, keep_ref):
    outer, tile, _ = send_ref.shape
    group_rows = lag_ref.shape[0] // (2 * outer)
    for mine in range(2):
        for at in range(outer):
            group = 2 * at + (core if mine else 1 - core)
            lags = pl.ds(pl.multiple_of(group * group_rows + part * tile, tile), tile)
            value = acc_ref[lags, :] + dot_nt(lag_ref[lags, :], cross[...])
            if mine:
                keep_ref[at] = value
            else:
                send_ref[at] = value.astype(send_ref.dtype)


def stack_outputs(acc, groups, parts):
    lags, pairs = acc.shape
    shape = (groups // 2, lags // groups // parts, pairs)
    return [jax.ShapeDtypeStruct(shape, jnp.bfloat16), jax.ShapeDtypeStruct(shape, jnp.float32)]


def stack_first_kernel(count, core_ref, first_ref, second_ref, *refs):
    bufs = refs[:count]
    lag_ref, acc_ref, send_ref, keep_ref, cross, table, rows = refs[count:]
    cross_big(first_ref, second_ref, bufs, table, rows, cross)
    finish(0, core_ref[0], lag_ref, acc_ref, cross, send_ref, keep_ref)


def stack_first(core, first, second, bufs, lag_table, acc, groups, parts):
    lags, depth = lag_table.shape
    pairs = acc.shape[1]
    return pl.pallas_call(
        functools.partial(stack_first_kernel, len(bufs)),
        name="stack1",
        in_specs=[SMEM] * 3 + [VMEM] * (len(bufs) + 2),
        out_specs=[VMEM] * 3,
        out_shape=stack_outputs(acc, groups, parts)
        + [jax.ShapeDtypeStruct((pairs, depth), jnp.bfloat16)],
        cost_estimate=stack_cost(lags // parts, depth, pairs),
        **scratch(bufs, pairs, BIG_ROWS),
    )(core, first, second, *bufs, lag_table, acc)


def stack_next_kernel(part, core_ref, lag_ref, acc_ref, cross, send_ref, keep_ref):
    finish(part, core_ref[0], lag_ref, acc_ref, cross, send_ref, keep_ref)


def stack_next(core, lag_table, acc, cross, groups, part, parts):
    lags, depth = lag_table.shape
    return pl.pallas_call(
        functools.partial(stack_next_kernel, part),
        name="stack2",
        in_specs=[SMEM] + [VMEM] * 3,
        out_specs=[VMEM] * 2,
        out_shape=stack_outputs(acc, groups, parts),
        compiler_params=params(),
        cost_estimate=stack_cost(lags // parts, depth, acc.shape[1]),
    )(core, lag_table, acc, cross)


def away_kernel(place_ref, keep_ref, near_ref, *outs):
    for d, out in enumerate(outs):
        at = place_ref[0] ^ (d + 1)
        out[...] = (keep_ref[at] + near_ref[at].astype(jnp.float32)).astype(out.dtype)


def sum_away(place, keep, near):
    outer, lags, pairs = keep.shape
    return pl.pallas_call(
        away_kernel,
        name="away",
        out_shape=[jax.ShapeDtypeStruct((lags, pairs), near.dtype)] * (outer - 1),
        in_specs=[SMEM, VMEM, VMEM],
        out_specs=[VMEM] * (outer - 1),
        compiler_params=params(2 * size(keep.shape, jnp.float32)),
        cost_estimate=pl.CostEstimate(
            flops=keep.size, bytes_accessed=6 * keep.size, transcendentals=0
        ),
    )(place, keep, near)


def result_kernel(scale, count, part, place_ref, *refs):
    keep, near, *far = refs[:count]
    out, rows, sem = refs[-3:]
    place = place_ref[0]
    total = keep[place] + near[place].astype(jnp.float32)
    for ref in far:
        total = total + ref[...].astype(jnp.float32)
    rows[...] = scale * total
    lags = rows.shape[0]
    copy = pltpu.make_async_copy(rows, out.at[pl.ds(part * lags, lags)], sem)
    copy.start()
    copy.wait()


def result(place, pieces, scale, part, parts, before):
    _, lags, pairs = pieces[0].shape
    specs = [VMEM] * len(pieces)
    operands = (place, *pieces)
    aliases = {}
    if before is not None:
        operands += (before,)
        specs.append(pl.BlockSpec(memory_space=pl.ANY))
        aliases = {len(operands) - 1: 0}
    return pl.pallas_call(
        functools.partial(result_kernel, scale, len(pieces), part),
        name="result",
        out_shape=jax.ShapeDtypeStruct((lags * parts, pairs), jnp.float32),
        in_specs=[SMEM] + specs,
        out_specs=pl.BlockSpec(memory_space=pl.ANY),
        scratch_shapes=[pltpu.VMEM((lags, pairs), jnp.float32), pltpu.SemaphoreType.DMA],
        input_output_aliases=aliases,
        compiler_params=params(size((lags, pairs), jnp.float32)),
        cost_estimate=pl.CostEstimate(
            flops=lags * pairs * 4, bytes_accessed=lags * pairs * 16, transcendentals=0
        ),
    )(*operands)


def swap(x, axis, mask):
    return lax.ppermute(x, axis, [(i, i ^ mask) for i in range(lax.axis_size(axis))])


def swap_both(x, mask_pairs, mask_win):
    groups = lax.axis_size("win")
    perm = [
        (p * groups + w, (p ^ mask_pairs) * groups + (w ^ mask_win))
        for p in range(lax.axis_size("pairs"))
        for w in range(groups)
    ]
    return lax.ppermute(x, ("pairs", "win"), perm)


def after(x, *earlier):
    return lax.optimization_barrier((x,) + earlier)[0]


def local(spectra, requests, pair_first, pair_second):
    stations, windows, _, bins = spectra.shape
    sources = lax.axis_size("pairs")
    groups = lax.axis_size("win")
    cap = requests.shape[2]
    me = lax.axis_index("pairs").astype(jnp.int32)
    group = lax.axis_index("win").astype(jnp.int32)
    core = group & 1
    blocks = bins // LANES
    half = blocks // 2
    assert windows == 2 and blocks == 2 * half + 1 and half == 12 and groups % 2 == 0
    assert stations % 2 == 0

    keep_big, keep_small, give_big, give_small = whiten(core[None], spectra)
    near_big = swap(give_big, "win", 1)
    near_small = swap(give_small, "win", 1)

    slots = sources * cap
    wanted = jnp.maximum(requests[0], 0)
    if two_stage(sources):
        far = sources // 2
        chunks = {
            "small": [
                keep_small,
                near_small,
                swap(keep_small, "pairs", far),
                swap_both(give_small, far, 1),
            ],
            "big": [keep_big, near_big, swap(keep_big, "pairs", far), swap_both(give_big, far, 1)],
        }
        wanted = after(wanted, keep_small)
        asked = [wanted] + [swap(wanted, "pairs", d) for d in range(1, far)]
        early = select_early(me[None], asked[1], keep_big, near_big, keep_small, near_small)
        early = swap(early, "pairs", 1)
        arrived = {}
        for name, chunk in chunks.items():
            outs = select(me[None], asked, chunk, cap, name == "small", (1,))
            rows = [swap(outs[d], "pairs", d) for d in range(1, far)]
            arrived[name] = [outs[0], early] + rows
        small, big = arrived["small"], arrived["big"]
        core_table = core

        def row_of(slot):
            apart = (slot // cap) ^ me
            return (apart % far) * (2 * cap) + (apart // far) * cap + slot % cap

    else:
        asked_rows = lax.all_to_all(wanted, "pairs", split_axis=0, concat_axis=0, tiled=True)

        def exchange(chunk):
            outgoing = chunk[asked_rows]
            arrived = lax.all_to_all(outgoing, "pairs", split_axis=0, concat_axis=0, tiled=True)
            return [arrived.reshape((slots,) + chunk.shape[1:])]

        big = exchange(join(keep_big, near_big, False))
        small = exchange(join(keep_small, near_small, True))
        core_table = core

        def row_of(slot):
            return slot

    coarse, fine = lag_bases(core_table, half, blocks)
    table_big, table_small = lag_table(coarse, fine)
    first = row_of(pair_first)
    second = row_of(pair_second)
    acc = stack_small(first, second, small, table_small, LAGS // groups)

    place = (group >> 1)[None]
    parts = 2
    out = None
    norm_scale = 1.0 / math.sqrt(bins * windows * groups)
    send, keep, cross = stack_first(core[None], first, second, big, table_big, acc, groups, parts)
    for part in range(parts):
        if part > 0:
            send, keep = stack_next(core[None], table_big, acc, cross, groups, part, parts)
        near = swap(send, "win", 1)
        away = sum_away(place, keep, near)
        pieces = [keep, near] + [swap(x, "win", 2 * (d + 1)) for d, x in enumerate(away)]
        out = result(place, pieces, norm_scale, part, parts, out)
    return out


def two_stage(sources):
    return sources & (sources - 1) == 0 and 4 <= sources <= 16


def solution(mesh):
    step = jax.shard_map(
        local,
        mesh=mesh,
        in_specs=(P("pairs", "win", None, None), P("pairs", None, None), P("pairs"), P("pairs")),
        out_specs=P("win", "pairs"),
        check_vma=False,
    )
    sources = mesh.shape["pairs"]
    if not two_stage(sources):
        return step
    return step
```

```python
import functools
import math

import jax
import jax.numpy as jnp
from jax import lax
from jax.experimental import pallas as pl
from jax.experimental.pallas import tpu as pltpu
from jax.sharding import PartitionSpec as P


LAGS = 2048
NFFT = 18000
K0 = 360
LANES = 128
EPS = 1e-06
FINE = 32
VMEM = pl.BlockSpec(memory_space=pltpu.VMEM)
SMEM = pl.BlockSpec(memory_space=pltpu.SMEM)


def params(*nbytes, roomy=False):
    limit = 60 if roomy else sum(nbytes) // 1024**2 + 5
    return pltpu.CompilerParams(vmem_limit_bytes=limit * 1024**2)


def size(shape, dtype):
    return math.prod(shape) * jnp.dtype(dtype).itemsize


def whiten_kernel(core_ref, raw_ref, keep_big, keep_small, give_big, give_small, tmp):
    stations, windows, _, bins = raw_ref.shape
    blocks = bins // LANES
    half = blocks // 2
    core = core_ref[0]

    def white(re, im):
        power = jnp.sum(re * re + im * im, axis=1, keepdims=True) * (1.0 / (2 * LANES))
        scale = lax.rsqrt(power + EPS)
        return re * scale, im * scale

    def station(s, slot):
        for w in range(windows):
            for b in range(blocks):
                value = raw_ref[s, w, :, b * LANES : (b + 1) * LANES]
                side, at = divmod(b, half)
                if side == 2:
                    row = 96 + w
                elif at < 8:
                    row = side * 48 + w * 16 + at
                else:
                    row = side * 48 + 32 + w * 4 + at - 8
                tmp[slot, pl.ds(row, 2, stride=8), :] = value
        for mine, big, small in ((True, keep_big, keep_small), (False, give_big, give_small)):
            base = pl.multiple_of((core if mine else 1 - core) * 48, 16)
            for g in range(3):
                re = tmp[slot, pl.ds(base + g * 16, 8), :]
                im = tmp[slot, pl.ds(base + g * 16 + 8, 8), :]
                rows = jnp.concatenate(white(re, im), axis=0).astype(jnp.bfloat16)
                if g < 2:
                    big[s, g * 16 : g * 16 + 16, :] = rows
                else:
                    small[s, 0:16, :] = rows
        re, im = white(tmp[slot, 96:104, :], tmp[slot, 104:112, :])
        tmp[slot, 112:114, :] = re[0:windows]
        tmp[slot, 114:116, :] = im[0:windows]
        keep_small[s, 16:24, :] = tmp[slot, 112:120, :].astype(jnp.bfloat16)

    tmp[...] = jnp.zeros_like(tmp)

    def several(i, carry):
        for slot in range(2):
            station(2 * i + slot, slot)
        return carry

    lax.fori_loop(0, stations // 2, several, 0)


def whiten(core, raw):
    stations = raw.shape[0]
    rows = (32, 24, 32, 16)
    return pl.pallas_call(
        whiten_kernel,
        name="whiten",
        out_shape=tuple(jax.ShapeDtypeStruct((stations, r, LANES), jnp.bfloat16) for r in rows),
        in_specs=[SMEM, VMEM],
        out_specs=(VMEM,) * 4,
        scratch_shapes=[pltpu.VMEM((2, 160, LANES), jnp.float32)],
        compiler_params=params(size(raw.shape, raw.dtype)),
        cost_estimate=pl.CostEstimate(flops=2_000_000, bytes_accessed=2_000_000, transcendentals=0),
    )(core, raw)


def join(keep, got, small):
    if small:
        return jnp.concatenate([keep[:, :16], got, keep[:, 16:]], axis=1)
    return jnp.concatenate([keep, got], axis=1)


def copy_row(out, at, keep, got, row, small):
    if small:
        out[at : at + 16] = keep[row, 0:16]
        out[at + 16 : at + 32] = got[row]
        out[at + 32 : at + 40] = keep[row, 16:24]
    else:
        out[at : at + 32] = keep[row]
        out[at + 32 : at + 64] = got[row]


def select_kernel(sources, cap, small, early, me_ref, *refs):
    peers = (len(refs) - 4) // 2
    asked = refs[:peers]
    chunks = refs[peers : peers + 4]
    me = me_ref[0]
    for d, out in enumerate(refs[peers + 4 :]):
        for h in range(1 if d in early else 0, 2):
            source = me ^ (h * (sources // 2))
            keep, got = chunks[2 * h : 2 * h + 2]
            for c in range(cap):
                at = c if d in early else h * cap + c
                copy_row(out.at[at], 0, keep, got, asked[d][source, c], small)


def select(me, asked, chunks, cap, small, early):
    sources = asked[0].shape[0]
    rows = chunks[0].shape[1] + chunks[1].shape[1]
    outs = [
        jax.ShapeDtypeStruct(((1 if d in early else 2) * cap, rows, LANES), chunks[0].dtype)
        for d in range(len(asked))
    ]
    return pl.pallas_call(
        functools.partial(select_kernel, sources, cap, small, early),
        name="select",
        out_shape=outs,
        in_specs=[SMEM] * (1 + len(asked)) + [VMEM] * 4,
        out_specs=[VMEM] * len(asked),
        compiler_params=params(),
        cost_estimate=pl.CostEstimate(flops=0, bytes_accessed=1_000_000, transcendentals=0),
    )(me, *asked, *chunks)


def early_kernel(me_ref, asked, keep_big, got_big, keep_small, got_small, out):
    for c in range(out.shape[0]):
        row = asked[me_ref[0], c]
        copy_row(out.at[c], 0, keep_big, got_big, row, False)
        copy_row(out.at[c], 64, keep_small, got_small, row, True)


def select_early(me, asked, keep_big, got_big, keep_small, got_small):
    return pl.pallas_call(
        early_kernel,
        name="selectearly",
        out_shape=jax.ShapeDtypeStruct((asked.shape[1], 104, LANES), keep_big.dtype),
        in_specs=[SMEM] * 2 + [VMEM] * 4,
        out_specs=VMEM,
        compiler_params=params(),
        cost_estimate=pl.CostEstimate(flops=0, bytes_accessed=500_000, transcendentals=0),
    )(me, asked, keep_big, got_big, keep_small, got_small)


def load_table(bufs, table, lo):
    rows = table.shape[1]
    at = 0
    for buf in bufs:
        start = lo if buf.shape[1] > rows else 0

        def copy(i, carry, buf=buf, at=at, start=start):
            table[at + i] = buf[i, start : start + rows].astype(jnp.float32)
            return carry

        lax.fori_loop(0, buf.shape[0], copy, 0, unroll=8)
        at += buf.shape[0]


def products(table, i, j, groups):
    re = im = None
    for g in range(groups):
        ar = table[i, g * 16 : g * 16 + 8, :]
        ai = table[i, g * 16 + 8 : g * 16 + 16, :]
        br = table[j, g * 16 : g * 16 + 8, :]
        bi = table[j, g * 16 + 8 : g * 16 + 16, :]
        r = ar * br + ai * bi
        m = ai * br - ar * bi
        re = r if re is None else re + r
        im = m if im is None else im + m
    return re, im


BIG_ROWS = 17
SMALL_ROWS = 25


def cross_big(first_ref, second_ref, bufs, table, cross, out):
    pairs = out.shape[0]
    load_table(bufs, table, 0)

    def pair(p, carry):
        re, im = products(table, first_ref[p], second_ref[p], 4)
        cross[pl.ds(p * BIG_ROWS, 8), :] = re
        cross[pl.ds(p * BIG_ROWS + 8, 8), :] = im
        return carry

    lax.fori_loop(0, pairs, pair, 0, unroll=16)
    for k in range(16):
        out[:, k * LANES : (k + 1) * LANES] = cross[pl.ds(k, pairs, stride=BIG_ROWS), :].astype(
            jnp.bfloat16
        )


def cross_small(first_ref, second_ref, bufs, table, cross, out):
    pairs = out.shape[0]
    load_table(bufs, table, 64)

    def pair(p, carry):
        i = first_ref[p]
        j = second_ref[p]
        re, im = products(table, i, j, 2)
        at = p * SMALL_ROWS
        cross[pl.ds(at, 8), :] = re
        cross[pl.ds(at + 8, 8), :] = im
        a = table[i, 32:40, :]
        b = table[j, 32:40, :]
        cross[pl.ds(at + 16, 2), :] = a[0:2] * b[0:2] + a[2:4] * b[2:4]
        cross[pl.ds(at + 18, 2), :] = a[2:4] * b[0:2] - a[0:2] * b[2:4]
        return carry

    lax.fori_loop(0, pairs, pair, 0, unroll=8)

    def column(row):
        return cross[pl.ds(row, pairs, stride=SMALL_ROWS), :]

    for k in range(8):
        row = (k // 4) * 8 + k % 4
        out[:, k * LANES : (k + 1) * LANES] = (column(row) + column(row + 4)).astype(jnp.bfloat16)
    for k in range(2):
        row = 16 + 2 * k
        out[:, (8 + k) * LANES : (9 + k) * LANES] = (column(row) + column(row + 1)).astype(
            jnp.bfloat16
        )


def table_kernel(coarse_ref, fine_ref, big_ref, small_ref):
    half = fine_ref.shape[2] // LANES - 1
    for g in range(half + 1):
        at = slice(g * LANES, (g + 1) * LANES)
        cf = fine_ref[0, :, at]
        sf = fine_ref[1, :, at]
        if g < 8:
            ref, re, im = big_ref, g, g + 8
        elif g < half:
            ref, re, im = small_ref, g - 8, g - 8 + half - 8
        else:
            ref, re, im = small_ref, 2 * (half - 8), 2 * (half - 8) + 1
        for u in range(coarse_ref.shape[1]):
            cc = coarse_ref[0, u : u + 1, at]
            sc = coarse_ref[1, u : u + 1, at]
            rows = slice(u * FINE, (u + 1) * FINE)
            ref[rows, re * LANES : (re + 1) * LANES] = (cc * cf - sc * sf).astype(jnp.bfloat16)
            ref[rows, im * LANES : (im + 1) * LANES] = (sc * cf + cc * sf).astype(jnp.bfloat16)


def lag_bases(core, half, blocks):
    block_index = jnp.concatenate(
        [core * half + jnp.arange(half, dtype=jnp.int32), jnp.full((1,), blocks - 1, jnp.int32)]
    )
    bins = (K0 + block_index[:, None] * LANES + jnp.arange(LANES, dtype=jnp.int32)).reshape(-1)

    def base(lags):
        angles = (lags[:, None] * bins[None, :] % NFFT).astype(jnp.float32) * (2.0 * math.pi / NFFT)
        return jnp.stack([jnp.cos(angles), -jnp.sin(angles)])

    coarse = base(jnp.arange(LAGS // FINE, dtype=jnp.int32) * FINE - LAGS // 2)
    fine = base(jnp.arange(FINE, dtype=jnp.int32))
    return coarse, fine


def lag_table(coarse, fine):
    width = fine.shape[2]
    half = width // LANES - 1
    step = 8
    return pl.pallas_call(
        table_kernel,
        name="lagtable",
        grid=(LAGS // FINE // step,),
        out_shape=(
            jax.ShapeDtypeStruct((LAGS, 16 * LANES), jnp.bfloat16),
            jax.ShapeDtypeStruct((LAGS, 2 * (half + 1 - 8) * LANES), jnp.bfloat16),
        ),
        in_specs=[
            pl.BlockSpec((2, step, width), lambda u: (0, u, 0)),
            pl.BlockSpec((2, FINE, width), lambda u: (0, 0, 0)),
        ],
        out_specs=(
            pl.BlockSpec((step * FINE, 16 * LANES), lambda u: (u, 0)),
            pl.BlockSpec((step * FINE, 2 * (half + 1 - 8) * LANES), lambda u: (u, 0)),
        ),
        compiler_params=params(),
        cost_estimate=pl.CostEstimate(
            flops=LAGS * width * 6, bytes_accessed=LAGS * width * 4, transcendentals=0
        ),
    )(coarse, fine)


def dot_nt(a, b):
    return lax.dot_general(a, b, (((1,), (1,)), ((), ())), preferred_element_type=jnp.float32)


def scratch(bufs, pairs, each, *more):
    slots = sum(buf.shape[0] for buf in bufs)
    shapes = (
        ((slots,) + bufs[0].shape[1:], jnp.float32),
        ((pairs * each + 64, LANES), jnp.float32),
    ) + more
    return dict(
        scratch_shapes=[pltpu.VMEM(*s) for s in shapes],
        compiler_params=params(*(size(*s) for s in shapes), roomy=len(bufs) == 1),
    )


def stack_cost(lags, depth, pairs):
    return pl.CostEstimate(
        flops=2 * lags * depth * pairs,
        bytes_accessed=2 * lags * depth + 4 * lags * pairs,
        transcendentals=0,
    )


def stack_small_kernel(count, tile, first_ref, second_ref, *refs):
    bufs = refs[:count]
    lag_ref, acc_ref, table, rows, cross = refs[count:]
    cross_small(first_ref, second_ref, bufs, table, rows, cross)
    for t in range(acc_ref.shape[0] // tile):
        at = slice(t * tile, (t + 1) * tile)
        acc_ref[at, :] = dot_nt(lag_ref[at, :], cross[...])


def stack_small(first, second, bufs, lag_table, tile):
    lags, depth = lag_table.shape
    pairs = first.shape[0]
    return pl.pallas_call(
        functools.partial(stack_small_kernel, len(bufs), tile),
        name="stack0",
        out_shape=jax.ShapeDtypeStruct((lags, pairs), jnp.float32),
        in_specs=[SMEM, SMEM] + [VMEM] * (len(bufs) + 1),
        out_specs=VMEM,
        cost_estimate=stack_cost(lags, depth, pairs),
        **scratch(bufs, pairs, SMALL_ROWS, ((pairs, depth), jnp.bfloat16)),
    )(first, second, *bufs, lag_table)


def finish(part, core, lag_ref, acc_ref, cross, send_ref, keep_ref):
    outer, tile, _ = send_ref.shape
    group_rows = lag_ref.shape[0] // (2 * outer)
    for mine in range(2):
        for at in range(outer):
            group = 2 * at + (core if mine else 1 - core)
            lags = pl.ds(pl.multiple_of(group * group_rows + part * tile, tile), tile)
            value = acc_ref[lags, :] + dot_nt(lag_ref[lags, :], cross[...])
            if mine:
                keep_ref[at] = value
            else:
                send_ref[at] = value.astype(send_ref.dtype)


def stack_outputs(acc, groups, parts):
    lags, pairs = acc.shape
    shape = (groups // 2, lags // groups // parts, pairs)
    return [jax.ShapeDtypeStruct(shape, jnp.bfloat16), jax.ShapeDtypeStruct(shape, jnp.float32)]


def stack_first_kernel(count, core_ref, first_ref, second_ref, *refs):
    bufs = refs[:count]
    lag_ref, acc_ref, send_ref, keep_ref, cross, table, rows = refs[count:]
    cross_big(first_ref, second_ref, bufs, table, rows, cross)
    finish(0, core_ref[0], lag_ref, acc_ref, cross, send_ref, keep_ref)


def stack_first(core, first, second, bufs, lag_table, acc, groups, parts):
    lags, depth = lag_table.shape
    pairs = acc.shape[1]
    return pl.pallas_call(
        functools.partial(stack_first_kernel, len(bufs)),
        name="stack1",
        in_specs=[SMEM] * 3 + [VMEM] * (len(bufs) + 2),
        out_specs=[VMEM] * 3,
        out_shape=stack_outputs(acc, groups, parts)
        + [jax.ShapeDtypeStruct((pairs, depth), jnp.bfloat16)],
        cost_estimate=stack_cost(lags // parts, depth, pairs),
        **scratch(bufs, pairs, BIG_ROWS),
    )(core, first, second, *bufs, lag_table, acc)


def stack_next_kernel(part, core_ref, lag_ref, acc_ref, cross, send_ref, keep_ref):
    finish(part, core_ref[0], lag_ref, acc_ref, cross, send_ref, keep_ref)


def stack_next(core, lag_table, acc, cross, groups, part, parts):
    lags, depth = lag_table.shape
    return pl.pallas_call(
        functools.partial(stack_next_kernel, part),
        name="stack2",
        in_specs=[SMEM] + [VMEM] * 3,
        out_specs=[VMEM] * 2,
        out_shape=stack_outputs(acc, groups, parts),
        compiler_params=params(),
        cost_estimate=stack_cost(lags // parts, depth, acc.shape[1]),
    )(core, lag_table, acc, cross)


def away_kernel(place_ref, keep_ref, near_ref, *outs):
    for d, out in enumerate(outs):
        at = place_ref[0] ^ (d + 1)
        out[...] = (keep_ref[at] + near_ref[at].astype(jnp.float32)).astype(out.dtype)


def sum_away(place, keep, near):
    outer, lags, pairs = keep.shape
    return pl.pallas_call(
        away_kernel,
        name="away",
        out_shape=[jax.ShapeDtypeStruct((lags, pairs), near.dtype)] * (outer - 1),
        in_specs=[SMEM, VMEM, VMEM],
        out_specs=[VMEM] * (outer - 1),
        compiler_params=params(2 * size(keep.shape, jnp.float32)),
        cost_estimate=pl.CostEstimate(
            flops=keep.size, bytes_accessed=6 * keep.size, transcendentals=0
        ),
    )(place, keep, near)


def result_kernel(scale, count, part, place_ref, *refs):
    keep, near, *far = refs[:count]
    out, rows, sem = refs[-3:]
    place = place_ref[0]
    total = keep[place] + near[place].astype(jnp.float32)
    for ref in far:
        total = total + ref[...].astype(jnp.float32)
    rows[...] = scale * total
    lags = rows.shape[0]
    copy = pltpu.make_async_copy(rows, out.at[pl.ds(part * lags, lags)], sem)
    copy.start()
    copy.wait()


def result(place, pieces, scale, part, parts, before):
    _, lags, pairs = pieces[0].shape
    specs = [VMEM] * len(pieces)
    operands = (place, *pieces)
    aliases = {}
    if before is not None:
        operands += (before,)
        specs.append(pl.BlockSpec(memory_space=pl.ANY))
        aliases = {len(operands) - 1: 0}
    return pl.pallas_call(
        functools.partial(result_kernel, scale, len(pieces), part),
        name="result",
        out_shape=jax.ShapeDtypeStruct((lags * parts, pairs), jnp.float32),
        in_specs=[SMEM] + specs,
        out_specs=pl.BlockSpec(memory_space=pl.ANY),
        scratch_shapes=[pltpu.VMEM((lags, pairs), jnp.float32), pltpu.SemaphoreType.DMA],
        input_output_aliases=aliases,
        compiler_params=params(size((lags, pairs), jnp.float32)),
        cost_estimate=pl.CostEstimate(
            flops=lags * pairs * 4, bytes_accessed=lags * pairs * 16, transcendentals=0
        ),
    )(*operands)


def swap(x, axis, mask):
    return lax.ppermute(x, axis, [(i, i ^ mask) for i in range(lax.axis_size(axis))])


def swap_both(x, mask_pairs, mask_win):
    groups = lax.axis_size("win")
    perm = [
        (p * groups + w, (p ^ mask_pairs) * groups + (w ^ mask_win))
        for p in range(lax.axis_size("pairs"))
        for w in range(groups)
    ]
    return lax.ppermute(x, ("pairs", "win"), perm)


def after(x, *earlier):
    return lax.optimization_barrier((x,) + earlier)[0]


def local(spectra, requests, pair_first, pair_second):
    stations, windows, _, bins = spectra.shape
    sources = lax.axis_size("pairs")
    groups = lax.axis_size("win")
    cap = requests.shape[2]
    me = lax.axis_index("pairs").astype(jnp.int32)
    group = lax.axis_index("win").astype(jnp.int32)
    core = group & 1
    blocks = bins // LANES
    half = blocks // 2
    assert windows == 2 and blocks == 2 * half + 1 and half == 12 and groups % 2 == 0
    assert stations % 2 == 0

    keep_big, keep_small, give_big, give_small = whiten(core[None], spectra)
    near_big = swap(give_big, "win", 1)
    near_small = swap(give_small, "win", 1)

    slots = sources * cap
    wanted = jnp.maximum(requests[0], 0)
    if two_stage(sources):
        far = sources // 2
        chunks = {
            "small": [
                keep_small,
                near_small,
                swap(keep_small, "pairs", far),
                swap_both(give_small, far, 1),
            ],
            "big": [keep_big, near_big, swap(keep_big, "pairs", far), swap_both(give_big, far, 1)],
        }
        wanted = after(wanted, keep_small)
        asked = [wanted] + [swap(wanted, "pairs", d) for d in range(1, far)]
        early = select_early(me[None], asked[1], keep_big, near_big, keep_small, near_small)
        early = swap(early, "pairs", 1)
        arrived = {}
        for name, chunk in chunks.items():
            outs = select(me[None], asked, chunk, cap, name == "small", (1,))
            rows = [swap(outs[d], "pairs", d) for d in range(1, far)]
            arrived[name] = [outs[0], early] + rows
        small, big = arrived["small"], arrived["big"]
        core_table = core

        def row_of(slot):
            apart = (slot // cap) ^ me
            return (apart % far) * (2 * cap) + (apart // far) * cap + slot % cap

    else:
        asked_rows = lax.all_to_all(wanted, "pairs", split_axis=0, concat_axis=0, tiled=True)

        def exchange(chunk):
            outgoing = chunk[asked_rows]
            arrived = lax.all_to_all(outgoing, "pairs", split_axis=0, concat_axis=0, tiled=True)
            return [arrived.reshape((slots,) + chunk.shape[1:])]

        big = exchange(join(keep_big, near_big, False))
        small = exchange(join(keep_small, near_small, True))
        core_table = core

        def row_of(slot):
            return slot

    coarse, fine = lag_bases(core_table, half, blocks)
    table_big, table_small = lag_table(coarse, fine)
    first = row_of(pair_first)
    second = row_of(pair_second)
    acc = stack_small(first, second, small, table_small, LAGS // groups)

    place = (group >> 1)[None]
    parts = 2
    out = None
    norm_scale = 1.0 / math.sqrt(bins * windows * groups)
    send, keep, cross = stack_first(core[None], first, second, big, table_big, acc, groups, parts)
    for part in range(parts):
        if part > 0:
            send, keep = stack_next(core[None], table_big, acc, cross, groups, part, parts)
        near = swap(send, "win", 1)
        away = sum_away(place, keep, near)
        pieces = [keep, near] + [swap(x, "win", 2 * (d + 1)) for d, x in enumerate(away)]
        out = result(place, pieces, norm_scale, part, parts, out)
    return out


def two_stage(sources):
    return sources & (sources - 1) == 0 and 4 <= sources <= 16


def solution(mesh):
    step = jax.shard_map(
        local,
        mesh=mesh,
        in_specs=(P("pairs", "win", None, None), P("pairs", None, None), P("pairs"), P("pairs")),
        out_specs=P("win", "pairs"),
        check_vma=False,
    )
    sources = mesh.shape["pairs"]
    if not two_stage(sources):
        return step
    return step
```
